32 devices in a mesh: end: 2 (over x), slab: 16 (over z, y, core).
Axes of the slice: x: 2, y: 2, z: 4, core: 2. Of those that a mesh axis runs over, the one named last changes fastest.
Arguments:
- w_field: float32 [128, 128, 256], P('slab'), may hold values from -4 to 4
- psi_init: float32 [128, 128, 256], P('slab'), may hold values from -3 to 3
- start_field: float32 [2, 128, 128, 256], P('end', 'slab'), may hold values from 0.25 to 8, as said below
- charges: int32 [5], replicated, may hold values from -1 to 1
Outputs:
- density: float32 [128, 128, 256], P('slab', 'end')
- potential: float32 [128, 128, 256], P('slab', 'end')
The draws below stay inside these ranges and needn't reach their ends.
Inputs may be any that keep to these rules, and one draw needn't show every extreme that they name: `start_field`: positive entries.
All inputs are finite; a program needn't handle non-finite values.
Results may differ from the reference program's by a relative error of at most 0.0003.
The reference program's roundings to bfloat16 on the way count: a program that leaves them out, or rounds other values in their place, can miss the bound.
Values may be sent and summed in bfloat16 or wider, within the bound.
A program may use at most 64 MiB of HBM per device.

```python
import jax
import jax.numpy as jnp
from jax import lax

NY = 128
NZ = 256
NS = 4
SWEEPS = 2
NX = 128


def draw_start_field(key, part):
    position = jnp.arange(NX, dtype=jnp.float32) / (NX - 1)
    base = jax.random.uniform(key, (2, NX, NY, NZ), jnp.float32, 0.5, 1.5)
    ramp = 1.0 + 2.0 * position
    return base * ramp[None, :, None, None]


def set_ends(drawn, key, low, largest):
    longest = drawn.shape.index(max(drawn.shape))
    spots = []
    for shift in (0, 1):
        where = [jax.random.randint(jax.random.fold_in(key, axis), (), 0, length) for axis, length in enumerate(drawn.shape)]
        where[longest] = (where[longest] + shift) % drawn.shape[longest]
        spots.append(tuple(where))
    return drawn.at[spots[0]].set(low).at[spots[1]].set(largest)


def levels(own_key, shape, split, least, top_value):
    factor_of = 1.0
    for dim, parts in split:
        heights = jax.random.uniform(jax.random.fold_in(jax.random.fold_in(own_key, 6), dim), (parts,), jnp.float32, least / len(split), top_value / len(split))
        factor_of = factor_of * jnp.repeat(jnp.exp(heights), shape[dim] // parts).reshape((-1,) + (1,) * (len(shape) - 1 - dim))
    return factor_of


def noise(rng, dims, deviation, bound, pieces=(), kind=jnp.bfloat16):
    factor_of = levels(rng, dims, pieces, -0.22, 0.18) if pieces else 1.0
    entries = jax.random.normal(rng, dims, jnp.float32) * deviation * factor_of
    return jnp.minimum(jnp.maximum(entries, -bound), bound).astype(kind)


def setup_inputs(seed: int = 0) -> dict:
    splits = jax.random.split(jax.random.key(seed), 5)
    w_field = noise(splits[0], (NX, NY, NZ), 1.0, 4.0, ((0, 16),), jnp.float32)
    psi_init = noise(splits[1], (NX, NY, NZ), 0.5, 3.0, ((0, 16),), jnp.float32)
    start_field = draw_start_field(jax.random.fold_in(splits[4], 71), 0)
    charges = set_ends(jax.random.randint(splits[3], (NS + 1,), -1, 2), jax.random.fold_in(splits[3], 1), -1, 1).astype(jnp.int32)
    return dict(w_field=w_field, psi_init=psi_init, start_field=start_field, charges=charges)


mobility = 0.15
screening = 1.0
crowding = 0.5


def neighbour_sum(field):
    total = jnp.roll(field, 1, 0) + jnp.roll(field, -1, 0)
    total = total + jnp.roll(field, 1, 1) + jnp.roll(field, -1, 1)
    return total + jnp.roll(field, 1, 2) + jnp.roll(field, -1, 2)


def ion_charge(value):
    return screening * jnp.sinh(value) / (1.0 + crowding * (jnp.cosh(value) - 1.0))


def reference(w_field, psi_init, start_field, charges):
    delta = 1.0 / NS
    valence = charges.astype(jnp.float32)

    def advance(field, contour):
        factor = jnp.exp(-0.5 * delta * (w_field + 0.5 * (valence[contour] + valence[contour + 1]) * psi_init))
        scaled = factor * field
        return factor * (scaled + mobility * (neighbour_sum(scaled) - 6.0 * scaled))

    def rounded(field):
        return lax.optimization_barrier(field.astype(jnp.bfloat16)).astype(jnp.float32)

    forward = [start_field[0]]
    for contour in range(NS):
        forward.append(advance(forward[-1], contour))
    conjugate = start_field[1]
    phi_raw = jnp.zeros(w_field.shape, jnp.float32)
    rho_raw = jnp.zeros(w_field.shape, jnp.float32)
    for contour in range(NS, -1, -1):
        if contour < NS:
            conjugate = advance(conjugate, contour)
        product = rounded(forward[contour]) * rounded(conjugate)
        weight = delta * (0.5 if contour in (0, NS) else 1.0)
        phi_raw = phi_raw + weight * product
        rho_raw = rho_raw + (weight * valence[contour]) * product
    total = jnp.mean(phi_raw)
    density = phi_raw / total
    charge = rho_raw / total
    potential = psi_init
    for sweep in range(SWEEPS):
        potential = (neighbour_sum(potential) + charge - ion_charge(potential) + screening * potential) / (6.0 + screening)
    return density, potential
```

```python
import functools

import jax
import jax.numpy as jnp
from jax import lax
from jax.experimental import pallas as pl
from jax.experimental.pallas import tpu as pltpu
from jax.sharding import PartitionSpec as P

NS = 4
PAD = 8
mobility = 0.15
screening = 1.0
OWN, FOREIGN = 0, 1
MESH = pl.DeviceIdType.MESH


def kernel(ends, slabs, charges_hbm, w_hbm, psi_hbm, start_hbm, density_ref, potential_ref,
           charges_ref, charges_sem, w_v, psi_v, start_v, factor, u, rounded, phi, rho, base, relaxed, sums,
           gate, local_sem, field_send, field_recv, psi_send, psi_recv, halo_send, halo_recv,
           rho_send, rho_recv, sum_send, sum_recv):
    side, slab = lax.axis_index("end"), lax.axis_index("slab")
    other = lax.rem(side + 1, ends)
    left = (side, lax.rem(slab + slabs - 1, slabs))
    right = (side, lax.rem(slab + 1, slabs))
    partner = (other, slab)
    layers, rows = w_hbm.shape[0], w_hbm.shape[1]
    half = rows // ends
    devices = ends * slabs
    flat = side * slabs + slab
    delta = 1.0 / NS

    def device(step):
        target = lax.rem(flat + step, devices)
        return (target // slabs, lax.rem(target, slabs))

    barrier = pltpu.get_barrier_semaphore()

    charges_copy = pltpu.make_async_copy(charges_hbm, charges_ref, charges_sem)
    charges_copy.start()

    near = []
    width = 1
    while width < slabs:
        near.append((side, slab + width - 2 * width * lax.rem(slab // width, 2)))
        width *= 2
    near.append(partner)
    for neighbour in near + [left, right]:
        pl.semaphore_signal(barrier, inc=1, device_id=neighbour, device_id_type=MESH)

    def pieces(which):
        first = which * half
        return (
            (pl.multiple_of(first, 8), PAD, half),
            (pl.multiple_of(lax.rem(first + rows - PAD, rows), 8), 0, PAD),
            (pl.multiple_of(lax.rem(first + half, rows), 8), PAD + half, PAD),
        )

    mine, theirs = pieces(side), pieces(other)
    local = []
    for k, (source, target, first) in enumerate(
        ((w_hbm, w_v, 0), (psi_hbm, psi_v, 2), (start_hbm.at[0], start_v.at[OWN], 0))
    ):
        for n, (begin, at, count) in enumerate(mine):
            local.append(
                pltpu.make_async_copy(
                    source.at[:, pl.ds(begin, count)],
                    target.at[pl.ds(first, layers), pl.ds(at, count)],
                    local_sem.at[k, n],
                )
            )
    for copy in local:
        copy.start()

    charges_copy.wait()
    q = [charges_ref[side * (NS - 2 * t) + t].astype(jnp.float32) for t in range(NS + 1)]
    pair = [0.5 * (q[k] + q[k + 1]) for k in range(NS)]

    def make_factor(x, carry):
        w, psi = w_v[x], psi_v[x + 2]
        for k in range(NS):
            factor[k, x] = jnp.exp(-0.5 * delta * (w + pair[k] * psi))
        return carry

    def index(chain, t):
        return t if chain == OWN else NS - 1 - t

    def begin_chain(chain, x):
        value = start_v[chain, x]
        rounded[chain, 0, x] = value.astype(jnp.bfloat16).astype(jnp.float32)
        u[chain, 0, x + 1] = factor[index(chain, 0), x] * value

    def around(value, axis):
        return pltpu.roll(value, 1, axis) + pltpu.roll(value, value.shape[axis] - 1, axis)

    def advanced(chain, t, x):
        center = u[chain, t, x + 1]
        total = u[chain, t, x] + u[chain, t, x + 2] + around(center, 0) + around(center, 1)
        return factor[index(chain, t), x] * ((1.0 - 6.0 * mobility) * center + mobility * total)

    def advance(chain, t, x):
        value = advanced(chain, t, x)
        rounded[chain, t + 1, x] = value.astype(jnp.bfloat16).astype(jnp.float32)
        if t + 1 < NS:
            u[chain, t + 1, x + 1] = factor[index(chain, t + 1), x] * value

    def loop(low, high, step):
        def body(x, carry):
            step(x)
            return carry

        lax.fori_loop(low, high, body, 0)

    def both(step):
        step(0)
        step(layers - 1)

    def halo(chain, t):
        return (
            pltpu.make_async_remote_copy(
                u.at[chain, t, 1], u.at[chain, t, layers + 1],
                halo_send.at[chain, t, 0], halo_recv.at[chain, t, 0],
                device_id=left, device_id_type=MESH,
            ),
            pltpu.make_async_remote_copy(
                u.at[chain, t, layers], u.at[chain, t, 0],
                halo_send.at[chain, t, 1], halo_recv.at[chain, t, 1],
                device_id=right, device_id_type=MESH,
            ),
        )

    sent = []

    def send_halo(chain, t):
        for copy in halo(chain, t):
            copy.start()
            sent.append(copy)

    def wait_halo(chain, t):
        for copy in halo(chain, t):
            copy.wait_recv()

    groups = [(0, layers - 1), (1, layers - 2), (2, layers - 3), tuple(range(3, layers - 3))]
    order = [x for group in groups for x in group]

    def field(x):
        return [
            pltpu.make_async_remote_copy(
                start_hbm.at[0, x, pl.ds(begin, count)],
                start_v.at[FOREIGN, x, pl.ds(at, count)],
                field_send.at[x, n], field_recv.at[x, n],
                device_id=partner, device_id_type=MESH,
            )
            for n, (begin, at, count) in enumerate(theirs)
        ]

    def arrive(group):
        for x in groups[group]:
            for copy in field(x):
                copy.wait_recv()
        for x in groups[group]:
            begin_chain(FOREIGN, x)

    def psi_halo():
        copies = []
        for n, (begin, at, count) in enumerate(mine):
            deep = 2 if count == half else 1
            copies.append(
                pltpu.make_async_remote_copy(
                    psi_hbm.at[pl.ds(0, deep), pl.ds(begin, count)],
                    psi_v.at[pl.ds(layers + 2, deep), pl.ds(at, count)],
                    psi_send.at[0, n], psi_recv.at[0, n],
                    device_id=left, device_id_type=MESH,
                )
            )
            copies.append(
                pltpu.make_async_remote_copy(
                    psi_hbm.at[pl.ds(layers - deep, deep), pl.ds(begin, count)],
                    psi_v.at[pl.ds(2 - deep, deep), pl.ds(at, count)],
                    psi_send.at[1, n], psi_recv.at[1, n],
                    device_id=right, device_id_type=MESH,
                )
            )
        return copies

    pl.semaphore_wait(barrier, len(near) + 2)
    for x in order:
        for copy in field(x):
            copy.start()
            sent.append(copy)
    for copy in local:
        copy.wait()
    stages = len(near)

    def open_gate(stage):
        pl.semaphore_signal(gate.at[stage], inc=1, device_id=near[stage], device_id_type=MESH)

    def pass_gate(stage):
        pl.semaphore_wait(gate.at[stage], 1)
        if stage + 1 < stages:
            open_gate(stage + 1)

    open_gate(0)
    for x in (0, layers - 1):
        make_factor(x, 0)
        begin_chain(OWN, x)
    send_halo(OWN, 0)
    pass_gate(0)
    lax.fori_loop(1, layers - 1, make_factor, 0)
    loop(1, layers - 1, functools.partial(begin_chain, OWN))
    loop(1, layers - 1, functools.partial(advance, OWN, 0))

    def make_base(x):
        center = psi_v[x + 1]
        total = psi_v[x] + psi_v[x + 2] + around(center, 0) + around(center, 1)
        base[x] = total - ion_charge(center) + screening * center

    loop(2, layers, make_base)

    pass_gate(1)
    arrive(0)
    send_halo(FOREIGN, 0)
    wait_halo(OWN, 0)
    both(functools.partial(advance, OWN, 0))
    send_halo(OWN, 1)
    loop(1, layers - 1, functools.partial(advance, OWN, 1))

    pass_gate(2)
    arrive(1)
    wait_halo(FOREIGN, 0)
    both(functools.partial(advance, FOREIGN, 0))
    send_halo(FOREIGN, 1)
    wait_halo(OWN, 1)
    both(functools.partial(advance, OWN, 1))
    send_halo(OWN, 2)
    loop(1, layers - 1, functools.partial(advance, OWN, 2))

    pass_gate(3)
    arrive(2)
    for x in (1, layers - 2):
        advance(FOREIGN, 0, x)
    wait_halo(FOREIGN, 1)
    both(functools.partial(advance, FOREIGN, 1))
    send_halo(FOREIGN, 2)
    wait_halo(OWN, 2)
    both(functools.partial(advance, OWN, 2))
    send_halo(OWN, 3)
    loop(1, layers - 1, functools.partial(advance, OWN, 3))

    for stage in range(4, stages):
        pass_gate(stage)
    arrive(3)
    for x in (2, layers - 3):
        advance(FOREIGN, 0, x)
    for x in (1, layers - 2):
        advance(FOREIGN, 1, x)
    wait_halo(FOREIGN, 2)
    both(functools.partial(advance, FOREIGN, 2))
    send_halo(FOREIGN, 3)
    psi_copies = psi_halo()
    for copy in psi_copies:
        copy.start()
        sent.append(copy)
    loop(3, layers - 3, functools.partial(advance, FOREIGN, 0))
    loop(2, layers - 2, functools.partial(advance, FOREIGN, 1))
    loop(1, layers - 1, functools.partial(advance, FOREIGN, 2))
    wait_halo(OWN, 3)
    both(functools.partial(advance, OWN, 3))

    weights = [delta * (0.5 if t in (0, NS) else 1.0) for t in range(NS + 1)]
    charged = [weights[t] * q[t] for t in range(NS + 1)]

    def gathered(x):
        phi_layer, rho_layer = 0.0, 0.0
        for t in range(1, NS + 1):
            product = rounded[OWN, t, x] * rounded[FOREIGN, NS - t, x]
            phi_layer = phi_layer + weights[t] * product
            rho_layer = rho_layer + charged[t] * product
        return phi_layer, rho_layer

    def gather(x):
        phi[x], rho[x + 1] = gathered(x)

    def last_product(x):
        value = advanced(FOREIGN, NS - 1, x).astype(jnp.bfloat16).astype(jnp.float32)
        return rounded[OWN, 0, x] * value

    def finish(x):
        product = last_product(x)
        phi[x] += weights[0] * product
        rho[x + 1] += charged[0] * product

    def whole(x):
        phi_layer, rho_layer = gathered(x)
        product = last_product(x)
        phi[x] = phi_layer + weights[0] * product
        rho[x + 1] = rho_layer + charged[0] * product

    both(gather)
    loop(1, layers - 1, whole)

    inner = pl.ds(PAD, half)

    def add(x, carry):
        return carry + phi[x, inner]

    partial = lax.fori_loop(2, layers - 1, add, phi[1, inner])
    wait_halo(FOREIGN, NS - 1)
    both(finish)
    rho_copies = (
        pltpu.make_async_remote_copy(
            rho.at[1, inner], rho.at[layers + 1, inner], rho_send.at[0], rho_recv.at[0],
            device_id=left, device_id_type=MESH,
        ),
        pltpu.make_async_remote_copy(
            rho.at[layers, inner], rho.at[0, inner], rho_send.at[1], rho_recv.at[1],
            device_id=right, device_id_type=MESH,
        ),
    )
    partial = partial + phi[0, inner] + phi[layers - 1, inner]
    sums[0] = jnp.sum(
        sum(partial[:, k:k + 128] for k in range(0, partial.shape[1], 128)), axis=0, keepdims=True
    )

    def share(step, carry):
        pltpu.make_async_remote_copy(
            sums.at[0], sums.at[step], sum_send, sum_recv,
            device_id=device(step), device_id_type=MESH,
        ).start()
        return carry

    lax.fori_loop(1, devices, share, 0)
    for copy in rho_copies:
        copy.start()
        sent.append(copy)

    for copy in psi_copies:
        copy.wait_recv()

    for x in (0, 1, layers, layers + 1):
        make_base(x)

    others = sums.at[pl.ds(1, devices - 1)]
    pltpu.make_async_copy(others, others, sum_recv).wait()
    cells = float(devices * layers * half * w_hbm.shape[2])
    inverse = cells / jnp.sum(sums[...])

    def relax_once(x):
        relaxed[x] = (base[x] + rho[x] * inverse) * (1.0 / (6.0 + screening))

    def first(x):
        density_ref[x] = phi[x, inner] * inverse
        relax_once(x + 1)

    loop(0, layers, first)

    def second(x):
        center = relaxed[x + 1]
        total = relaxed[x] + relaxed[x + 2] + around(center, 0) + around(center, 1)
        value = total + rho[x + 1] * inverse - ion_charge(center) + screening * center
        potential_ref[x] = value[PAD:PAD + half] * (1.0 / (6.0 + screening))

    loop(1, layers - 1, second)
    for copy in rho_copies:
        copy.wait_recv()
    relax_once(0)
    relax_once(layers + 1)
    both(second)

    for copy in sent:
        copy.wait_send()
    pltpu.make_async_copy(others, others, sum_send).wait()


def ion_charge(value):
    return (2.0 * screening) * jnp.tanh(0.5 * value)


def body(ends, slabs, w_field, psi_init, start_field, charges):
    layers, rows, depth = w_field.shape
    half = rows // ends
    wide = half + 2 * PAD
    devices = ends * slabs
    stages = slabs.bit_length()
    out = jax.ShapeDtypeStruct((layers, half, depth), jnp.float32)
    dma = pltpu.SemaphoreType.DMA

    def tile(*lead):
        return pltpu.VMEM((*lead, wide, depth), jnp.float32)

    hbm = pl.BlockSpec(memory_space=pltpu.HBM)
    vmem = pl.BlockSpec(memory_space=pltpu.VMEM)
    return pl.pallas_call(
        functools.partial(kernel, ends, slabs),
        out_shape=(out, out),
        in_specs=[hbm, hbm, hbm, hbm],
        out_specs=(vmem, vmem),
        scratch_shapes=[
            pltpu.SMEM((NS + 1,), jnp.int32), dma(()), tile(layers), tile(layers + 4), tile(2, layers), tile(NS, layers),
            tile(2, NS, layers + 2), tile(2, NS + 1, layers), tile(layers), tile(layers + 2),
            tile(layers + 2), tile(layers + 2), pltpu.VMEM((devices, 1, 128), jnp.float32),
            pltpu.SemaphoreType.REGULAR((stages,)), dma((3, 3)), dma((layers, 3)), dma((layers, 3)), dma((2, 3)), dma((2, 3)),
            dma((2, NS, 2)), dma((2, NS, 2)), dma((2,)), dma((2,)), dma(()), dma(()),
        ],
        compiler_params=pltpu.CompilerParams(
            collective_id=0, has_side_effects=True, vmem_limit_bytes=30 * 1024 * 1024
        ),
        name="scf_step",
    )(*[pltpu.with_memory_space_constraint(v, pltpu.HBM) for v in (charges, w_field, psi_init, start_field)])


def solution(mesh):
    in_specs = (P("slab", None, None), P("slab", None, None), P("end", "slab", None, None), P())
    out_specs = (P("slab", "end", None), P("slab", "end", None))
    step = functools.partial(body, mesh.shape["end"], mesh.shape["slab"])
    return jax.shard_map(step, mesh=mesh, in_specs=in_specs, out_specs=out_specs, check_vma=False)
```

```python
import functools
import math

import jax
import jax.numpy as jnp
from jax import lax
from jax.experimental import pallas as pl
from jax.experimental.pallas import tpu as pltpu
from jax.sharding import PartitionSpec as P

NS = 4
PAD = 8
mobility = 0.15
screening = 1.0
OWN, FOREIGN = 0, 1
W_MAX, PSI_MAX = 4.0, 3.0
START_MIN, START_MAX = 0.25, 8.0
CODES, OFFSET = 65535.0, 32768
MARGIN = 0.001
MESH = pl.DeviceIdType.MESH


def kernel(ends, slabs, charges_hbm, w_hbm, psi_hbm, start_hbm, density_ref, potential_ref,
           charges_ref, w_v, psi_v, start_v, theirs_v, factor, u, rounded, phi, rho, base, relaxed, sums,
           field_out, field_in, edge_out, edge_in, halo_out, halo_in,
           gate, charges_sem, local_sem, field_send, field_recv, edge_send, edge_recv, halo_send, halo_recv,
           rho_send, rho_recv, sum_send, sum_recv):
    side, slab = lax.axis_index("end"), lax.axis_index("slab")
    other = lax.rem(side + 1, ends)
    left = (side, lax.rem(slab + slabs - 1, slabs))
    right = (side, lax.rem(slab + 1, slabs))
    partner = (other, slab)
    layers, rows = w_hbm.shape[0], w_hbm.shape[1]
    half = rows // ends
    devices = ends * slabs
    flat = side * slabs + slab
    delta = 1.0 / NS

    def device(step):
        target = lax.rem(flat + step, devices)
        return (target // slabs, lax.rem(target, slabs))

    barrier = pltpu.get_barrier_semaphore()
    charges_copy = pltpu.make_async_copy(charges_hbm, charges_ref, charges_sem)
    charges_copy.start()

    near = []
    width = 1
    while width < slabs:
        near.append((side, slab + width - 2 * width * lax.rem(slab // width, 2)))
        width *= 2
    near.append(partner)
    for neighbour in near + [left, right]:
        pl.semaphore_signal(barrier, inc=1, device_id=neighbour, device_id_type=MESH)

    def pieces(which):
        first = which * half
        return (
            (pl.multiple_of(first, 8), PAD, half),
            (pl.multiple_of(lax.rem(first + rows - PAD, rows), 8), 0, PAD),
            (pl.multiple_of(lax.rem(first + half, rows), 8), PAD + half, PAD),
        )

    mine, theirs = pieces(side), pieces(other)
    local = []
    for k, (source, target, first, parts) in enumerate((
        (start_hbm.at[0], theirs_v, 0, theirs), (w_hbm, w_v, 1, mine),
        (psi_hbm, psi_v, 2, mine), (start_hbm.at[0], start_v, 0, mine),
    )):
        local.append([
            pltpu.make_async_copy(
                source.at[:, pl.ds(begin, count)],
                target.at[pl.ds(first, layers), pl.ds(at, count)],
                local_sem.at[k, n],
            )
            for n, (begin, at, count) in enumerate(parts)
        ])
    for copies in local:
        for copy in copies:
            copy.start()

    def loop(low, high, step):
        def body(x, carry):
            step(x)
            return carry

        lax.fori_loop(low, high, body, 0)

    def span(t):
        reach = 0.5 * delta * (W_MAX + PSI_MAX) * t + MARGIN
        return math.log(START_MIN) - reach, math.log(START_MAX) + reach

    def write_code(value, low, high):
        scaled = value * (CODES / (high - low)) + (0.5 - low * (CODES / (high - low)))
        return (scaled.astype(jnp.int32) - OFFSET).astype(jnp.int16)

    def read_code(code, low, high):
        step = (high - low) / CODES
        return code.astype(jnp.int32).astype(jnp.float32) * step + (low + OFFSET * step)

    def write_log(value, t):
        return write_code(jnp.log(value), *span(t))

    def read_log(code, t):
        return jnp.exp(read_code(code, *span(t)))

    w_span, psi_span = (-W_MAX - MARGIN, W_MAX + MARGIN), (-PSI_MAX - MARGIN, PSI_MAX + MARGIN)

    for copy in local[0]:
        copy.wait()

    def code_field(x):
        field_out[x] = write_log(theirs_v[x], 0)

    loop(0, layers, code_field)

    charges_copy.wait()
    q = [charges_ref[side * (NS - 2 * t) + t].astype(jnp.float32) for t in range(NS + 1)]
    pair = [0.5 * (q[k] + q[k + 1]) for k in range(NS)]

    def make_factor(x):
        w, psi = w_v[x + 1], psi_v[x + 2]
        for k in range(NS):
            factor[k, x + 1] = jnp.exp(-0.5 * delta * (w + pair[k] * psi))

    def index(chain, t):
        return t if chain == OWN else NS - 1 - t

    def to_bfloat16(value):
        return value.astype(jnp.bfloat16).astype(jnp.float32)

    def begin_chain(chain, x):
        value = start_v[x] if chain == OWN else read_log(field_in[x], 0)
        rounded[chain, 0, x] = to_bfloat16(value)
        u[chain, 0, x + 2] = factor[index(chain, 0), x + 1] * value

    def around(value, axis):
        return pltpu.roll(value, 1, axis) + pltpu.roll(value, value.shape[axis] - 1, axis)

    def advanced(chain, t, x):
        center = u[chain, t, x + 2]
        total = u[chain, t, x + 1] + u[chain, t, x + 3] + around(center, 0) + around(center, 1)
        return factor[index(chain, t), x + 1] * ((1.0 - 6.0 * mobility) * center + mobility * total)

    def advance_halo(chain, t, x):
        u[chain, t + 1, x + 2] = factor[index(chain, t + 1), x + 1] * advanced(chain, t, x)

    def advance(chain, t, x):
        value = advanced(chain, t, x)
        rounded[chain, t + 1, x] = to_bfloat16(value)
        if t + 1 < NS:
            u[chain, t + 1, x + 2] = factor[index(chain, t + 1), x + 1] * value

    def adv(chain, t, low, high):
        loop(low, high, functools.partial(advance, chain, t))

    def outer(step):
        loop(0, 2, lambda k: step((layers - 1) * k))

    def beyond(step):
        loop(0, 2, lambda k: step((layers + 1) * k - 1))

    def edge_pair(d, step):
        loop(0, 2, lambda j: step(j + d * (layers - 2)))

    def out_layer(d, j):
        return layers - 1 - j if d else j

    def in_layer(d, j):
        return -1 - j if d else layers + j

    targets = (left, right)

    for copies in local[1:]:
        for copy in copies:
            copy.wait()
    loop(0, layers, make_factor)
    loop(0, layers, functools.partial(begin_chain, OWN))
    for d in (0, 1):
        def code_edge(j, d=d):
            x = out_layer(d, j)
            edge_out[d, j] = write_log(u[OWN, 0, x + 2], 1)
            edge_out[d, 3 + j] = write_code(psi_v[x + 2], *psi_span)

        loop(0, 2, code_edge)
        edge_out[d, 2] = write_code(w_v[out_layer(d, 0) + 1], *w_span)
    adv(OWN, 0, 1, layers - 1)
    adv(OWN, 1, 2, layers - 2)

    def make_base(x):
        center = psi_v[x + 2]
        total = psi_v[x + 1] + psi_v[x + 3] + around(center, 0) + around(center, 1)
        base[x + 1] = (total - ion_charge(center) + screening * center) * (1.0 / (6.0 + screening))

    groups = [(0, layers - 1), (1, layers - 2), (2, layers - 3), tuple(range(3, layers - 3))]
    order = [x for group in groups for x in group]
    sent = []

    def send(copy):
        copy.start()
        sent.append(copy)
        return copy

    pl.semaphore_wait(barrier, len(near) + 2)
    fields = {
        x: send(pltpu.make_async_remote_copy(
            field_out.at[x], field_in.at[x], field_send.at[x], field_recv.at[x],
            device_id=partner, device_id_type=MESH,
        ))
        for x in order
    }
    edges = [
        send(pltpu.make_async_remote_copy(
            edge_out.at[d, pl.ds(first, count)], edge_in.at[d, pl.ds(first, count)],
            edge_send.at[d, n], edge_recv.at[d, n], device_id=targets[d], device_id_type=MESH,
        ))
        for n, (first, count) in enumerate(((0, 4), (4, 1))) for d in (0, 1)
    ]

    def halo(kind, d, first, count):
        return pltpu.make_async_remote_copy(
            halo_out.at[kind, d, pl.ds(first, count)], halo_in.at[kind, d, pl.ds(first, count)],
            halo_send.at[kind, d, first], halo_recv.at[kind, d, first],
            device_id=targets[d], device_id_type=MESH,
        )

    stages = len(near)

    def open_gate(stage):
        pl.semaphore_signal(gate.at[stage], inc=1, device_id=near[stage], device_id_type=MESH)

    def pass_gate(stage):
        pl.semaphore_wait(gate.at[stage], 1)
        if stage + 1 < stages:
            open_gate(stage + 1)

    open_gate(0)
    adv(OWN, 2, 3, layers - 3)
    pass_gate(0)
    loop(1, layers - 1, make_base)
    pass_gate(1)

    def arrive(group):
        for x in groups[group]:
            fields[x].wait_recv()
        for x in groups[group]:
            begin_chain(FOREIGN, x)

    copies = []
    for j in (0, 1):
        arrive(j)
        for d in (0, 1):
            halo_out[0, d, j] = write_log(u[FOREIGN, 0, out_layer(d, j) + 2], 1)
            copies.append(send(halo(0, d, j, 1)))

    pass_gate(2)
    arrive(2)
    adv(FOREIGN, 0, 1, 2)
    adv(FOREIGN, 0, layers - 2, layers - 1)

    for copy in edges[:2]:
        copy.wait_recv()
    for d in (0, 1):
        x = in_layer(d, 0)
        w_v[x + 1] = read_code(edge_in[d, 2], *w_span)
        psi_v[x + 2] = read_code(edge_in[d, 3], *psi_span)
        for j in (0, 1):
            u[OWN, 0, in_layer(d, j) + 2] = read_log(edge_in[d, j], 1)
    beyond(make_factor)
    beyond(functools.partial(advance_halo, OWN, 0))
    outer(functools.partial(advance, OWN, 0))

    def half_way(chain, kind):
        result = []
        for d in (0, 1):
            edge_pair(d, functools.partial(advance, chain, 1))
            for j in (0, 1):
                halo_out[kind, d, j] = write_log(u[chain, 2, out_layer(d, j) + 2], 5)
            result.append(send(halo(kind, d, 0, 2)))
        return result

    own_copies = half_way(OWN, 1)

    pass_gate(3)
    arrive(3)
    adv(FOREIGN, 0, 2, layers - 2)
    adv(FOREIGN, 1, 2, layers - 2)
    for copy in copies:
        copy.wait_recv()
    for d in (0, 1):
        for j in (0, 1):
            u[FOREIGN, 0, in_layer(d, j) + 2] = read_log(halo_in[0, d, j], 1)
    beyond(functools.partial(advance_halo, FOREIGN, 0))
    outer(functools.partial(advance, FOREIGN, 0))
    foreign_copies = half_way(FOREIGN, 2)

    for stage in range(4, stages):
        pass_gate(stage)
    adv(OWN, 2, 1, 3)
    adv(OWN, 2, layers - 3, layers - 1)
    adv(OWN, 3, 2, layers - 2)
    adv(FOREIGN, 2, 1, layers - 1)

    def second_half(chain, kind, copies):
        for copy in copies:
            copy.wait_recv()
        for d in (0, 1):
            for j in (0, 1):
                u[chain, 2, in_layer(d, j) + 2] = read_log(halo_in[kind, d, j], 5)
        beyond(functools.partial(advance_halo, chain, 2))
        outer(functools.partial(advance, chain, 2))

    weights = [delta * (0.5 if t in (0, NS) else 1.0) for t in range(NS + 1)]
    charged = [weights[t] * q[t] for t in range(NS + 1)]

    def gathered(x):
        phi_layer, rho_layer = 0.0, 0.0
        for t in range(1, NS + 1):
            product = rounded[OWN, t, x] * rounded[FOREIGN, NS - t, x]
            phi_layer = phi_layer + weights[t] * product
            rho_layer = rho_layer + charged[t] * product
        return phi_layer, rho_layer

    def whole(x):
        phi_layer, rho_layer = gathered(x)
        product = rounded[OWN, 0, x] * to_bfloat16(advanced(FOREIGN, NS - 1, x))
        phi[x] = phi_layer + weights[0] * product
        rho[x + 1] = rho_layer + charged[0] * product

    loop(2, layers - 2, whole)

    second_half(OWN, 1, own_copies)
    for d in (0, 1):
        edge_pair(d, functools.partial(advance, OWN, 3))

    inner = pl.ds(PAD, half)

    def add(x, carry):
        return carry + phi[x, inner]

    partial = lax.fori_loop(3, layers - 2, add, phi[2, inner])

    for copy in edges[2:]:
        copy.wait_recv()
    for d in (0, 1):
        psi_v[in_layer(d, 1) + 2] = read_code(edge_in[d, 4], *psi_span)
    for k in (-1, 0):
        make_base(k)
        make_base(layers - 1 - k)

    second_half(FOREIGN, 2, foreign_copies)
    rho_copies = []
    for d in (0, 1):
        edge_pair(d, whole)
        rho_copies.append(pltpu.make_async_remote_copy(
            rho.at[out_layer(d, 0) + 1, inner], rho.at[0 if d else layers + 1, inner],
            rho_send.at[d], rho_recv.at[d], device_id=targets[d], device_id_type=MESH,
        ))
    for x in (0, 1, layers - 2, layers - 1):
        partial = partial + phi[x, inner]
    sums[0] = jnp.sum(
        sum(partial[:, k:k + 128] for k in range(0, partial.shape[1], 128)), axis=0, keepdims=True
    )

    def share(step, carry):
        pltpu.make_async_remote_copy(
            sums.at[0], sums.at[step], sum_send, sum_recv,
            device_id=device(step), device_id_type=MESH,
        ).start()
        return carry

    lax.fori_loop(1, devices, share, 0)
    for copy in rho_copies:
        send(copy)

    others = sums.at[pl.ds(1, devices - 1)]
    pltpu.make_async_copy(others, others, sum_recv).wait()
    cells = float(devices * layers * half * w_hbm.shape[2])
    inverse = cells / jnp.sum(sums[...])
    scaled = inverse * (1.0 / (6.0 + screening))

    def relax_once(x):
        relaxed[x + 1] = base[x + 1] + rho[x + 1] * scaled

    def first(x):
        density_ref[x] = phi[x, inner] * inverse
        relax_once(x)

    loop(0, layers, first)

    def second(x):
        center = relaxed[x + 1]
        total = relaxed[x] + relaxed[x + 2] + around(center, 0) + around(center, 1)
        value = (total - ion_charge(center) + screening * center) * (1.0 / (6.0 + screening))
        potential_ref[x] = (value + rho[x + 1] * scaled)[PAD:PAD + half]

    loop(1, layers - 1, second)
    for copy in rho_copies:
        copy.wait_recv()
    relax_once(-1)
    relax_once(layers)
    outer(second)

    for copy in sent:
        copy.wait_send()
    pltpu.make_async_copy(others, others, sum_send).wait()


def ion_charge(value):
    return (2.0 * screening) * jnp.tanh(0.5 * value)


def body(ends, slabs, w_field, psi_init, start_field, charges):
    layers, rows, depth = w_field.shape
    half = rows // ends
    wide = half + 2 * PAD
    devices = ends * slabs
    stages = slabs.bit_length()
    out = jax.ShapeDtypeStruct((layers, half, depth), jnp.float32)
    dma = pltpu.SemaphoreType.DMA

    def tile(*lead):
        return pltpu.VMEM((*lead, wide, depth), jnp.float32)

    def code(*lead):
        return pltpu.VMEM((*lead, wide, depth), jnp.int16)

    hbm = pl.BlockSpec(memory_space=pltpu.HBM)
    vmem = pl.BlockSpec(memory_space=pltpu.VMEM)
    return pl.pallas_call(
        functools.partial(kernel, ends, slabs),
        out_shape=(out, out),
        in_specs=[hbm, hbm, hbm, hbm],
        out_specs=(vmem, vmem),
        scratch_shapes=[
            pltpu.SMEM((NS + 1,), jnp.int32), tile(layers + 2), tile(layers + 4), tile(layers), tile(layers),
            tile(NS, layers + 2), tile(2, NS, layers + 4), tile(2, NS + 1, layers),
            tile(layers), tile(layers + 2), tile(layers + 2), tile(layers + 2),
            pltpu.VMEM((devices, 1, 128), jnp.float32),
            code(layers), code(layers), code(2, 5), code(2, 5), code(3, 2, 2), code(3, 2, 2),
            pltpu.SemaphoreType.REGULAR((stages,)), dma(()), dma((4, 3)), dma((layers,)), dma((layers,)),
            dma((2, 2)), dma((2, 2)), dma((3, 2, 2)), dma((3, 2, 2)), dma((2,)), dma((2,)), dma(()), dma(()),
        ],
        compiler_params=pltpu.CompilerParams(
            collective_id=0, has_side_effects=True, vmem_limit_bytes=40 * 1024 * 1024
        ),
        name="scf_step",
    )(*[pltpu.with_memory_space_constraint(v, pltpu.HBM) for v in (charges, w_field, psi_init, start_field)])


def solution(mesh):
    in_specs = (P("slab", None, None), P("slab", None, None), P("end", "slab", None, None), P())
    out_specs = (P("slab", "end", None), P("slab", "end", None))
    step = functools.partial(body, mesh.shape["end"], mesh.shape["slab"])
    return jax.shard_map(step, mesh=mesh, in_specs=in_specs, out_specs=out_specs, check_vma=False)
```

```python
import functools
import math

import jax
import jax.numpy as jnp
from jax import lax
from jax.experimental import pallas as pl
from jax.experimental.pallas import tpu as pltpu
from jax.sharding import PartitionSpec as P

NS = 4
PAD = 8
EDGE = 4
LANES = 128
mobility = 0.15
screening = 1.0
OWN, FOREIGN = 0, 1
W_MAX, PSI_MAX = 4.0, 3.0
START_MIN, START_MAX = 0.25, 8.0
CODES, OFFSET = 65535.0, 32768
MARGIN = 0.001
MESH = pl.DeviceIdType.MESH


def kernel(ends, slabs, charges_hbm, w_hbm, psi_hbm, start_hbm, density_ref, potential_ref,
           charges_ref, w_v, psi_v, start_v, theirs_v, factor, u, rounded, phi, rho, base, relaxed, sums,
           field_out, field_in, edge_out, edge_in, halo_out, halo_in,
           gate, charges_sem, local_sem, field_send, field_recv, edge_send, edge_recv, halo_send, halo_recv,
           rho_send, rho_recv, sum_send, sum_recv):
    side, slab = lax.axis_index("end"), lax.axis_index("slab")
    other = lax.rem(side + 1, ends)
    left = (side, lax.rem(slab + slabs - 1, slabs))
    right = (side, lax.rem(slab + 1, slabs))
    partner = (other, slab)
    layers, rows = w_hbm.shape[0], w_hbm.shape[1]
    half = rows // ends
    parts = w_hbm.shape[2] // LANES
    devices = ends * slabs
    flat = side * slabs + slab
    delta = 1.0 / NS

    def device(step):
        target = lax.rem(flat + step, devices)
        return (target // slabs, lax.rem(target, slabs))

    barrier = pltpu.get_barrier_semaphore()
    charges_copy = pltpu.make_async_copy(charges_hbm, charges_ref, charges_sem)
    charges_copy.start()

    near = []
    width = 1
    while width < slabs:
        near.append((side, slab + width - 2 * width * lax.rem(slab // width, 2)))
        width *= 2
    near.append(partner)
    for neighbour in near + [left, right]:
        pl.semaphore_signal(barrier, inc=1, device_id=neighbour, device_id_type=MESH)

    def pieces(which):
        first = which * half
        return (
            (pl.multiple_of(first, 8), PAD, half),
            (pl.multiple_of(lax.rem(first + rows - PAD, rows), 8), 0, PAD),
            (pl.multiple_of(lax.rem(first + half, rows), 8), PAD + half, PAD),
        )

    mine, theirs = pieces(side), pieces(other)
    local = []
    for k, (source, target, first, pieces_of) in enumerate((
        (start_hbm.at[0], theirs_v, 0, theirs), (w_hbm, w_v, 1, mine),
        (psi_hbm, psi_v, 2, mine), (start_hbm.at[0], start_v, 0, mine),
    )):
        local.append([
            pltpu.make_async_copy(
                source.at[:, pl.ds(begin, count), pl.ds(h * LANES, LANES)],
                target.at[pl.ds(first, layers), h, pl.ds(at, count)],
                local_sem.at[k, n, h],
            )
            for n, (begin, at, count) in enumerate(pieces_of) for h in range(parts)
        ])
    for copies in local:
        for copy in copies:
            copy.start()

    def loop(low, high, step):
        def body(x, carry):
            step(x)
            return carry

        lax.fori_loop(low, high, body, 0, unroll=True)

    def span(t):
        reach = 0.5 * delta * (W_MAX + PSI_MAX) * t + MARGIN
        shift = 0.5 * math.log(mobility) if t else 0.0
        return math.log(START_MIN) - reach + shift, math.log(START_MAX) + reach + shift

    def write_code(value, low, high):
        scaled = value * (CODES / (high - low)) + (0.5 - low * (CODES / (high - low)))
        return (scaled.astype(jnp.int32) - OFFSET).astype(jnp.int16)

    def read_code(code, low, high):
        step = (high - low) / CODES
        return code.astype(jnp.int32).astype(jnp.float32) * step + (low + OFFSET * step)

    def write_log(value, t):
        return write_code(jnp.log(value), *span(t))

    def read_log(code, t):
        return jnp.exp(read_code(code, *span(t)))

    w_span, psi_span = (-W_MAX - MARGIN, W_MAX + MARGIN), (-PSI_MAX - MARGIN, PSI_MAX + MARGIN)

    for copy in local[0]:
        copy.wait()

    def code_field(x):
        field_out[x] = write_log(theirs_v[x], 0)

    loop(0, layers, code_field)

    charges_copy.wait()
    q = [charges_ref[side * (NS - 2 * t) + t].astype(jnp.float32) for t in range(NS + 1)]
    pair = [0.5 * (q[k] + q[k + 1]) for k in range(NS)]

    def make_factor(x):
        for h in range(parts):
            level = 0.5 * math.log(mobility) - 0.5 * delta * w_v[x + 1, h]
            psi = psi_v[x + 2, h]
            for k in range(NS):
                factor[k, x + 1, h] = jnp.exp(level - (0.5 * delta * pair[k]) * psi)

    def index(chain, t):
        return t if chain == OWN else NS - 1 - t

    def to_bfloat16(value):
        return value.astype(jnp.bfloat16).astype(jnp.float32)

    window = pl.ds(EDGE, half + 2 * (PAD - EDGE))
    inner = pl.ds(PAD - EDGE, half)

    def begin_chain(chain, x):
        value = start_v[x] if chain == OWN else read_log(field_in[x], 0)
        u[chain, 0, x + 2] = factor[index(chain, 0), x + 1] * value
        rounded[chain, 0, x] = to_bfloat16(value)

    lane = lax.broadcasted_iota(jnp.int32, (1, LANES), 1)
    lowest, highest = lane == 0, lane == LANES - 1

    def around(ref, at, first, count):
        center = [ref[(*at, h, pl.ds(first, count))] for h in range(parts)]
        lower = [pltpu.roll(value, 1, 1) for value in center]
        upper = [pltpu.roll(value, LANES - 1, 1) for value in center]
        sums = []
        for h in range(parts):
            total = ref[(*at, h, pl.ds(first - 1, count))] + ref[(*at, h, pl.ds(first + 1, count))]
            total = total + jnp.where(lowest, lower[h - 1], lower[h])
            sums.append(total + jnp.where(highest, upper[(h + 1) % parts], upper[h]))
        return center, sums

    def advanced(chain, t, x):
        center, sums = around(u, (chain, t, x + 2), EDGE, window.size)
        return [
            factor[index(chain, t), x + 1, h, window] * (
                (u[chain, t, x + 1, h, window] + u[chain, t, x + 3, h, window])
                + (sums[h] + ((1.0 - 6.0 * mobility) / mobility) * center[h])
            )
            for h in range(parts)
        ]

    def advance_halo(chain, t, x):
        for h, value in enumerate(advanced(chain, t, x)):
            u[chain, t + 1, x + 2, h, window] = factor[index(chain, t + 1), x + 1, h, window] * value

    def advance(chain, t, x):
        for h, value in enumerate(advanced(chain, t, x)):
            rounded[chain, t + 1, x, h, window] = to_bfloat16(value)
            if t + 1 < NS:
                u[chain, t + 1, x + 2, h, window] = factor[index(chain, t + 1), x + 1, h, window] * value

    def adv(chain, t, low, high):
        loop(low, high, functools.partial(advance, chain, t))

    def outer(step):
        loop(0, 2, lambda k: step((layers - 1) * k))

    def beyond(step):
        loop(0, 2, lambda k: step((layers + 1) * k - 1))

    def edge_pair(d, step):
        loop(0, 2, lambda j: step(j + d * (layers - 2)))

    def out_layer(d, j):
        return layers - 1 - j if d else j

    def in_layer(d, j):
        return -1 - j if d else layers + j

    targets = (left, right)

    for copies in local[1:]:
        for copy in copies:
            copy.wait()
    loop(0, layers, make_factor)
    loop(0, layers, functools.partial(begin_chain, OWN))
    for d in (0, 1):
        def code_edge(j, d=d):
            x = out_layer(d, j)
            edge_out[d, j] = write_log(u[OWN, 0, x + 2], 1)
            edge_out[d, 3 + j] = write_code(psi_v[x + 2], *psi_span)

        loop(0, 2, code_edge)
        edge_out[d, 2] = write_code(w_v[out_layer(d, 0) + 1], *w_span)
    adv(OWN, 0, 1, layers - 1)
    adv(OWN, 1, 2, layers - 2)
    adv(OWN, 2, 3, layers - 3)

    def relaxation(center, total):
        return (total - ion_charge(center) + screening * center) * (1.0 / (6.0 + screening))

    def make_base(x):
        center, sums = around(psi_v, (x + 2,), EDGE, window.size)
        for h in range(parts):
            total = psi_v[x + 1, h, window] + psi_v[x + 3, h, window] + sums[h]
            base[x + 1, h] = relaxation(center[h], total)

    loop(1, layers - 1, make_base)

    groups = [(0, layers - 1), (1, layers - 2), (2, layers - 3), tuple(range(3, layers - 3))]
    order = [x for group in groups for x in group]
    sent = []

    def send(copy):
        copy.start()
        sent.append(copy)
        return copy

    pl.semaphore_wait(barrier, len(near) + 2)
    fields = {
        x: send(pltpu.make_async_remote_copy(
            field_out.at[x], field_in.at[x], field_send.at[x], field_recv.at[x],
            device_id=partner, device_id_type=MESH,
        ))
        for x in order
    }
    edges = [
        send(pltpu.make_async_remote_copy(
            edge_out.at[d, pl.ds(first, count)], edge_in.at[d, pl.ds(first, count)],
            edge_send.at[d, n], edge_recv.at[d, n], device_id=targets[d], device_id_type=MESH,
        ))
        for n, (first, count) in enumerate(((0, 4), (4, 1))) for d in (0, 1)
    ]

    def halo(kind, d, first, count):
        return pltpu.make_async_remote_copy(
            halo_out.at[kind, d, pl.ds(first, count)], halo_in.at[kind, d, pl.ds(first, count)],
            halo_send.at[kind, d, first], halo_recv.at[kind, d, first],
            device_id=targets[d], device_id_type=MESH,
        )

    stages = len(near)

    def open_gate(stage):
        pl.semaphore_signal(gate.at[stage], inc=1, device_id=near[stage], device_id_type=MESH)

    def pass_gate(stage):
        pl.semaphore_wait(gate.at[stage], 1)
        if stage + 1 < stages:
            open_gate(stage + 1)

    open_gate(0)
    pass_gate(0)
    pass_gate(1)

    def arrive(group):
        for x in groups[group]:
            fields[x].wait_recv()
        for x in groups[group]:
            begin_chain(FOREIGN, x)

    copies = []
    for j in (0, 1):
        arrive(j)
        for d in (0, 1):
            halo_out[0, d, j] = write_log(u[FOREIGN, 0, out_layer(d, j) + 2], 1)
            copies.append(send(halo(0, d, j, 1)))

    pass_gate(2)
    for copy in edges[:2]:
        copy.wait_recv()
    for d in (0, 1):
        x = in_layer(d, 0)
        w_v[x + 1] = read_code(edge_in[d, 2], *w_span)
        psi_v[x + 2] = read_code(edge_in[d, 3], *psi_span)
        for j in (0, 1):
            u[OWN, 0, in_layer(d, j) + 2] = read_log(edge_in[d, j], 1)
    beyond(make_factor)
    beyond(functools.partial(advance_halo, OWN, 0))
    outer(functools.partial(advance, OWN, 0))

    def half_way(chain, kind):
        result = []
        for d in (0, 1):
            edge_pair(d, functools.partial(advance, chain, 1))
            for j in (0, 1):
                halo_out[kind, d, j] = write_log(u[chain, 2, out_layer(d, j) + 2], 5)
            result.append(send(halo(kind, d, 0, 2)))
        return result

    own_copies = half_way(OWN, 1)
    adv(OWN, 2, 1, 3)
    adv(OWN, 2, layers - 3, layers - 1)
    adv(OWN, 3, 2, layers - 2)

    pass_gate(3)
    arrive(2)
    adv(FOREIGN, 0, 1, 2)
    adv(FOREIGN, 0, layers - 2, layers - 1)
    arrive(3)
    adv(FOREIGN, 0, 2, layers - 2)
    adv(FOREIGN, 1, 2, layers - 2)
    adv(FOREIGN, 2, 3, layers - 3)
    for copy in copies:
        copy.wait_recv()
    for d in (0, 1):
        for j in (0, 1):
            u[FOREIGN, 0, in_layer(d, j) + 2] = read_log(halo_in[0, d, j], 1)
    beyond(functools.partial(advance_halo, FOREIGN, 0))
    outer(functools.partial(advance, FOREIGN, 0))
    foreign_copies = half_way(FOREIGN, 2)

    for stage in range(4, stages):
        pass_gate(stage)
    adv(FOREIGN, 2, 1, 3)
    adv(FOREIGN, 2, layers - 3, layers - 1)

    def second_half(chain, kind, copies):
        for copy in copies:
            copy.wait_recv()
        for d in (0, 1):
            for j in (0, 1):
                u[chain, 2, in_layer(d, j) + 2] = read_log(halo_in[kind, d, j], 5)
        beyond(functools.partial(advance_halo, chain, 2))
        outer(functools.partial(advance, chain, 2))

    weights = [0.5 if t in (0, NS) else 1.0 for t in range(NS + 1)]
    charged = [weights[t] * q[t] for t in range(NS + 1)]

    def gathered(x, h, terms):
        phi_layer, rho_layer = 0.0, 0.0
        for t in terms:
            product = rounded[OWN, t, x, h, window] * rounded[FOREIGN, NS - t, x, h, window]
            phi_layer = phi_layer + (product if weights[t] == 1.0 else weights[t] * product)
            rho_layer = rho_layer + charged[t] * product
        return phi_layer, rho_layer

    def gather(x):
        for h in range(parts):
            phi[x, h], rho[x + 1, h] = gathered(x, h, range(2, NS + 1))

    def complete(x, early):
        for h, value in enumerate(advanced(FOREIGN, NS - 1, x)):
            phi_layer, rho_layer = gathered(x, h, range(1, 2 if early else NS + 1))
            product = rounded[OWN, 0, x, h, window] * to_bfloat16(value)
            phi_layer = phi_layer + weights[0] * product
            rho_layer = rho_layer + charged[0] * product
            phi[x, h] = phi[x, h] + phi_layer if early else phi_layer
            rho[x + 1, h] = rho[x + 1, h] + rho_layer if early else rho_layer

    def whole(x):
        complete(x, False)

    def finish(x):
        complete(x, True)

    loop(2, layers - 2, whole)

    second_half(OWN, 1, own_copies)
    for d in (0, 1):
        edge_pair(d, functools.partial(advance, OWN, 3))

    def cells_of(x):
        return sum(phi[x, h, inner] for h in range(parts))

    partial = sum(cells_of(x) for x in range(2, layers - 2))

    for d in (0, 1):
        edge_pair(d, gather)

    for copy in edges[2:]:
        copy.wait_recv()
    for d in (0, 1):
        psi_v[in_layer(d, 1) + 2] = read_code(edge_in[d, 4], *psi_span)
    for k in (-1, 0):
        make_base(k)
        make_base(layers - 1 - k)

    second_half(FOREIGN, 2, foreign_copies)
    rho_copies = []
    for d in (0, 1):
        edge_pair(d, finish)
        rho_copies.append(pltpu.make_async_remote_copy(
            rho.at[out_layer(d, 0) + 1], rho.at[0 if d else layers + 1],
            rho_send.at[d], rho_recv.at[d], device_id=targets[d], device_id_type=MESH,
        ))
    for x in (0, 1, layers - 2, layers - 1):
        partial = partial + cells_of(x)
    sums[0] = jnp.sum(partial, axis=0, keepdims=True)

    def share(step, carry):
        pltpu.make_async_remote_copy(
            sums.at[0], sums.at[step], sum_send, sum_recv,
            device_id=device(step), device_id_type=MESH,
        ).start()
        return carry

    lax.fori_loop(1, devices, share, 0)
    for copy in rho_copies:
        send(copy)

    others = sums.at[pl.ds(1, devices - 1)]
    pltpu.make_async_copy(others, others, sum_recv).wait()
    cells = float(devices * layers * half * w_hbm.shape[2])
    inverse = cells / jnp.sum(sums[...])
    scaled = inverse * (1.0 / (6.0 + screening))

    def relax_once(x):
        for h in range(parts):
            relaxed[x + 1, h] = base[x + 1, h] + rho[x + 1, h] * scaled

    def first(x):
        for h in range(parts):
            density_ref[x, :, h * LANES:(h + 1) * LANES] = phi[x, h, inner] * inverse
        relax_once(x)

    loop(0, layers, first)

    def second(x):
        center, sums = around(relaxed, (x + 1,), PAD - EDGE, half)
        for h in range(parts):
            total = relaxed[x, h, inner] + relaxed[x + 2, h, inner] + sums[h]
            value = relaxation(center[h], total) + rho[x + 1, h, inner] * scaled
            potential_ref[x, :, h * LANES:(h + 1) * LANES] = value

    loop(1, layers - 1, second)
    for copy in rho_copies:
        copy.wait_recv()
    relax_once(-1)
    relax_once(layers)
    outer(second)

    for copy in sent:
        copy.wait_send()
    pltpu.make_async_copy(others, others, sum_send).wait()


def ion_charge(value):
    return (2.0 * screening) * jnp.tanh(0.5 * value)


def body(ends, slabs, w_field, psi_init, start_field, charges):
    layers, rows, depth = w_field.shape
    half = rows // ends
    wide = half + 2 * PAD
    devices = ends * slabs
    stages = slabs.bit_length()
    out = jax.ShapeDtypeStruct((layers, half, depth), jnp.float32)
    dma = pltpu.SemaphoreType.DMA

    parts = depth // LANES
    narrow = half + 2 * (PAD - EDGE)

    def tile(*lead):
        return pltpu.VMEM((*lead, parts, wide, LANES), jnp.float32)

    def slim(*lead):
        return pltpu.VMEM((*lead, parts, narrow, LANES), jnp.float32)

    def code(*lead):
        return pltpu.VMEM((*lead, parts, wide, LANES), jnp.int16)

    hbm = pl.BlockSpec(memory_space=pltpu.HBM)
    vmem = pl.BlockSpec(memory_space=pltpu.VMEM)
    return pl.pallas_call(
        functools.partial(kernel, ends, slabs),
        out_shape=(out, out),
        in_specs=[hbm, hbm, hbm, hbm],
        out_specs=(vmem, vmem),
        scratch_shapes=[
            pltpu.SMEM((NS + 1,), jnp.int32), tile(layers + 2), tile(layers + 4), tile(layers), tile(layers),
            tile(NS, layers + 2), tile(2, NS, layers + 4), tile(2, NS + 1, layers),
            slim(layers), slim(layers + 2), slim(layers + 2), slim(layers + 2),
            pltpu.VMEM((devices, 1, 128), jnp.float32),
            code(layers), code(layers), code(2, 5), code(2, 5), code(3, 2, 2), code(3, 2, 2),
            pltpu.SemaphoreType.REGULAR((stages,)), dma(()), dma((4, 3, parts)), dma((layers,)), dma((layers,)),
            dma((2, 2)), dma((2, 2)), dma((3, 2, 2)), dma((3, 2, 2)), dma((2,)), dma((2,)), dma(()), dma(()),
        ],
        compiler_params=pltpu.CompilerParams(
            collective_id=0, has_side_effects=True, vmem_limit_bytes=40 * 1024 * 1024
        ),
        name="scf_step",
    )(*[pltpu.with_memory_space_constraint(v, pltpu.HBM) for v in (charges, w_field, psi_init, start_field)])


def solution(mesh):
    in_specs = (P("slab", None, None), P("slab", None, None), P("end", "slab", None, None), P())
    out_specs = (P("slab", "end", None), P("slab", "end", None))
    step = functools.partial(body, mesh.shape["end"], mesh.shape["slab"])
    return jax.shard_map(step, mesh=mesh, in_specs=in_specs, out_specs=out_specs, check_vma=False)
```

```python
import functools
import math

import jax
import jax.numpy as jnp
from jax import lax
from jax.experimental import pallas as pl
from jax.experimental.pallas import tpu as pltpu
from jax.sharding import PartitionSpec as P

NS = 4
PAD = 8
EDGE = 4
LANES = 128
mobility = 0.15
screening = 1.0
OWN, FOREIGN = 0, 1
W_MAX, PSI_MAX = 4.0, 3.0
START_MIN, START_MAX = 0.25, 8.0
CODES, OFFSET = 65535.0, 32768
MARGIN = 0.001
MESH = pl.DeviceIdType.MESH


def kernel(ends, slabs, charges_hbm, w_hbm, psi_hbm, start_hbm, density_ref, potential_ref,
           charges_ref, w_v, psi_v, start_v, theirs_v, factor, u, rounded, phi, rho, base, relaxed, sums,
           field_out, field_in, edge_out, edge_in, halo_out, halo_in, rho_out, rho_in,
           gate, charges_sem, field_sem, local_sem, field_send, field_recv, edge_send, edge_recv, halo_send, halo_recv,
           rho_send, rho_recv, sum_send, sum_recv):
    side, slab = lax.axis_index("end"), lax.axis_index("slab")
    other = lax.rem(side + 1, ends)
    left = (side, lax.rem(slab + slabs - 1, slabs))
    right = (side, lax.rem(slab + 1, slabs))
    partner = (other, slab)
    layers, rows = w_hbm.shape[0], w_hbm.shape[1]
    half = rows // ends
    parts = w_hbm.shape[2] // LANES
    devices = ends * slabs
    flat = side * slabs + slab
    delta = 1.0 / NS

    def device(step):
        target = lax.rem(flat + step, devices)
        return (target // slabs, lax.rem(target, slabs))

    barrier = pltpu.get_barrier_semaphore()
    charges_copy = pltpu.make_async_copy(charges_hbm, charges_ref, charges_sem)
    charges_copy.start()

    near = []
    width = 1
    while width < slabs:
        near.append((side, slab + width - 2 * width * lax.rem(slab // width, 2)))
        width *= 2
    near.append(partner)
    for neighbour in near:
        pl.semaphore_signal(barrier, inc=1, device_id=neighbour, device_id_type=MESH)
    targets = (left, right)
    seams = (slab == 0, slab == slabs - 1)
    for d in (0, 1):
        @pl.when(jnp.logical_not(seams[d]))
        def _(d=d):
            pl.semaphore_signal(barrier, inc=1, device_id=targets[d], device_id_type=MESH)

    greeted = len(near) + jnp.where(slab % (slabs - 1) == 0, 1, 2)

    def pieces(which):
        first = which * half
        return (
            (pl.multiple_of(first, 8), PAD, half),
            (pl.multiple_of(lax.rem(first + rows - PAD, rows), 8), 0, PAD),
            (pl.multiple_of(lax.rem(first + half, rows), 8), PAD + half, PAD),
        )

    mine, theirs = pieces(side), pieces(other)
    groups = [(0, layers - 1), (1, layers - 2), (2, layers - 3), tuple(range(3, layers - 3))]
    order = [x for group in groups for x in group]
    field_copies = {
        x: [
            pltpu.make_async_copy(
                start_hbm.at[0, x, pl.ds(begin, count)], theirs_v.at[x, pl.ds(at, count)], field_sem.at[x, n],
            )
            for n, (begin, at, count) in enumerate(theirs)
        ]
        for x in order
    }
    for x in order:
        for copy in field_copies[x]:
            copy.start()
    local = [
        pltpu.make_async_copy(
            source.at[:, pl.ds(begin, count)], target.at[pl.ds(first, layers), pl.ds(at, count)], local_sem.at[k, n],
        )
        for k, (source, target, first) in enumerate(((w_hbm, w_v, 1), (start_hbm.at[0], start_v, 0)))
        for n, (begin, at, count) in enumerate(mine)
    ]
    local += [
        pltpu.make_async_copy(
            psi_hbm.at[:, pl.ds(begin, count), pl.ds(h * LANES, LANES)],
            psi_v.at[pl.ds(2, layers), h, pl.ds(at, count)], local_sem.at[2 + h, n],
        )
        for n, (begin, at, count) in enumerate(mine) for h in range(parts)
    ]
    for copy in local:
        copy.start()

    def loop(low, high, step):
        def body(x, carry):
            step(x)
            return carry

        lax.fori_loop(low, high, body, 0, unroll=True)

    def span(t):
        reach = 0.5 * delta * (W_MAX + PSI_MAX) * t + MARGIN
        shift = 0.5 * math.log(mobility) if t else 0.0
        return math.log(START_MIN) - reach + shift, math.log(START_MAX) + reach + shift

    def write_code(value, low, high):
        scaled = value * (CODES / (high - low)) + (0.5 - low * (CODES / (high - low)))
        return (scaled.astype(jnp.int32) - OFFSET).astype(jnp.int16)

    def read_code(code, low, high):
        step = (high - low) / CODES
        return code.astype(jnp.int32).astype(jnp.float32) * step + (low + OFFSET * step)

    def write_log(value, t):
        return write_code(jnp.log(value), *span(t))

    def read_log(code, t):
        return jnp.exp(read_code(code, *span(t)))

    w_span, psi_span = (-W_MAX - MARGIN, W_MAX + MARGIN), (-PSI_MAX - MARGIN, PSI_MAX + MARGIN)

    sent = []

    def send(copy):
        copy.start()
        sent.append(copy)
        return copy

    def plane(h):
        return slice(h * LANES, (h + 1) * LANES)

    fields = {}
    for group in groups:
        for x in group:
            for copy in field_copies[x]:
                copy.wait()
            for h in range(parts):
                field_out[x, h] = write_log(theirs_v[x, :, plane(h)], 0)
        if not fields:
            pl.semaphore_wait(barrier, greeted)
        for x in group:
            fields[x] = send(pltpu.make_async_remote_copy(
                field_out.at[x], field_in.at[x], field_send.at[x], field_recv.at[x],
                device_id=partner, device_id_type=MESH,
            ))

    charges_copy.wait()
    q = [charges_ref[side * (NS - 2 * t) + t].astype(jnp.float32) for t in range(NS + 1)]
    pair = [0.5 * (q[k] + q[k + 1]) for k in range(NS)]

    def make_factor(x):
        for h in range(parts):
            level = 0.5 * math.log(mobility) - 0.5 * delta * w_v[x + 1, :, plane(h)]
            psi = psi_v[x + 2, h]
            for k in range(NS):
                factor[k, x + 1, h] = jnp.exp(level - (0.5 * delta * pair[k]) * psi)

    def index(chain, t):
        return t if chain == OWN else NS - 1 - t

    def to_bfloat16(value):
        return value.astype(jnp.bfloat16).astype(jnp.float32)

    window = pl.ds(EDGE, half + 2 * (PAD - EDGE))
    inner = pl.ds(PAD - EDGE, half)

    def begin_chain(chain, x):
        for h in range(parts):
            value = start_v[x, :, plane(h)] if chain == OWN else read_log(field_in[x, h], 0)
            u[chain, 0, x + 2, h] = factor[index(chain, 0), x + 1, h] * value
            rounded[chain, 0, x, h] = to_bfloat16(value)

    lane = lax.broadcasted_iota(jnp.int32, (1, LANES), 1)
    lowest, highest = lane == 0, lane == LANES - 1

    def around(ref, at, first, count):
        center = [ref[(*at, h, pl.ds(first, count))] for h in range(parts)]
        lower = [pltpu.roll(value, 1, 1) for value in center]
        upper = [pltpu.roll(value, LANES - 1, 1) for value in center]
        sums = []
        for h in range(parts):
            total = ref[(*at, h, pl.ds(first - 1, count))] + ref[(*at, h, pl.ds(first + 1, count))]
            total = total + jnp.where(lowest, lower[h - 1], lower[h])
            sums.append(total + jnp.where(highest, upper[(h + 1) % parts], upper[h]))
        return center, sums

    def advanced(chain, t, x):
        center, sums = around(u, (chain, t, x + 2), EDGE, window.size)
        return [
            factor[index(chain, t), x + 1, h, window] * (
                (u[chain, t, x + 1, h, window] + u[chain, t, x + 3, h, window])
                + (sums[h] + ((1.0 - 6.0 * mobility) / mobility) * center[h])
            )
            for h in range(parts)
        ]

    def advance_halo(chain, t, x):
        for h, value in enumerate(advanced(chain, t, x)):
            u[chain, t + 1, x + 2, h, window] = factor[index(chain, t + 1), x + 1, h, window] * value

    def advance(chain, t, x):
        for h, value in enumerate(advanced(chain, t, x)):
            rounded[chain, t + 1, x, h, window] = to_bfloat16(value)
            if t + 1 < NS:
                u[chain, t + 1, x + 2, h, window] = factor[index(chain, t + 1), x + 1, h, window] * value

    def adv(chain, t, low, high):
        loop(low, high, functools.partial(advance, chain, t))

    def outer(step):
        loop(0, 2, lambda k: step((layers - 1) * k))

    def beyond(step):
        loop(0, 2, lambda k: step((layers + 1) * k - 1))

    def edge_pair(d, step):
        loop(0, 2, lambda j: step(j + d * (layers - 2)))

    def out_layer(d, j):
        return layers - 1 - j if d else j

    def in_layer(d, j):
        return -1 - j if d else layers + j

    for copy in local:
        copy.wait()
    for d in (0, 1):
        edge_pair(d, make_factor)
        edge_pair(d, functools.partial(begin_chain, OWN))

        def code_edge(j, d=d):
            x = out_layer(d, j)
            edge_out[d, j] = write_log(u[OWN, 0, x + 2], 1)
            edge_out[d, 3 + j] = write_code(psi_v[x + 2], *psi_span)

        loop(0, 2, code_edge)
        for h in range(parts):
            edge_out[d, 2, h] = write_code(w_v[out_layer(d, 0) + 1, :, plane(h)], *w_span)
    edges = [
        pltpu.make_async_remote_copy(
            edge_out.at[d, pl.ds(first, count)], edge_in.at[d, pl.ds(first, count)],
            edge_send.at[d, n], edge_recv.at[d, n], device_id=targets[d], device_id_type=MESH,
        )
        for n, (first, count) in enumerate(((0, 4), (4, 1))) for d in (0, 1)
    ]
    sent += edges

    def send_edges(seam):
        for d in (0, 1):
            @pl.when(seams[d] if seam else jnp.logical_not(seams[d]))
            def _(d=d):
                edges[d].start()
                edges[2 + d].start()

    send_edges(False)
    stages = len(near)

    def open_gate(stage):
        pl.semaphore_signal(gate.at[stage], inc=1, device_id=near[stage], device_id_type=MESH)

    def pass_gate(stage):
        pl.semaphore_wait(gate.at[stage], 1)
        if stage + 1 < stages:
            open_gate(stage + 1)

    open_gate(0)
    loop(2, layers - 2, make_factor)
    loop(2, layers - 2, functools.partial(begin_chain, OWN))
    pass_gate(0)
    adv(OWN, 0, 1, layers - 1)
    adv(OWN, 1, 2, layers - 2)
    pass_gate(1)
    adv(OWN, 2, 3, layers - 3)

    def relaxation(center, total):
        return (total - ion_charge(center) + screening * center) * (1.0 / (6.0 + screening))

    def make_base(x):
        center, sums = around(psi_v, (x + 2,), EDGE, window.size)
        for h in range(parts):
            total = psi_v[x + 1, h, window] + psi_v[x + 3, h, window] + sums[h]
            base[x + 1, h] = relaxation(center[h], total)

    loop(1, layers - 1, make_base)
    for stage in range(2, stages - 1):
        pass_gate(stage)
    send_edges(True)

    def halo(kind, d, first, count):
        return pltpu.make_async_remote_copy(
            halo_out.at[kind, d, pl.ds(first, count)], halo_in.at[kind, d, pl.ds(first, count)],
            halo_send.at[kind, d, first], halo_recv.at[kind, d, first],
            device_id=targets[d], device_id_type=MESH,
        )

    def arrive(group):
        for x in groups[group]:
            fields[x].wait_recv()
        for x in groups[group]:
            begin_chain(FOREIGN, x)

    copies = []
    for j in (0, 1):
        arrive(j)
        for d in (0, 1):
            halo_out[0, d, j] = write_log(u[FOREIGN, 0, out_layer(d, j) + 2], 1)
            copies.append(send(halo(0, d, j, 1)))

    for copy in edges[:2]:
        copy.wait_recv()
    for d in (0, 1):
        x = in_layer(d, 0)
        for h in range(parts):
            w_v[x + 1, :, plane(h)] = read_code(edge_in[d, 2, h], *w_span)
        psi_v[x + 2] = read_code(edge_in[d, 3], *psi_span)
        for j in (0, 1):
            u[OWN, 0, in_layer(d, j) + 2] = read_log(edge_in[d, j], 1)
    beyond(make_factor)
    beyond(functools.partial(advance_halo, OWN, 0))
    outer(functools.partial(advance, OWN, 0))

    def half_way(chain, kind):
        result = []
        for d in (0, 1):
            edge_pair(d, functools.partial(advance, chain, 1))
            for j in (0, 1):
                halo_out[kind, d, j] = write_log(u[chain, 2, out_layer(d, j) + 2], 5)
            result.append(send(halo(kind, d, 0, 2)))
        return result

    own_copies = half_way(OWN, 1)
    adv(OWN, 2, 1, 3)
    adv(OWN, 2, layers - 3, layers - 1)
    adv(OWN, 3, 2, layers - 2)

    arrive(2)
    adv(FOREIGN, 0, 1, 2)
    adv(FOREIGN, 0, layers - 2, layers - 1)
    arrive(3)
    adv(FOREIGN, 0, 2, layers - 2)
    adv(FOREIGN, 1, 2, layers - 2)
    adv(FOREIGN, 2, 3, layers - 3)
    for copy in copies:
        copy.wait_recv()
    for d in (0, 1):
        for j in (0, 1):
            u[FOREIGN, 0, in_layer(d, j) + 2] = read_log(halo_in[0, d, j], 1)
    beyond(functools.partial(advance_halo, FOREIGN, 0))
    outer(functools.partial(advance, FOREIGN, 0))
    foreign_copies = half_way(FOREIGN, 2)

    pass_gate(stages - 1)
    adv(FOREIGN, 2, 1, 3)
    adv(FOREIGN, 2, layers - 3, layers - 1)

    def second_half(chain, kind, copies):
        for copy in copies:
            copy.wait_recv()
        for d in (0, 1):
            for j in (0, 1):
                u[chain, 2, in_layer(d, j) + 2] = read_log(halo_in[kind, d, j], 5)
        beyond(functools.partial(advance_halo, chain, 2))
        outer(functools.partial(advance, chain, 2))

    weights = [0.5 if t in (0, NS) else 1.0 for t in range(NS + 1)]
    charged = [weights[t] * q[t] for t in range(NS + 1)]

    def gathered(x, h, terms):
        phi_layer, rho_layer = 0.0, 0.0
        for t in terms:
            product = rounded[OWN, t, x, h, window] * rounded[FOREIGN, NS - t, x, h, window]
            phi_layer = phi_layer + (product if weights[t] == 1.0 else weights[t] * product)
            rho_layer = rho_layer + charged[t] * product
        return phi_layer, rho_layer

    def gather(x):
        for h in range(parts):
            phi[x, h], rho[x + 1, h] = gathered(x, h, range(2, NS + 1))

    def complete(x, early):
        for h, value in enumerate(advanced(FOREIGN, NS - 1, x)):
            phi_layer, rho_layer = gathered(x, h, range(1, 2 if early else NS + 1))
            product = rounded[OWN, 0, x, h, window] * to_bfloat16(value)
            phi_layer = phi_layer + weights[0] * product
            rho_layer = rho_layer + charged[0] * product
            phi[x, h] = phi[x, h] + phi_layer if early else phi_layer
            rho[x + 1, h] = rho[x + 1, h] + rho_layer if early else rho_layer

    def whole(x):
        complete(x, False)

    def finish(x):
        complete(x, True)

    loop(2, layers - 2, whole)

    second_half(OWN, 1, own_copies)
    for d in (0, 1):
        edge_pair(d, functools.partial(advance, OWN, 3))

    def cells_of(x):
        return sum(phi[x, h, inner] for h in range(parts))

    partial = sum(cells_of(x) for x in range(2, layers - 2))

    for d in (0, 1):
        edge_pair(d, gather)

    for copy in edges[2:]:
        copy.wait_recv()
    for d in (0, 1):
        psi_v[in_layer(d, 1) + 2] = read_code(edge_in[d, 4], *psi_span)
    for k in (-1, 0):
        make_base(k)
        make_base(layers - 1 - k)

    second_half(FOREIGN, 2, foreign_copies)
    rho_copies = []
    for d in (0, 1):
        edge_pair(d, finish)
        rho_out[d] = rho[out_layer(d, 0) + 1].astype(jnp.bfloat16)
        rho_copies.append(send(pltpu.make_async_remote_copy(
            rho_out.at[d], rho_in.at[d], rho_send.at[d], rho_recv.at[d], device_id=targets[d], device_id_type=MESH,
        )))
    for x in (0, 1, layers - 2, layers - 1):
        partial = partial + cells_of(x)
    sums[0] = jnp.sum(partial, axis=0, keepdims=True)

    def share(step, carry):
        pltpu.make_async_remote_copy(
            sums.at[0], sums.at[step], sum_send, sum_recv,
            device_id=device(step), device_id_type=MESH,
        ).start()
        return carry

    lax.fori_loop(1, devices, share, 0)

    others = sums.at[pl.ds(1, devices - 1)]
    pltpu.make_async_copy(others, others, sum_recv).wait()
    cells = float(devices * layers * half * w_hbm.shape[2])
    inverse = cells / jnp.sum(sums[...])
    scaled = inverse * (1.0 / (6.0 + screening))

    def relax_once(x):
        for h in range(parts):
            relaxed[x + 1, h] = base[x + 1, h] + rho[x + 1, h] * scaled

    def first(x):
        for h in range(parts):
            density_ref[x, :, h * LANES:(h + 1) * LANES] = phi[x, h, inner] * inverse
        relax_once(x)

    loop(0, layers, first)

    def second(x):
        center, sums = around(relaxed, (x + 1,), PAD - EDGE, half)
        for h in range(parts):
            total = relaxed[x, h, inner] + relaxed[x + 2, h, inner] + sums[h]
            value = relaxation(center[h], total) + rho[x + 1, h, inner] * scaled
            potential_ref[x, :, h * LANES:(h + 1) * LANES] = value

    loop(1, layers - 1, second)
    for copy in rho_copies:
        copy.wait_recv()
    for d in (0, 1):
        rho[in_layer(d, 0) + 1] = rho_in[d].astype(jnp.float32)
        relax_once(in_layer(d, 0))
    outer(second)

    for copy in sent:
        copy.wait_send()
    pltpu.make_async_copy(others, others, sum_send).wait()


def ion_charge(value):
    return (2.0 * screening) * jnp.tanh(0.5 * value)


def body(ends, slabs, w_field, psi_init, start_field, charges):
    layers, rows, depth = w_field.shape
    half = rows // ends
    wide = half + 2 * PAD
    devices = ends * slabs
    stages = slabs.bit_length()
    out = jax.ShapeDtypeStruct((layers, half, depth), jnp.float32)
    dma = pltpu.SemaphoreType.DMA

    parts = depth // LANES
    narrow = half + 2 * (PAD - EDGE)

    def tile(*lead):
        return pltpu.VMEM((*lead, parts, wide, LANES), jnp.float32)

    def slim(*lead):
        return pltpu.VMEM((*lead, parts, narrow, LANES), jnp.float32)

    def whole_rows(*lead):
        return pltpu.VMEM((*lead, wide, depth), jnp.float32)

    edge_rho = pltpu.VMEM((2, parts, narrow, LANES), jnp.bfloat16)

    def code(*lead):
        return pltpu.VMEM((*lead, parts, wide, LANES), jnp.int16)

    hbm = pl.BlockSpec(memory_space=pltpu.HBM)
    vmem = pl.BlockSpec(memory_space=pltpu.VMEM)
    return pl.pallas_call(
        functools.partial(kernel, ends, slabs),
        out_shape=(out, out),
        in_specs=[hbm, hbm, hbm, hbm],
        out_specs=(vmem, vmem),
        scratch_shapes=[
            pltpu.SMEM((NS + 1,), jnp.int32), whole_rows(layers + 2), tile(layers + 4), whole_rows(layers), whole_rows(layers),
            tile(NS, layers + 2), tile(2, NS, layers + 4), tile(2, NS + 1, layers),
            slim(layers), slim(layers + 2), slim(layers + 2), slim(layers + 2),
            pltpu.VMEM((devices, 1, LANES), jnp.float32),
            code(layers), code(layers), code(2, 5), code(2, 5), code(3, 2, 2), code(3, 2, 2), edge_rho, edge_rho,
            pltpu.SemaphoreType.REGULAR((stages,)), dma(()), dma((layers, 3)), dma((2 + parts, 3)), dma((layers,)), dma((layers,)),
            dma((2, 2)), dma((2, 2)), dma((3, 2, 2)), dma((3, 2, 2)), dma((2,)), dma((2,)), dma(()), dma(()),
        ],
        compiler_params=pltpu.CompilerParams(
            collective_id=0, has_side_effects=True, vmem_limit_bytes=40 * 1024 * 1024
        ),
        name="scf_step",
    )(*[pltpu.with_memory_space_constraint(v, pltpu.HBM) for v in (charges, w_field, psi_init, start_field)])


def solution(mesh):
    in_specs = (P("slab", None, None), P("slab", None, None), P("end", "slab", None, None), P())
    out_specs = (P("slab", "end", None), P("slab", "end", None))
    step = functools.partial(body, mesh.shape["end"], mesh.shape["slab"])
    return jax.shard_map(step, mesh=mesh, in_specs=in_specs, out_specs=out_specs, check_vma=False)
```

```python
import functools
import math

import jax
import jax.numpy as jnp
from jax import lax
from jax.experimental import pallas as pl
from jax.experimental.pallas import tpu as pltpu
from jax.sharding import PartitionSpec as P

NS = 4
PAD = 8
EDGE = 4
LANES = 128
mobility = 0.15
screening = 1.0
OWN, FOREIGN = 0, 1
W_MAX, PSI_MAX = 4.0, 3.0
START_MIN, START_MAX = 0.25, 8.0
CODES, OFFSET = 65535.0, 32768
MARGIN = 0.001
MESH = pl.DeviceIdType.MESH


def kernel(ends, slabs, charges_hbm, w_hbm, psi_hbm, start_hbm, density_ref, potential_ref,
           charges_ref, w_v, psi_v, start_v, theirs_v, factor, u, rounded, phi, rho, base, relaxed, sums,
           field_out, field_in, edge_out, edge_in, halo_out, halo_in, rho_out, rho_in,
           gate, seam_gate, charges_sem, field_sem, local_sem, field_send, field_recv, edge_send, edge_recv, halo_send, halo_recv,
           rho_send, rho_recv, sum_send, sum_recv):
    side, slab = lax.axis_index("end"), lax.axis_index("slab")
    other = lax.rem(side + 1, ends)
    left = (side, lax.rem(slab + slabs - 1, slabs))
    right = (side, lax.rem(slab + 1, slabs))
    partner = (other, slab)
    layers, rows = w_hbm.shape[0], w_hbm.shape[1]
    half = rows // ends
    parts = w_hbm.shape[2] // LANES
    devices = ends * slabs
    flat = side * slabs + slab
    delta = 1.0 / NS

    def device(distance):
        target = lax.rem(flat + distance, devices)
        return (target // slabs, lax.rem(target, slabs))

    barrier = pltpu.get_barrier_semaphore()
    charges_copy = pltpu.make_async_copy(charges_hbm, charges_ref, charges_sem)
    charges_copy.start()

    near = []
    width = 1
    while width < slabs:
        near.append((side, slab + width - 2 * width * lax.rem(slab // width, 2)))
        width *= 2
    near.append(partner)
    first_slab, last_slab = slab == 0, slab == slabs - 1
    for neighbour in near + [left]:
        pl.semaphore_signal(barrier, inc=1, device_id=neighbour, device_id_type=MESH)

    @pl.when(jnp.logical_not(last_slab))
    def _():
        pl.semaphore_signal(barrier, inc=1, device_id=right, device_id_type=MESH)

    greeted = len(near) + jnp.where(first_slab, 1, 2)
    targets = (left, right)

    def pieces(which):
        first = which * half
        return (
            (pl.multiple_of(first, 8), PAD, half),
            (pl.multiple_of(lax.rem(first + rows - PAD, rows), 8), 0, PAD),
            (pl.multiple_of(lax.rem(first + half, rows), 8), PAD + half, PAD),
        )

    mine, theirs = pieces(side), pieces(other)
    groups = [(0, layers - 1), (1, layers - 2), (2, layers - 3), tuple(range(3, layers - 3))]
    firsts = [sum(len(group) for group in groups[:k]) for k in range(len(groups))]
    slots = [pl.ds(first, len(group)) for first, group in zip(firsts, groups)]
    slot_of = {x: first + k for first, group in zip(firsts, groups) for k, x in enumerate(group)}
    for k, group in enumerate(groups):
        for x in group:
            for begin, at, count in theirs:
                pltpu.make_async_copy(
                    start_hbm.at[0, x, pl.ds(begin, count)], theirs_v.at[slot_of[x], pl.ds(at, count)], field_sem.at[k],
                ).start()
    for begin, at, count in mine:
        pltpu.make_async_copy(
            w_hbm.at[:, pl.ds(begin, count)], w_v.at[pl.ds(1, layers), pl.ds(at, count)], local_sem.at[0],
        ).start()
        for h in range(parts):
            pltpu.make_async_copy(
                psi_hbm.at[:, pl.ds(begin, count), pl.ds(h * LANES, LANES)],
                psi_v.at[pl.ds(2, layers), h, pl.ds(at, count)], local_sem.at[1],
            ).start()
        pltpu.make_async_copy(
            start_hbm.at[0, :, pl.ds(begin, count)], start_v.at[:, pl.ds(at, count)], local_sem.at[2],
        ).start()

    def taken(ref, semaphore):
        pltpu.make_async_copy(ref, ref, semaphore).wait()

    def loop(low, high, step):
        def body(x, carry):
            step(x)
            return carry

        lax.fori_loop(low, high, body, 0, unroll=True)

    def span(t):
        reach = 0.5 * delta * (W_MAX + PSI_MAX) * t + MARGIN
        shift = 0.5 * math.log(mobility) if t else 0.0
        return math.log(START_MIN) - reach + shift, math.log(START_MAX) + reach + shift

    def write_code(value, low, high):
        scaled = value * (CODES / (high - low)) + (0.5 - low * (CODES / (high - low)))
        return (scaled.astype(jnp.int32) - OFFSET).astype(jnp.int16)

    def read_code(code, low, high):
        step = (high - low) / CODES
        return code.astype(jnp.int32).astype(jnp.float32) * step + (low + OFFSET * step)

    def write_log(value, t):
        return write_code(jnp.log(value), *span(t))

    def read_log(code, t):
        return jnp.exp(read_code(code, *span(t)))

    w_span, psi_span = (-W_MAX - MARGIN, W_MAX + MARGIN), (-PSI_MAX - MARGIN, PSI_MAX + MARGIN)

    def plane(h):
        return slice(h * LANES, (h + 1) * LANES)

    for k, group in enumerate(groups):
        taken(theirs_v.at[slots[k]], field_sem.at[k])
        for x in group:
            for h in range(parts):
                field_out[slot_of[x], h] = write_log(theirs_v[slot_of[x], :, plane(h)], 0)
        if k == 0:
            pl.semaphore_wait(barrier, greeted)

            @pl.when(last_slab)
            def _():
                pl.semaphore_signal(seam_gate, inc=1, device_id=right, device_id_type=MESH)

        pltpu.make_async_remote_copy(
            field_out.at[slots[k]], field_in.at[slots[k]], field_send, field_recv.at[k],
            device_id=partner, device_id_type=MESH,
        ).start()

    charges_copy.wait()
    q = [charges_ref[side * (NS - 2 * t) + t].astype(jnp.float32) for t in range(NS + 1)]
    pair = [0.5 * (q[k] + q[k + 1]) for k in range(NS)]

    def make_factor(x):
        for h in range(parts):
            level = 0.5 * math.log(mobility) - 0.5 * delta * w_v[x + 1, :, plane(h)]
            psi = psi_v[x + 2, h]
            for k in range(NS):
                factor[k, x + 1, h] = jnp.exp(level - (0.5 * delta * pair[k]) * psi)

    def index(chain, t):
        return t if chain == OWN else NS - 1 - t

    def to_bfloat16(value):
        return value.astype(jnp.bfloat16).astype(jnp.float32)

    window = pl.ds(EDGE, half + 2 * (PAD - EDGE))
    inner = pl.ds(PAD - EDGE, half)

    def begin_chain(chain, x):
        for h in range(parts):
            value = start_v[x, :, plane(h)] if chain == OWN else read_log(field_in[slot_of[x], h], 0)
            u[chain, 0, x + 2, h] = factor[index(chain, 0), x + 1, h] * value
            rounded[chain, 0, x, h] = to_bfloat16(value)

    lane = lax.broadcasted_iota(jnp.int32, (1, LANES), 1)
    lowest, highest = lane == 0, lane == LANES - 1

    def around(ref, at, first, count):
        center = [ref[(*at, h, pl.ds(first, count))] for h in range(parts)]
        lower = [pltpu.roll(value, 1, 1) for value in center]
        upper = [pltpu.roll(value, LANES - 1, 1) for value in center]
        sums = []
        for h in range(parts):
            total = ref[(*at, h, pl.ds(first - 1, count))] + ref[(*at, h, pl.ds(first + 1, count))]
            total = total + jnp.where(lowest, lower[h - 1], lower[h])
            sums.append(total + jnp.where(highest, upper[(h + 1) % parts], upper[h]))
        return center, sums

    def advanced(chain, t, x):
        center, sums = around(u, (chain, t, x + 2), EDGE, window.size)
        return [
            factor[index(chain, t), x + 1, h, window] * (
                (u[chain, t, x + 1, h, window] + u[chain, t, x + 3, h, window])
                + (sums[h] + ((1.0 - 6.0 * mobility) / mobility) * center[h])
            )
            for h in range(parts)
        ]

    def advance_halo(chain, t, x):
        for h, value in enumerate(advanced(chain, t, x)):
            u[chain, t + 1, x + 2, h, window] = factor[index(chain, t + 1), x + 1, h, window] * value

    def advance(chain, t, x):
        for h, value in enumerate(advanced(chain, t, x)):
            rounded[chain, t + 1, x, h, window] = to_bfloat16(value)
            if t + 1 < NS:
                u[chain, t + 1, x + 2, h, window] = factor[index(chain, t + 1), x + 1, h, window] * value

    def adv(chain, t, low, high):
        loop(low, high, functools.partial(advance, chain, t))

    def outer(step):
        loop(0, 2, lambda k: step((layers - 1) * k))

    def ring(first, step):
        loop(0, 2, lambda k: step(first + (layers - 1 - 2 * first) * k))

    def beyond(step):
        loop(0, 2, lambda k: step((layers + 1) * k - 1))

    def edge_pair(d, step):
        loop(0, 2, lambda j: step(j + d * (layers - 2)))

    def out_layer(d, j):
        return layers - 1 - j if d else j

    def in_layer(d, j):
        return -1 - j if d else layers + j

    taken(w_v.at[pl.ds(1, layers)], local_sem.at[0])
    taken(psi_v.at[pl.ds(2, layers)], local_sem.at[1])
    taken(start_v, local_sem.at[2])
    for d in (0, 1):
        edge_pair(d, make_factor)
        edge_pair(d, functools.partial(begin_chain, OWN))

        def code_edge(j, d=d):
            x = out_layer(d, j)
            edge_out[d, j] = write_log(u[OWN, 0, x + 2], 1)
            edge_out[d, 3 + j] = write_code(psi_v[x + 2], *psi_span)

        loop(0, 2, code_edge)
        for h in range(parts):
            edge_out[d, 2, h] = write_code(w_v[out_layer(d, 0) + 1, :, plane(h)], *w_span)
    edges = [
        pltpu.make_async_remote_copy(
            edge_out.at[d, pl.ds(first, count)], edge_in.at[d, pl.ds(first, count)],
            edge_send, edge_recv.at[n], device_id=targets[d], device_id_type=MESH,
        )
        for n, (first, count) in enumerate(((0, 4), (4, 1))) for d in (0, 1)
    ]

    @pl.when(jnp.logical_not(first_slab))
    def _():
        edges[0].start()
        edges[2].start()

    edges[1].start()
    edges[3].start()
    stages = len(near)

    def open_gate(stage):
        pl.semaphore_signal(gate.at[stage], inc=1, device_id=near[stage], device_id_type=MESH)

    def pass_gate(stage):
        pl.semaphore_wait(gate.at[stage], 1)
        if stage + 1 < stages:
            open_gate(stage + 1)

    open_gate(0)
    loop(2, layers - 2, make_factor)
    loop(2, layers - 2, functools.partial(begin_chain, OWN))
    pass_gate(0)
    adv(OWN, 0, 1, layers - 1)
    adv(OWN, 1, 2, layers - 2)
    adv(OWN, 2, 3, layers - 3)

    def relaxation(center, total):
        return (total - ion_charge(center) + screening * center) * (1.0 / (6.0 + screening))

    def make_base(x):
        center, sums = around(psi_v, (x + 2,), EDGE, window.size)
        for h in range(parts):
            total = psi_v[x + 1, h, window] + psi_v[x + 3, h, window] + sums[h]
            base[x + 1, h] = relaxation(center[h], total)

    @pl.when(first_slab)
    def _():
        pl.semaphore_wait(seam_gate, 1)
        edges[0].start()
        edges[2].start()

    loop(1, layers - 1, make_base)
    pass_gate(1)

    def halo(kind, d, first, count):
        return pltpu.make_async_remote_copy(
            halo_out.at[kind, d, pl.ds(first, count)], halo_in.at[kind, d, pl.ds(first, count)],
            halo_send, halo_recv.at[kind],
            device_id=targets[d], device_id_type=MESH,
        )

    def arrive(group):
        taken(field_in.at[slots[group]], field_recv.at[group])
        for x in groups[group]:
            begin_chain(FOREIGN, x)

    for j in (0, 1):
        arrive(j)
        for d in (0, 1):
            halo_out[0, d, j] = write_log(u[FOREIGN, 0, out_layer(d, j) + 2], 1)
            halo(0, d, j, 1).start()

    pass_gate(2)
    taken(edge_in.at[:, pl.ds(0, 4)], edge_recv.at[0])
    for d in (0, 1):
        x = in_layer(d, 0)
        for h in range(parts):
            w_v[x + 1, :, plane(h)] = read_code(edge_in[d, 2, h], *w_span)
        psi_v[x + 2] = read_code(edge_in[d, 3], *psi_span)
        for j in (0, 1):
            u[OWN, 0, in_layer(d, j) + 2] = read_log(edge_in[d, j], 1)
    beyond(make_factor)
    beyond(functools.partial(advance_halo, OWN, 0))
    outer(functools.partial(advance, OWN, 0))

    def half_way(chain, kind):
        for d in (0, 1):
            edge_pair(d, functools.partial(advance, chain, 1))
            for j in (0, 1):
                halo_out[kind, d, j] = write_log(u[chain, 2, out_layer(d, j) + 2], 5)
            halo(kind, d, 0, 2).start()

    half_way(OWN, 1)
    arrive(2)
    ring(1, functools.partial(advance, FOREIGN, 0))
    arrive(3)
    ring(2, functools.partial(advance, FOREIGN, 0))
    taken(halo_in.at[0], halo_recv.at[0])
    for d in (0, 1):
        for j in (0, 1):
            u[FOREIGN, 0, in_layer(d, j) + 2] = read_log(halo_in[0, d, j], 1)
    beyond(functools.partial(advance_halo, FOREIGN, 0))
    outer(functools.partial(advance, FOREIGN, 0))
    half_way(FOREIGN, 2)

    adv(FOREIGN, 0, 3, layers - 3)
    for stage in range(3, stages - 1):
        pass_gate(stage)
    adv(OWN, 2, 1, 3)
    adv(OWN, 2, layers - 3, layers - 1)
    adv(OWN, 3, 2, layers - 2)
    adv(FOREIGN, 1, 2, layers - 2)
    adv(FOREIGN, 2, 1, layers - 1)

    def second_half(chain, kind):
        taken(halo_in.at[kind], halo_recv.at[kind])
        for d in (0, 1):
            for j in (0, 1):
                u[chain, 2, in_layer(d, j) + 2] = read_log(halo_in[kind, d, j], 5)
        beyond(functools.partial(advance_halo, chain, 2))
        outer(functools.partial(advance, chain, 2))

    weights = [0.5 if t in (0, NS) else 1.0 for t in range(NS + 1)]
    charged = [weights[t] * q[t] for t in range(NS + 1)]

    def gathered(x, h, terms):
        phi_layer, rho_layer = 0.0, 0.0
        for t in terms:
            product = rounded[OWN, t, x, h, window] * rounded[FOREIGN, NS - t, x, h, window]
            phi_layer = phi_layer + (product if weights[t] == 1.0 else weights[t] * product)
            rho_layer = rho_layer + charged[t] * product
        return phi_layer, rho_layer

    def gather(x):
        for h in range(parts):
            phi[x, h], rho[x + 1, h] = gathered(x, h, range(2, NS + 1))

    def complete(x, early):
        for h, value in enumerate(advanced(FOREIGN, NS - 1, x)):
            phi_layer, rho_layer = gathered(x, h, range(1, 2 if early else NS + 1))
            product = rounded[OWN, 0, x, h, window] * to_bfloat16(value)
            phi_layer = phi_layer + weights[0] * product
            rho_layer = rho_layer + charged[0] * product
            phi[x, h] = phi[x, h] + phi_layer if early else phi_layer
            rho[x + 1, h] = rho[x + 1, h] + rho_layer if early else rho_layer

    def whole(x):
        complete(x, False)

    def finish(x):
        complete(x, True)

    loop(2, layers - 2, whole)

    pass_gate(stages - 1)
    second_half(OWN, 1)
    for d in (0, 1):
        edge_pair(d, functools.partial(advance, OWN, 3))

    def cells_of(x):
        return sum(phi[x, h, inner] for h in range(parts))

    partial = sum(cells_of(x) for x in range(2, layers - 2))

    for d in (0, 1):
        edge_pair(d, gather)

    taken(edge_in.at[:, pl.ds(4, 1)], edge_recv.at[1])
    for d in (0, 1):
        psi_v[in_layer(d, 1) + 2] = read_code(edge_in[d, 4], *psi_span)
    for k in (-1, 0):
        make_base(k)
        make_base(layers - 1 - k)

    steps = sorted(range(1, devices), key=lambda k: -min(k % slabs, slabs - k % slabs))
    receivers = [(k, device(k)) for k in steps] if devices <= 32 else None
    second_half(FOREIGN, 2)
    for d in (0, 1):
        edge_pair(d, finish)
        rho_out[d] = rho[out_layer(d, 0) + 1].astype(jnp.bfloat16)
        pltpu.make_async_remote_copy(
            rho_out.at[d], rho_in.at[d], rho_send, rho_recv, device_id=targets[d], device_id_type=MESH,
        ).start()
    for x in (0, 1, layers - 2, layers - 1):
        partial = partial + cells_of(x)
    sums[0] = jnp.sum(partial, axis=0, keepdims=True)

    def share(step, target):
        pltpu.make_async_remote_copy(
            sums.at[0], sums.at[step], sum_send, sum_recv, device_id=target, device_id_type=MESH,
        ).start()

    if receivers is not None:
        for step, target in receivers:
            share(step, target)
    else:
        lax.fori_loop(1, devices, lambda step, carry: (share(step, device(step)), carry)[1], 0)

    others = sums.at[pl.ds(1, devices - 1)]
    taken(others, sum_recv)
    cells = float(devices * layers * half * w_hbm.shape[2])
    inverse = cells / jnp.sum(sums[...])
    scaled = inverse * (1.0 / (6.0 + screening))

    def relax_once(x):
        for h in range(parts):
            relaxed[x + 1, h] = base[x + 1, h] + rho[x + 1, h] * scaled

    def first(x):
        for h in range(parts):
            density_ref[x, :, h * LANES:(h + 1) * LANES] = phi[x, h, inner] * inverse
        relax_once(x)

    loop(0, layers, first)

    def second(x):
        center, sums = around(relaxed, (x + 1,), PAD - EDGE, half)
        for h in range(parts):
            total = relaxed[x, h, inner] + relaxed[x + 2, h, inner] + sums[h]
            value = relaxation(center[h], total) + rho[x + 1, h, inner] * scaled
            potential_ref[x, :, h * LANES:(h + 1) * LANES] = value

    loop(1, layers - 1, second)
    taken(rho_in, rho_recv)
    for d in (0, 1):
        rho[in_layer(d, 0) + 1] = rho_in[d].astype(jnp.float32)
        relax_once(in_layer(d, 0))
    outer(second)

    for ref, semaphore in (
        (field_out, field_send), (edge_out, edge_send), (halo_out, halo_send), (rho_out, rho_send), (others, sum_send)
    ):
        taken(ref, semaphore)


def ion_charge(value):
    return (2.0 * screening) * jnp.tanh(0.5 * value)


def store(density_v, potential_v, density_hbm, potential_hbm, sems):
    copies = [
        pltpu.make_async_copy(source, target, sems.at[k])
        for k, (source, target) in enumerate(((density_v, density_hbm), (potential_v, potential_hbm)))
    ]
    for copy in copies:
        copy.start()
    for copy in copies:
        copy.wait()


def body(ends, slabs, w_field, psi_init, start_field, charges):
    layers, rows, depth = w_field.shape
    half = rows // ends
    wide = half + 2 * PAD
    devices = ends * slabs
    stages = slabs.bit_length()
    out = jax.ShapeDtypeStruct((layers, half, depth), jnp.float32)
    dma = pltpu.SemaphoreType.DMA

    parts = depth // LANES
    narrow = half + 2 * (PAD - EDGE)

    def tile(*lead):
        return pltpu.VMEM((*lead, parts, wide, LANES), jnp.float32)

    def slim(*lead):
        return pltpu.VMEM((*lead, parts, narrow, LANES), jnp.float32)

    def whole_rows(*lead):
        return pltpu.VMEM((*lead, wide, depth), jnp.float32)

    edge_rho = pltpu.VMEM((2, parts, narrow, LANES), jnp.bfloat16)

    def code(*lead):
        return pltpu.VMEM((*lead, parts, wide, LANES), jnp.int16)

    hbm = pl.BlockSpec(memory_space=pltpu.HBM)
    vmem = pl.BlockSpec(memory_space=pltpu.VMEM)
    density, potential = pl.pallas_call(
        functools.partial(kernel, ends, slabs),
        out_shape=(out, out),
        in_specs=[hbm, hbm, hbm, hbm],
        out_specs=(vmem, vmem),
        scratch_shapes=[
            pltpu.SMEM((NS + 1,), jnp.int32), whole_rows(layers + 2), tile(layers + 4), whole_rows(layers), whole_rows(layers),
            tile(NS, layers + 2), tile(2, NS, layers + 4), tile(2, NS + 1, layers),
            slim(layers), slim(layers + 2), slim(layers + 2), slim(layers + 2),
            pltpu.VMEM((devices, 1, LANES), jnp.float32),
            code(layers), code(layers), code(2, 5), code(2, 5), code(3, 2, 2), code(3, 2, 2), edge_rho, edge_rho,
            pltpu.SemaphoreType.REGULAR((stages,)), pltpu.SemaphoreType.REGULAR, dma(()), dma((4,)), dma((3,)), dma(()), dma((4,)),
            dma(()), dma((2,)), dma(()), dma((3,)), dma(()), dma(()), dma(()), dma(()),
        ],
        compiler_params=pltpu.CompilerParams(
            collective_id=0, has_side_effects=True, vmem_limit_bytes=40 * 1024 * 1024
        ),
        name="scf_step",
    )(*[pltpu.with_memory_space_constraint(v, pltpu.HBM) for v in (charges, w_field, psi_init, start_field)])
    return pl.pallas_call(
        store,
        out_shape=(out, out),
        in_specs=[pl.BlockSpec(memory_space=pl.ANY)] * 2,
        out_specs=(hbm, hbm),
        scratch_shapes=[dma((2,))],
        name="store",
    )(*[pltpu.with_memory_space_constraint(v, pltpu.VMEM) for v in (density, potential)])


def solution(mesh):
    in_specs = (P("slab", None, None), P("slab", None, None), P("end", "slab", None, None), P())
    out_specs = (P("slab", "end", None), P("slab", "end", None))
    step = functools.partial(body, mesh.shape["end"], mesh.shape["slab"])
    return jax.shard_map(step, mesh=mesh, in_specs=in_specs, out_specs=out_specs, check_vma=False)
```

```python
import functools
import math

import jax
import jax.numpy as jnp
from jax import lax
from jax.experimental import pallas as pl
from jax.experimental.pallas import tpu as pltpu
from jax.sharding import PartitionSpec as P

NS = 4
PAD = 8
EDGE = 4
LANES = 128
mobility = 0.15
screening = 1.0
OWN, FOREIGN = 0, 1
W_MAX, PSI_MAX = 4.0, 3.0
START_MIN, START_MAX = 0.25, 8.0
CODES, OFFSET = 65535.0, 32768
MARGIN = 0.001
MESH = pl.DeviceIdType.MESH


def kernel(ends, slabs, charges_hbm, w_hbm, psi_hbm, start_hbm, density_ref, potential_ref,
           charges_ref, w_v, psi_v, start_v, theirs_v, factor, u, rounded, phi, rho, base, relaxed, sums,
           field_out, field_in, edge_out, edge_in, halo_out, halo_in, rho_out, rho_in,
           gate, seam_gate, charges_sem, field_sem, local_sem, field_send, field_recv, edge_send, edge_recv, halo_send, halo_recv,
           rho_send, rho_recv, sum_send, sum_recv):
    side, slab = lax.axis_index("end"), lax.axis_index("slab")
    other = lax.rem(side + 1, ends)
    left = (side, lax.rem(slab + slabs - 1, slabs))
    right = (side, lax.rem(slab + 1, slabs))
    partner = (other, slab)
    layers, rows = w_hbm.shape[0], w_hbm.shape[1]
    half = rows // ends
    parts = w_hbm.shape[2] // LANES
    devices = ends * slabs
    flat = side * slabs + slab
    delta = 1.0 / NS

    def device(distance):
        target = lax.rem(flat + distance, devices)
        return (target // slabs, lax.rem(target, slabs))

    barrier = pltpu.get_barrier_semaphore()
    charges_copy = pltpu.make_async_copy(charges_hbm, charges_ref, charges_sem)
    charges_copy.start()

    near = []
    width = 1
    while width < slabs:
        near.append((side, slab + width - 2 * width * lax.rem(slab // width, 2)))
        width *= 2
    near.append(partner)
    first_slab, last_slab = slab == 0, slab == slabs - 1
    for neighbour in near + [left]:
        pl.semaphore_signal(barrier, inc=1, device_id=neighbour, device_id_type=MESH)

    @pl.when(jnp.logical_not(last_slab))
    def _():
        pl.semaphore_signal(barrier, inc=1, device_id=right, device_id_type=MESH)

    greeted = len(near) + jnp.where(first_slab, 1, 2)
    targets = (left, right)

    def pieces(which):
        first = which * half
        return (
            (pl.multiple_of(first, 8), PAD, half),
            (pl.multiple_of(lax.rem(first + rows - PAD, rows), 8), 0, PAD),
            (pl.multiple_of(lax.rem(first + half, rows), 8), PAD + half, PAD),
        )

    mine, theirs = pieces(side), pieces(other)
    groups = [(0, layers - 1), (1, layers - 2), (2, layers - 3), tuple(range(3, layers - 3))]
    firsts = [sum(len(group) for group in groups[:k]) for k in range(len(groups))]
    slots = [pl.ds(first, len(group)) for first, group in zip(firsts, groups)]
    slot_of = {x: first + k for first, group in zip(firsts, groups) for k, x in enumerate(group)}
    for k, group in enumerate(groups):
        for x in group:
            for begin, at, count in theirs:
                pltpu.make_async_copy(
                    start_hbm.at[0, x, pl.ds(begin, count)], theirs_v.at[slot_of[x], pl.ds(at, count)], field_sem.at[k],
                ).start()
    for begin, at, count in mine:
        pltpu.make_async_copy(
            w_hbm.at[:, pl.ds(begin, count)], w_v.at[pl.ds(1, layers), pl.ds(at, count)], local_sem.at[0],
        ).start()
        for h in range(parts):
            pltpu.make_async_copy(
                psi_hbm.at[:, pl.ds(begin, count), pl.ds(h * LANES, LANES)],
                psi_v.at[pl.ds(2, layers), h, pl.ds(at, count)], local_sem.at[1],
            ).start()
        pltpu.make_async_copy(
            start_hbm.at[0, :, pl.ds(begin, count)], start_v.at[:, pl.ds(at, count)], local_sem.at[2],
        ).start()

    def taken(ref, semaphore):
        pltpu.make_async_copy(ref, ref, semaphore).wait()

    def loop(low, high, step):
        def body(x, carry):
            step(x)
            return carry

        lax.fori_loop(low, high, body, 0, unroll=True)

    def span(t):
        reach = 0.5 * delta * (W_MAX + PSI_MAX) * t + MARGIN
        shift = 0.5 * math.log(mobility) if t else 0.0
        return math.log(START_MIN) - reach + shift, math.log(START_MAX) + reach + shift

    def write_code(value, low, high):
        scaled = value * (CODES / (high - low)) + (0.5 - low * (CODES / (high - low)))
        return (scaled.astype(jnp.int32) - OFFSET).astype(jnp.int16)

    def read_code(code, low, high):
        step = (high - low) / CODES
        return code.astype(jnp.int32).astype(jnp.float32) * step + (low + OFFSET * step)

    def write_log(value, t):
        return write_code(jnp.log(value), *span(t))

    def read_log(code, t):
        return jnp.exp(read_code(code, *span(t)))

    w_span, psi_span = (-W_MAX - MARGIN, W_MAX + MARGIN), (-PSI_MAX - MARGIN, PSI_MAX + MARGIN)

    def plane(h):
        return slice(h * LANES, (h + 1) * LANES)

    for k, group in enumerate(groups):
        taken(theirs_v.at[slots[k]], field_sem.at[k])
        for x in group:
            for h in range(parts):
                field_out[slot_of[x], h] = write_log(theirs_v[slot_of[x], :, plane(h)], 0)
        if k == 0:
            pl.semaphore_wait(barrier, greeted)

            @pl.when(last_slab)
            def _():
                pl.semaphore_signal(seam_gate, inc=1, device_id=right, device_id_type=MESH)

        pltpu.make_async_remote_copy(
            field_out.at[slots[k]], field_in.at[slots[k]], field_send, field_recv.at[k],
            device_id=partner, device_id_type=MESH,
        ).start()

    charges_copy.wait()
    q = [charges_ref[side * (NS - 2 * t) + t].astype(jnp.float32) for t in range(NS + 1)]
    pair = [0.5 * (q[k] + q[k + 1]) for k in range(NS)]

    def make_factor(x):
        for h in range(parts):
            level = 0.5 * math.log(mobility) - 0.5 * delta * w_v[x + 1, :, plane(h)]
            psi = psi_v[x + 2, h]
            for k in range(NS):
                factor[k, x + 1, h] = jnp.exp(level - (0.5 * delta * pair[k]) * psi)

    def index(chain, t):
        return t if chain == OWN else NS - 1 - t

    def to_bfloat16(value):
        return value.astype(jnp.bfloat16).astype(jnp.float32)

    window = pl.ds(EDGE, half + 2 * (PAD - EDGE))
    inner = pl.ds(PAD - EDGE, half)

    def begin_chain(chain, x):
        for h in range(parts):
            value = start_v[x, :, plane(h)] if chain == OWN else read_log(field_in[slot_of[x], h], 0)
            u[chain, 0, x + 2, h] = factor[index(chain, 0), x + 1, h] * value
            rounded[chain, 0, x, h] = to_bfloat16(value)

    lane = lax.broadcasted_iota(jnp.int32, (1, LANES), 1)
    lowest, highest = lane == 0, lane == LANES - 1

    def around(ref, at, first, count):
        center = [ref[(*at, h, pl.ds(first, count))] for h in range(parts)]
        lower = [pltpu.roll(value, 1, 1) for value in center]
        upper = [pltpu.roll(value, LANES - 1, 1) for value in center]
        sums = []
        for h in range(parts):
            total = ref[(*at, h, pl.ds(first - 1, count))] + ref[(*at, h, pl.ds(first + 1, count))]
            total = total + jnp.where(lowest, lower[h - 1], lower[h])
            sums.append(total + jnp.where(highest, upper[(h + 1) % parts], upper[h]))
        return center, sums

    def advanced(chain, t, x):
        center, sums = around(u, (chain, t, x + 2), EDGE, window.size)
        return [
            factor[index(chain, t), x + 1, h, window] * (
                (u[chain, t, x + 1, h, window] + u[chain, t, x + 3, h, window])
                + (sums[h] + ((1.0 - 6.0 * mobility) / mobility) * center[h])
            )
            for h in range(parts)
        ]

    def advance_halo(chain, t, x):
        for h, value in enumerate(advanced(chain, t, x)):
            u[chain, t + 1, x + 2, h, window] = factor[index(chain, t + 1), x + 1, h, window] * value

    def advance(chain, t, x):
        for h, value in enumerate(advanced(chain, t, x)):
            rounded[chain, t + 1, x, h, window] = to_bfloat16(value)
            if t + 1 < NS:
                u[chain, t + 1, x + 2, h, window] = factor[index(chain, t + 1), x + 1, h, window] * value

    def adv(chain, t, low, high):
        loop(low, high, functools.partial(advance, chain, t))

    def outer(step):
        loop(0, 2, lambda k: step((layers - 1) * k))

    def ring(first, step):
        loop(0, 2, lambda k: step(first + (layers - 1 - 2 * first) * k))

    def beyond(step):
        loop(0, 2, lambda k: step((layers + 1) * k - 1))

    def edge_pair(d, step):
        loop(0, 2, lambda j: step(j + d * (layers - 2)))

    def out_layer(d, j):
        return layers - 1 - j if d else j

    def in_layer(d, j):
        return -1 - j if d else layers + j

    taken(w_v.at[pl.ds(1, layers)], local_sem.at[0])
    taken(psi_v.at[pl.ds(2, layers)], local_sem.at[1])
    taken(start_v, local_sem.at[2])
    for d in (0, 1):
        edge_pair(d, make_factor)
        edge_pair(d, functools.partial(begin_chain, OWN))

        def code_edge(j, d=d):
            x = out_layer(d, j)
            edge_out[d, j] = write_log(u[OWN, 0, x + 2], 1)
            edge_out[d, 3 + j] = write_code(psi_v[x + 2], *psi_span)

        loop(0, 2, code_edge)
        for h in range(parts):
            edge_out[d, 2, h] = write_code(w_v[out_layer(d, 0) + 1, :, plane(h)], *w_span)
    edges = [
        pltpu.make_async_remote_copy(
            edge_out.at[d, pl.ds(first, count)], edge_in.at[d, pl.ds(first, count)],
            edge_send, edge_recv.at[n], device_id=targets[d], device_id_type=MESH,
        )
        for n, (first, count) in enumerate(((0, 4), (4, 1))) for d in (0, 1)
    ]

    @pl.when(jnp.logical_not(first_slab))
    def _():
        edges[0].start()
        edges[2].start()

    edges[1].start()
    edges[3].start()
    stages = len(near)

    def open_gate(stage):
        pl.semaphore_signal(gate.at[stage], inc=1, device_id=near[stage], device_id_type=MESH)

    def pass_gate(stage):
        pl.semaphore_wait(gate.at[stage], 1)
        if stage + 1 < stages:
            open_gate(stage + 1)

    open_gate(0)
    loop(2, layers - 2, make_factor)
    loop(2, layers - 2, functools.partial(begin_chain, OWN))
    pass_gate(0)
    adv(OWN, 0, 1, layers - 1)
    adv(OWN, 1, 2, layers - 2)
    adv(OWN, 2, 3, layers - 3)

    def relaxation(center, total):
        return (total - ion_charge(center) + screening * center) * (1.0 / (6.0 + screening))

    def make_base(x):
        center, sums = around(psi_v, (x + 2,), EDGE, window.size)
        for h in range(parts):
            total = psi_v[x + 1, h, window] + psi_v[x + 3, h, window] + sums[h]
            base[x + 1, h] = relaxation(center[h], total)

    @pl.when(first_slab)
    def _():
        pl.semaphore_wait(seam_gate, 1)
        edges[0].start()
        edges[2].start()

    loop(1, layers - 1, make_base)
    pass_gate(1)

    def neighbour_of(d):
        return (side, lax.rem(slab + slabs + 2 * d - 1, slabs))

    def edge(d, k):
        return d * (layers - 1) + k * (1 - 2 * d)

    def halo(kind, d, first, count):
        return pltpu.make_async_remote_copy(
            halo_out.at[kind, d, pl.ds(first, count)], halo_in.at[kind, d, pl.ds(first, count)],
            halo_send, halo_recv.at[kind, d],
            device_id=neighbour_of(d), device_id_type=MESH,
        )

    def arrive(group):
        taken(field_in.at[slots[group]], field_recv.at[group])
        for x in groups[group]:
            begin_chain(FOREIGN, x)

    for j in (0, 1):
        arrive(j)
        for d in (0, 1):
            halo_out[0, d, j] = write_log(u[FOREIGN, 0, out_layer(d, j) + 2], 1)
            halo(0, d, j, 1).start()

    pass_gate(2)
    taken(edge_in.at[:, pl.ds(0, 4)], edge_recv.at[0])
    for d in (0, 1):
        x = in_layer(d, 0)
        for h in range(parts):
            w_v[x + 1, :, plane(h)] = read_code(edge_in[d, 2, h], *w_span)
        psi_v[x + 2] = read_code(edge_in[d, 3], *psi_span)
        for j in (0, 1):
            u[OWN, 0, in_layer(d, j) + 2] = read_log(edge_in[d, j], 1)
    beyond(make_factor)
    beyond(functools.partial(advance_halo, OWN, 0))
    outer(functools.partial(advance, OWN, 0))

    def half_way(chain, kind):
        for d in (0, 1):
            edge_pair(d, functools.partial(advance, chain, 1))
            for j in (0, 1):
                halo_out[kind, d, j] = write_log(u[chain, 2, out_layer(d, j) + 2], 5)
            halo(kind, d, 0, 2).start()

    half_way(OWN, 1)
    arrive(2)
    ring(1, functools.partial(advance, FOREIGN, 0))
    arrive(3)
    ring(2, functools.partial(advance, FOREIGN, 0))
    sides = (1 - slab % 2, slab % 2)
    first_side = jnp.where(slab % (slabs - 1) == 0, sides[0], sides[1])
    for d in (first_side, 1 - first_side):
        taken(halo_in.at[0, 1 - d], halo_recv.at[0, 1 - d])
        for j in (0, 1):
            u[FOREIGN, 0, edge(d, -1 - j) + 2] = read_log(halo_in[0, 1 - d, j], 1)
        advance_halo(FOREIGN, 0, edge(d, -1))
        for j in (0,):
            advance(FOREIGN, 0, edge(d, j))
        for j in (0, 1):
            advance(FOREIGN, 1, edge(d, j))
            halo_out[2, d, j] = write_log(u[FOREIGN, 2, edge(d, j) + 2], 5)
        halo(2, d, 0, 2).start()

    adv(FOREIGN, 0, 3, layers - 3)
    for stage in range(3, stages - 1):
        pass_gate(stage)
    adv(OWN, 2, 1, 3)
    adv(OWN, 2, layers - 3, layers - 1)
    adv(OWN, 3, 2, layers - 2)
    adv(FOREIGN, 1, 2, layers - 2)
    adv(FOREIGN, 2, 1, layers - 1)

    def second_half(chain, kind):
        for d in (0, 1):
            taken(halo_in.at[kind, d], halo_recv.at[kind, d])
            for j in (0, 1):
                u[chain, 2, in_layer(d, j) + 2] = read_log(halo_in[kind, d, j], 5)
        beyond(functools.partial(advance_halo, chain, 2))
        outer(functools.partial(advance, chain, 2))

    weights = [0.5 if t in (0, NS) else 1.0 for t in range(NS + 1)]
    charged = [weights[t] * q[t] for t in range(NS + 1)]

    def gathered(x, h, terms):
        phi_layer, rho_layer = 0.0, 0.0
        for t in terms:
            product = rounded[OWN, t, x, h, window] * rounded[FOREIGN, NS - t, x, h, window]
            phi_layer = phi_layer + (product if weights[t] == 1.0 else weights[t] * product)
            rho_layer = rho_layer + charged[t] * product
        return phi_layer, rho_layer

    def gather(x):
        for h in range(parts):
            phi[x, h], rho[x + 1, h] = gathered(x, h, range(2, NS + 1))

    def complete(x, early):
        for h, value in enumerate(advanced(FOREIGN, NS - 1, x)):
            phi_layer, rho_layer = gathered(x, h, range(1, 2 if early else NS + 1))
            product = rounded[OWN, 0, x, h, window] * to_bfloat16(value)
            phi_layer = phi_layer + weights[0] * product
            rho_layer = rho_layer + charged[0] * product
            phi[x, h] = phi[x, h] + phi_layer if early else phi_layer
            rho[x + 1, h] = rho[x + 1, h] + rho_layer if early else rho_layer

    def whole(x):
        complete(x, False)

    def finish(x):
        complete(x, True)

    loop(2, layers - 2, whole)

    pass_gate(stages - 1)
    second_half(OWN, 1)
    for d in (0, 1):
        edge_pair(d, functools.partial(advance, OWN, 3))

    def cells_of(x):
        return sum(phi[x, h, inner] for h in range(parts))

    partial = sum(cells_of(x) for x in range(2, layers - 2))

    for d in (0, 1):
        edge_pair(d, gather)

    taken(edge_in.at[:, pl.ds(4, 1)], edge_recv.at[1])
    for d in (0, 1):
        psi_v[in_layer(d, 1) + 2] = read_code(edge_in[d, 4], *psi_span)
    for k in (-1, 0):
        make_base(k)
        make_base(layers - 1 - k)

    bits = [1 << k for k in range(slabs.bit_length() - 1)]
    flips = [bit - 2 * bit * lax.rem(slab // bit, 2) for bit in bits]

    def mirror(mask):
        target = slab
        for bit, flip in zip(bits, flips):
            target = target + flip if mask & bit else target
        return (other if mask >= slabs else side, target)

    masks = sorted(range(1, devices), key=lambda mask: (-(mask % slabs // 4), -mask))
    receivers = [(mask, mirror(mask)) for mask in masks] if ends == 2 and devices <= 32 else None
    for d in sides:
        taken(halo_in.at[2, 1 - d], halo_recv.at[2, 1 - d])
        for j in (0, 1):
            u[FOREIGN, 2, edge(d, -1 - j) + 2] = read_log(halo_in[2, 1 - d, j], 5)
        advance_halo(FOREIGN, 2, edge(d, -1))
        advance(FOREIGN, 2, edge(d, 0))
        finish(edge(d, 0))
        rho_out[d] = rho[edge(d, 0) + 1].astype(jnp.bfloat16)
        pltpu.make_async_remote_copy(
            rho_out.at[d], rho_in.at[d], rho_send, rho_recv, device_id=neighbour_of(d), device_id_type=MESH,
        ).start()
        finish(edge(d, 1))
        partial = partial + cells_of(edge(d, 0)) + cells_of(edge(d, 1))
    sums[0] = jnp.sum(partial, axis=0, keepdims=True)

    def share(step, target):
        pltpu.make_async_remote_copy(
            sums.at[0], sums.at[step], sum_send, sum_recv, device_id=target, device_id_type=MESH,
        ).start()

    if receivers is not None:
        for step, target in receivers:
            share(step, target)
    else:
        lax.fori_loop(1, devices, lambda step, carry: (share(step, device(step)), carry)[1], 0)

    others = sums.at[pl.ds(1, devices - 1)]
    taken(rho_in, rho_recv)
    for d in (0, 1):
        rho[in_layer(d, 0) + 1] = rho_in[d].astype(jnp.float32)
    taken(others, sum_recv)
    cells = float(devices * layers * half * w_hbm.shape[2])
    inverse = cells / jnp.sum(sums[...])
    scaled = inverse * (1.0 / (6.0 + screening))

    def relax_once(x):
        for h in range(parts):
            relaxed[x + 1, h] = base[x + 1, h] + rho[x + 1, h] * scaled

    def first(x):
        for h in range(parts):
            density_ref[x, :, h * LANES:(h + 1) * LANES] = phi[x, h, inner] * inverse
    loop(-1, layers + 1, relax_once)

    def second(x):
        center, sums = around(relaxed, (x + 1,), PAD - EDGE, half)
        for h in range(parts):
            total = relaxed[x, h, inner] + relaxed[x + 2, h, inner] + sums[h]
            value = relaxation(center[h], total) + rho[x + 1, h, inner] * scaled
            potential_ref[x, :, h * LANES:(h + 1) * LANES] = value

    loop(0, layers, second)
    loop(0, layers, first)

    for ref, semaphore in (
        (field_out, field_send), (edge_out, edge_send), (halo_out, halo_send), (rho_out, rho_send), (others, sum_send)
    ):
        taken(ref, semaphore)


def ion_charge(value):
    return (2.0 * screening) * jnp.tanh(0.5 * value)


def store(density_v, potential_v, density_hbm, potential_hbm, sems):
    copies = [
        pltpu.make_async_copy(source, target, sems.at[k])
        for k, (source, target) in enumerate(((density_v, density_hbm), (potential_v, potential_hbm)))
    ]
    for copy in copies:
        copy.start()
    for copy in copies:
        copy.wait()


def body(ends, slabs, w_field, psi_init, start_field, charges):
    layers, rows, depth = w_field.shape
    half = rows // ends
    wide = half + 2 * PAD
    devices = ends * slabs
    stages = slabs.bit_length()
    out = jax.ShapeDtypeStruct((layers, half, depth), jnp.float32)
    dma = pltpu.SemaphoreType.DMA

    parts = depth // LANES
    narrow = half + 2 * (PAD - EDGE)

    def tile(*lead):
        return pltpu.VMEM((*lead, parts, wide, LANES), jnp.float32)

    def slim(*lead):
        return pltpu.VMEM((*lead, parts, narrow, LANES), jnp.float32)

    def whole_rows(*lead):
        return pltpu.VMEM((*lead, wide, depth), jnp.float32)

    edge_rho = pltpu.VMEM((2, parts, narrow, LANES), jnp.bfloat16)

    def code(*lead):
        return pltpu.VMEM((*lead, parts, wide, LANES), jnp.int16)

    hbm = pl.BlockSpec(memory_space=pltpu.HBM)
    vmem = pl.BlockSpec(memory_space=pltpu.VMEM)
    density, potential = pl.pallas_call(
        functools.partial(kernel, ends, slabs),
        out_shape=(out, out),
        in_specs=[hbm, hbm, hbm, hbm],
        out_specs=(vmem, vmem),
        scratch_shapes=[
            pltpu.SMEM((NS + 1,), jnp.int32), whole_rows(layers + 2), tile(layers + 4), whole_rows(layers), whole_rows(layers),
            tile(NS, layers + 2), tile(2, NS, layers + 4), tile(2, NS + 1, layers),
            slim(layers), slim(layers + 2), slim(layers + 2), slim(layers + 2),
            pltpu.VMEM((devices, 1, LANES), jnp.float32),
            code(layers), code(layers), code(2, 5), code(2, 5), code(3, 2, 2), code(3, 2, 2), edge_rho, edge_rho,
            pltpu.SemaphoreType.REGULAR((stages,)), pltpu.SemaphoreType.REGULAR, dma(()), dma((4,)), dma((3,)), dma(()), dma((4,)),
            dma(()), dma((2,)), dma(()), dma((3, 2)), dma(()), dma(()), dma(()), dma(()),
        ],
        compiler_params=pltpu.CompilerParams(
            collective_id=0, has_side_effects=True, vmem_limit_bytes=40 * 1024 * 1024
        ),
        name="scf_step",
    )(*[pltpu.with_memory_space_constraint(v, pltpu.HBM) for v in (charges, w_field, psi_init, start_field)])
    return pl.pallas_call(
        store,
        out_shape=(out, out),
        in_specs=[pl.BlockSpec(memory_space=pl.ANY)] * 2,
        out_specs=(hbm, hbm),
        scratch_shapes=[dma((2,))],
        name="store",
    )(*[pltpu.with_memory_space_constraint(v, pltpu.VMEM) for v in (density, potential)])


def solution(mesh):
    in_specs = (P("slab", None, None), P("slab", None, None), P("end", "slab", None, None), P())
    out_specs = (P("slab", "end", None), P("slab", "end", None))
    step = functools.partial(body, mesh.shape["end"], mesh.shape["slab"])
    return jax.shard_map(step, mesh=mesh, in_specs=in_specs, out_specs=out_specs, check_vma=False)
```

```python
import functools
import math

import jax
import jax.numpy as jnp
from jax import lax
from jax.experimental import pallas as pl
from jax.experimental.pallas import tpu as pltpu
from jax.sharding import PartitionSpec as P

NS = 4
PAD = 8
EDGE = 4
LANES = 128
CHUNK = 4
mobility = 0.15
screening = 1.0
OWN, FOREIGN = 0, 1
W_MAX, PSI_MAX = 4.0, 3.0
START_MIN, START_MAX = 0.25, 8.0
CODES, OFFSET = 65535.0, 32768
MARGIN = 0.001
MESH = pl.DeviceIdType.MESH


def kernel(ends, slabs, charges_hbm, w_hbm, psi_hbm, start_hbm, phi, rho, base, scale_ref,
           charges_ref, w_v, psi_v, start_v, theirs_v, factor, u, rounded, sums,
           field_out, field_in, edge_out, edge_in, halo_out, halo_in, rho_out, rho_in,
           gate, seam_gate, charges_sem, field_sem, local_sem, field_send, field_recv, edge_send, edge_recv, halo_send, halo_recv,
           rho_send, rho_recv, sum_send, sum_recv):
    side, slab = lax.axis_index("end"), lax.axis_index("slab")
    other = lax.rem(side + 1, ends)
    left = (side, lax.rem(slab + slabs - 1, slabs))
    right = (side, lax.rem(slab + 1, slabs))
    partner = (other, slab)
    layers, rows = w_hbm.shape[0], w_hbm.shape[1]
    half = rows // ends
    parts = w_hbm.shape[2] // LANES
    devices = ends * slabs
    flat = side * slabs + slab
    delta = 1.0 / NS

    def device(distance):
        target = lax.rem(flat + distance, devices)
        return (target // slabs, lax.rem(target, slabs))

    barrier = pltpu.get_barrier_semaphore()
    charges_copy = pltpu.make_async_copy(charges_hbm, charges_ref, charges_sem)
    charges_copy.start()

    near = []
    width = 1
    while width < slabs:
        near.append((side, slab + width - 2 * width * lax.rem(slab // width, 2)))
        width *= 2
    near.append(partner)
    first_slab, last_slab = slab == 0, slab == slabs - 1
    for neighbour in near + [left]:
        pl.semaphore_signal(barrier, inc=1, device_id=neighbour, device_id_type=MESH)

    @pl.when(jnp.logical_not(last_slab))
    def _():
        pl.semaphore_signal(barrier, inc=1, device_id=right, device_id_type=MESH)

    greeted = len(near) + jnp.where(first_slab, 1, 2)
    targets = (left, right)

    def pieces(which):
        first = which * half
        return (
            (pl.multiple_of(first, 8), PAD, half),
            (pl.multiple_of(lax.rem(first + rows - PAD, rows), 8), 0, PAD),
            (pl.multiple_of(lax.rem(first + half, rows), 8), PAD + half, PAD),
        )

    mine, theirs = pieces(side), pieces(other)
    groups = [(0, layers - 1), (1, layers - 2), (2, layers - 3), tuple(range(3, layers - 3))]
    firsts = [sum(len(group) for group in groups[:k]) for k in range(len(groups))]
    slots = [pl.ds(first, len(group)) for first, group in zip(firsts, groups)]
    slot_of = {x: first + k for first, group in zip(firsts, groups) for k, x in enumerate(group)}
    for k, group in enumerate(groups):
        for x in group:
            for begin, at, count in theirs:
                pltpu.make_async_copy(
                    start_hbm.at[0, x, pl.ds(begin, count)], theirs_v.at[slot_of[x], pl.ds(at, count)], field_sem.at[k],
                ).start()
    for begin, at, count in mine:
        pltpu.make_async_copy(
            w_hbm.at[:, pl.ds(begin, count)], w_v.at[pl.ds(1, layers), pl.ds(at, count)], local_sem.at[0],
        ).start()
        for h in range(parts):
            pltpu.make_async_copy(
                psi_hbm.at[:, pl.ds(begin, count), pl.ds(h * LANES, LANES)],
                psi_v.at[pl.ds(2, layers), h, pl.ds(at, count)], local_sem.at[1],
            ).start()
        pltpu.make_async_copy(
            start_hbm.at[0, :, pl.ds(begin, count)], start_v.at[:, pl.ds(at, count)], local_sem.at[2],
        ).start()

    def taken(ref, semaphore):
        pltpu.make_async_copy(ref, ref, semaphore).wait()

    def loop(low, high, step):
        def body(x, carry):
            step(x)
            return carry

        lax.fori_loop(low, high, body, 0, unroll=True)

    def span(t):
        reach = 0.5 * delta * (W_MAX + PSI_MAX) * t + MARGIN
        shift = 0.5 * math.log(mobility) if t else 0.0
        return math.log(START_MIN) - reach + shift, math.log(START_MAX) + reach + shift

    def write_code(value, low, high):
        scaled = value * (CODES / (high - low)) + (0.5 - low * (CODES / (high - low)))
        return (scaled.astype(jnp.int32) - OFFSET).astype(jnp.int16)

    def read_code(code, low, high):
        step = (high - low) / CODES
        return code.astype(jnp.int32).astype(jnp.float32) * step + (low + OFFSET * step)

    def write_log(value, t):
        return write_code(jnp.log(value), *span(t))

    def read_log(code, t):
        return jnp.exp(read_code(code, *span(t)))

    w_span, psi_span = (-W_MAX - MARGIN, W_MAX + MARGIN), (-PSI_MAX - MARGIN, PSI_MAX + MARGIN)

    def plane(h):
        return slice(h * LANES, (h + 1) * LANES)

    def field(k):
        return pltpu.make_async_remote_copy(
            field_out.at[slots[k]], field_in.at[slots[k]], field_send, field_recv.at[k],
            device_id=partner, device_id_type=MESH,
        )

    holds_back = slab % 2 == 1
    for k, group in enumerate(groups):
        taken(theirs_v.at[slots[k]], field_sem.at[k])
        for x in group:
            for h in range(parts):
                field_out[slot_of[x], h] = write_log(theirs_v[slot_of[x], :, plane(h)], 0)
        if k == 0:
            pl.semaphore_wait(barrier, greeted)

            @pl.when(last_slab)
            def _():
                pl.semaphore_signal(seam_gate, inc=1, device_id=right, device_id_type=MESH)

        if k < 2:
            field(k).start()
        else:
            @pl.when(jnp.logical_not(holds_back))
            def _(k=k):
                field(k).start()

    charges_copy.wait()
    q = [charges_ref[side * (NS - 2 * t) + t].astype(jnp.float32) for t in range(NS + 1)]
    pair = [0.5 * (q[k] + q[k + 1]) for k in range(NS)]

    def make_factor(x):
        for h in range(parts):
            level = 0.5 * math.log(mobility) - 0.5 * delta * w_v[x + 1, :, plane(h)]
            psi = psi_v[x + 2, h]
            for k in range(NS):
                factor[k, x + 1, h] = jnp.exp(level - (0.5 * delta * pair[k]) * psi)

    def index(chain, t):
        return t if chain == OWN else NS - 1 - t

    def to_bfloat16(value):
        return value.astype(jnp.bfloat16).astype(jnp.float32)

    window = pl.ds(EDGE, half + 2 * (PAD - EDGE))
    inner = pl.ds(PAD - EDGE, half)

    def begin_chain(chain, x):
        for h in range(parts):
            value = start_v[x, :, plane(h)] if chain == OWN else read_log(field_in[slot_of[x], h], 0)
            u[chain, 0, x + 2, h] = factor[index(chain, 0), x + 1, h] * value
            rounded[chain, 0, x, h] = to_bfloat16(value)

    def advanced(chain, t, x):
        center, sums = around(u, (chain, t, x + 2), EDGE, window.size)
        return [
            factor[index(chain, t), x + 1, h, window] * (
                (u[chain, t, x + 1, h, window] + u[chain, t, x + 3, h, window])
                + (sums[h] + ((1.0 - 6.0 * mobility) / mobility) * center[h])
            )
            for h in range(parts)
        ]

    def advance_halo(chain, t, x):
        for h, value in enumerate(advanced(chain, t, x)):
            u[chain, t + 1, x + 2, h, window] = factor[index(chain, t + 1), x + 1, h, window] * value

    def advance(chain, t, x):
        for h, value in enumerate(advanced(chain, t, x)):
            rounded[chain, t + 1, x, h, window] = to_bfloat16(value)
            if t + 1 < NS:
                u[chain, t + 1, x + 2, h, window] = factor[index(chain, t + 1), x + 1, h, window] * value

    def adv(chain, t, low, high):
        loop(low, high, functools.partial(advance, chain, t))

    def outer(step):
        loop(0, 2, lambda k: step((layers - 1) * k))

    def ring(first, step):
        loop(0, 2, lambda k: step(first + (layers - 1 - 2 * first) * k))

    def beyond(step):
        loop(0, 2, lambda k: step((layers + 1) * k - 1))

    def edge_pair(d, step):
        loop(0, 2, lambda j: step(j + d * (layers - 2)))

    def out_layer(d, j):
        return layers - 1 - j if d else j

    def in_layer(d, j):
        return -1 - j if d else layers + j

    taken(w_v.at[pl.ds(1, layers)], local_sem.at[0])
    taken(psi_v.at[pl.ds(2, layers)], local_sem.at[1])
    taken(start_v, local_sem.at[2])
    for d in (0, 1):
        edge_pair(d, make_factor)
        edge_pair(d, functools.partial(begin_chain, OWN))

        def code_edge(j, d=d):
            x = out_layer(d, j)
            edge_out[d, j] = write_log(u[OWN, 0, x + 2], 1)
            edge_out[d, 3 + j] = write_code(psi_v[x + 2], *psi_span)

        loop(0, 2, code_edge)
        for h in range(parts):
            edge_out[d, 2, h] = write_code(w_v[out_layer(d, 0) + 1, :, plane(h)], *w_span)
    edges = [
        pltpu.make_async_remote_copy(
            edge_out.at[d, pl.ds(first, count)], edge_in.at[d, pl.ds(first, count)],
            edge_send, edge_recv.at[n], device_id=targets[d], device_id_type=MESH,
        )
        for n, (first, count) in enumerate(((0, 4), (4, 1))) for d in (0, 1)
    ]

    @pl.when(jnp.logical_not(first_slab))
    def _():
        edges[0].start()

    edges[1].start()
    stages = len(near)

    def open_gate(stage):
        pl.semaphore_signal(gate.at[stage], inc=1, device_id=near[stage], device_id_type=MESH)

    def pass_gate(stage):
        pl.semaphore_wait(gate.at[stage], 1)
        if stage + 1 < stages:
            open_gate(stage + 1)

    open_gate(0)
    loop(2, layers - 2, make_factor)
    loop(2, layers - 2, functools.partial(begin_chain, OWN))
    pass_gate(0)
    adv(OWN, 0, 1, layers - 1)
    adv(OWN, 1, 2, layers - 2)
    adv(OWN, 2, 3, layers - 3)

    @pl.when(holds_back)
    def _():
        field(2).start()
        field(3).start()


    def make_base(x):
        center, sums = around(psi_v, (x + 2,), EDGE, window.size)
        for h in range(parts):
            total = psi_v[x + 1, h, window] + psi_v[x + 3, h, window] + sums[h]
            base[x + 1, h] = relaxation(center[h], total)

    @pl.when(first_slab)
    def _():
        pl.semaphore_wait(seam_gate, 1)
        edges[0].start()

    loop(1, layers - 1, make_base)
    pass_gate(1)

    def neighbour_of(d):
        return (side, lax.rem(slab + slabs + 2 * d - 1, slabs))

    def edge(d, k):
        return d * (layers - 1) + k * (1 - 2 * d)

    def halo(kind, d, first, count):
        return pltpu.make_async_remote_copy(
            halo_out.at[kind, d, pl.ds(first, count)], halo_in.at[kind, d, pl.ds(first, count)],
            halo_send, halo_recv.at[kind, d],
            device_id=neighbour_of(d), device_id_type=MESH,
        )

    def arrive(group):
        taken(field_in.at[slots[group]], field_recv.at[group])
        for x in groups[group]:
            begin_chain(FOREIGN, x)

    for j in (0, 1):
        arrive(j)
        for d in (0, 1):
            halo_out[0, d, j] = write_log(u[FOREIGN, 0, out_layer(d, j) + 2], 1)
            halo(0, d, j, 1).start()
    edges[2].start()
    edges[3].start()

    pass_gate(2)
    taken(edge_in.at[:, pl.ds(0, 4)], edge_recv.at[0])
    for d in (0, 1):
        x = in_layer(d, 0)
        for h in range(parts):
            w_v[x + 1, :, plane(h)] = read_code(edge_in[d, 2, h], *w_span)
        psi_v[x + 2] = read_code(edge_in[d, 3], *psi_span)
        for j in (0, 1):
            u[OWN, 0, in_layer(d, j) + 2] = read_log(edge_in[d, j], 1)
    beyond(make_factor)
    beyond(functools.partial(advance_halo, OWN, 0))
    outer(functools.partial(advance, OWN, 0))

    def half_way(chain, kind):
        for d in (0, 1):
            edge_pair(d, functools.partial(advance, chain, 1))
            for j in (0, 1):
                halo_out[kind, d, j] = write_log(u[chain, 2, out_layer(d, j) + 2], 5)
            halo(kind, d, 0, 2).start()

    half_way(OWN, 1)
    arrive(2)
    ring(1, functools.partial(advance, FOREIGN, 0))
    arrive(3)
    ring(2, functools.partial(advance, FOREIGN, 0))
    sides = (1 - slab % 2, slab % 2)
    first_side = jnp.where(slab % (slabs - 1) == 0, sides[0], sides[1])
    for d in (first_side, 1 - first_side):
        taken(halo_in.at[0, 1 - d], halo_recv.at[0, 1 - d])
        for j in (0, 1):
            u[FOREIGN, 0, edge(d, -1 - j) + 2] = read_log(halo_in[0, 1 - d, j], 1)
        advance_halo(FOREIGN, 0, edge(d, -1))
        for j in (0,):
            advance(FOREIGN, 0, edge(d, j))
        for j in (0, 1):
            advance(FOREIGN, 1, edge(d, j))
            halo_out[2, d, j] = write_log(u[FOREIGN, 2, edge(d, j) + 2], 5)
        halo(2, d, 0, 2).start()

    adv(FOREIGN, 0, 3, layers - 3)
    for stage in range(3, stages - 1):
        pass_gate(stage)
    adv(OWN, 2, 1, 3)
    adv(OWN, 2, layers - 3, layers - 1)
    adv(OWN, 3, 2, layers - 2)
    adv(FOREIGN, 1, 2, layers - 2)
    adv(FOREIGN, 2, 1, layers - 1)

    def second_half(chain, kind):
        for d in (0, 1):
            taken(halo_in.at[kind, d], halo_recv.at[kind, d])
            for j in (0, 1):
                u[chain, 2, in_layer(d, j) + 2] = read_log(halo_in[kind, d, j], 5)
        beyond(functools.partial(advance_halo, chain, 2))
        outer(functools.partial(advance, chain, 2))

    weights = [0.5 if t in (0, NS) else 1.0 for t in range(NS + 1)]
    charged = [weights[t] * q[t] for t in range(NS + 1)]

    def gathered(x, h, terms):
        phi_layer, rho_layer = 0.0, 0.0
        for t in terms:
            product = rounded[OWN, t, x, h, window] * rounded[FOREIGN, NS - t, x, h, window]
            phi_layer = phi_layer + (product if weights[t] == 1.0 else weights[t] * product)
            rho_layer = rho_layer + charged[t] * product
        return phi_layer, rho_layer

    def gather(x):
        for h in range(parts):
            phi[x, h], rho[x + 1, h] = gathered(x, h, range(2, NS + 1))

    def complete(x, early):
        for h, value in enumerate(advanced(FOREIGN, NS - 1, x)):
            phi_layer, rho_layer = gathered(x, h, range(1, 2 if early else NS + 1))
            product = rounded[OWN, 0, x, h, window] * to_bfloat16(value)
            phi_layer = phi_layer + weights[0] * product
            rho_layer = rho_layer + charged[0] * product
            phi[x, h] = phi[x, h] + phi_layer if early else phi_layer
            rho[x + 1, h] = rho[x + 1, h] + rho_layer if early else rho_layer

    def whole(x):
        complete(x, False)

    def finish(x):
        complete(x, True)

    loop(2, layers - 2, whole)

    pass_gate(stages - 1)
    second_half(OWN, 1)
    for d in (0, 1):
        edge_pair(d, functools.partial(advance, OWN, 3))

    def cells_of(x):
        return sum(phi[x, h, inner] for h in range(parts))

    partial = sum(cells_of(x) for x in range(2, layers - 2))

    for d in (0, 1):
        edge_pair(d, gather)

    taken(edge_in.at[:, pl.ds(4, 1)], edge_recv.at[1])
    for d in (0, 1):
        psi_v[in_layer(d, 1) + 2] = read_code(edge_in[d, 4], *psi_span)
    for k in (-1, 0):
        make_base(k)
        make_base(layers - 1 - k)

    bits = [1 << k for k in range(slabs.bit_length() - 1)]
    flips = [bit - 2 * bit * lax.rem(slab // bit, 2) for bit in bits]

    def mirror(mask):
        target = slab
        for bit, flip in zip(bits, flips):
            target = target + flip if mask & bit else target
        return (other if mask >= slabs else side, target)

    masks = sorted(range(1, devices), key=lambda mask: (-(mask % slabs // 4), -mask))
    receivers = [(mask, mirror(mask)) for mask in masks] if ends == 2 and devices <= 32 else None
    for d in sides:
        taken(halo_in.at[2, 1 - d], halo_recv.at[2, 1 - d])
        for j in (0, 1):
            u[FOREIGN, 2, edge(d, -1 - j) + 2] = read_log(halo_in[2, 1 - d, j], 5)
        advance_halo(FOREIGN, 2, edge(d, -1))
        advance(FOREIGN, 2, edge(d, 0))
        finish(edge(d, 0))
        rho_out[d] = rho[edge(d, 0) + 1].astype(jnp.bfloat16)
        pltpu.make_async_remote_copy(
            rho_out.at[d], rho_in.at[d], rho_send, rho_recv, device_id=neighbour_of(d), device_id_type=MESH,
        ).start()
        finish(edge(d, 1))
        partial = partial + cells_of(edge(d, 0)) + cells_of(edge(d, 1))
    sums[0] = jnp.sum(partial, axis=0, keepdims=True)

    def share(step, target):
        pltpu.make_async_remote_copy(
            sums.at[0], sums.at[step], sum_send, sum_recv, device_id=target, device_id_type=MESH,
        ).start()

    if receivers is not None:
        for step, target in receivers:
            share(step, target)
    else:
        lax.fori_loop(1, devices, lambda step, carry: (share(step, device(step)), carry)[1], 0)

    others = sums.at[pl.ds(1, devices - 1)]
    taken(rho_in, rho_recv)
    for d in (0, 1):
        rho[in_layer(d, 0) + 1] = rho_in[d].astype(jnp.float32)
    taken(others, sum_recv)
    cells = float(devices * layers * half * w_hbm.shape[2])
    inverse = cells / jnp.sum(sums[...])
    scale_ref[...] = jnp.broadcast_to(inverse, scale_ref.shape)

    for ref, semaphore in (
        (field_out, field_send), (edge_out, edge_send), (halo_out, halo_send), (rho_out, rho_send), (others, sum_send)
    ):
        taken(ref, semaphore)


def ion_charge(value):
    return (2.0 * screening) * jnp.tanh(0.5 * value)


def relaxation(center, total):
    return (total - ion_charge(center) + screening * center) * (1.0 / (6.0 + screening))


def around(ref, at, first, count):
    parts = ref.shape[-3]
    lane = lax.broadcasted_iota(jnp.int32, (1, LANES), 1)
    lowest, highest = lane == 0, lane == LANES - 1
    center = [ref[(*at, h, pl.ds(first, count))] for h in range(parts)]
    lower = [pltpu.roll(value, 1, 1) for value in center]
    upper = [pltpu.roll(value, LANES - 1, 1) for value in center]
    sums = []
    for h in range(parts):
        total = ref[(*at, h, pl.ds(first - 1, count))] + ref[(*at, h, pl.ds(first + 1, count))]
        total = total + jnp.where(lowest, lower[h - 1], lower[h])
        sums.append(total + jnp.where(highest, upper[(h + 1) % parts], upper[h]))
    return center, sums


def finishing(phi, rho, base, scale_ref, density_hbm, potential_hbm, density, potential, relaxed, density_sem, potential_sem):
    layers, half = density_hbm.shape[0], density_hbm.shape[1]
    parts = phi.shape[1]
    inner = pl.ds(PAD - EDGE, half)
    inverse = scale_ref[...]
    scaled = inverse * (1.0 / (6.0 + screening))

    def plane(h):
        return slice(h * LANES, (h + 1) * LANES)

    for x in range(layers):
        for h in range(parts):
            density[x, :, plane(h)] = phi[x, h, inner] * inverse
    pltpu.make_async_copy(density, density_hbm, density_sem).start()
    for x in range(layers + 2):
        for h in range(parts):
            relaxed[x, h] = base[x, h] + rho[x, h] * scaled
    for x in range(layers):
        center, sums = around(relaxed, (x + 1,), PAD - EDGE, half)
        for h in range(parts):
            total = relaxed[x, h, inner] + relaxed[x + 2, h, inner] + sums[h]
            potential[x, :, plane(h)] = relaxation(center[h], total) + rho[x + 1, h, inner] * scaled
        if x % CHUNK == CHUNK - 1:
            done = pl.ds(x + 1 - CHUNK, CHUNK)
            pltpu.make_async_copy(potential.at[done], potential_hbm.at[done], potential_sem).start()
    pltpu.make_async_copy(density, density_hbm, density_sem).wait()
    pltpu.make_async_copy(potential, potential_hbm, potential_sem).wait()


def body(ends, slabs, w_field, psi_init, start_field, charges):
    layers, rows, depth = w_field.shape
    half = rows // ends
    wide = half + 2 * PAD
    devices = ends * slabs
    stages = slabs.bit_length()
    out = jax.ShapeDtypeStruct((layers, half, depth), jnp.float32)
    dma = pltpu.SemaphoreType.DMA

    parts = depth // LANES
    narrow = half + 2 * (PAD - EDGE)

    def tile(*lead):
        return pltpu.VMEM((*lead, parts, wide, LANES), jnp.float32)

    def slim(*lead):
        return pltpu.VMEM((*lead, parts, narrow, LANES), jnp.float32)

    def whole_rows(*lead):
        return pltpu.VMEM((*lead, wide, depth), jnp.float32)

    edge_rho = pltpu.VMEM((2, parts, narrow, LANES), jnp.bfloat16)

    def code(*lead):
        return pltpu.VMEM((*lead, parts, wide, LANES), jnp.int16)

    hbm = pl.BlockSpec(memory_space=pltpu.HBM)
    vmem = pl.BlockSpec(memory_space=pltpu.VMEM)
    def planes(count):
        return jax.ShapeDtypeStruct((count, parts, narrow, LANES), jnp.float32)

    fields = pl.pallas_call(
        functools.partial(kernel, ends, slabs),
        out_shape=(planes(layers), planes(layers + 2), planes(layers + 2), jax.ShapeDtypeStruct((1, LANES), jnp.float32)),
        in_specs=[hbm, hbm, hbm, hbm],
        out_specs=(vmem, vmem, vmem, vmem),
        scratch_shapes=[
            pltpu.SMEM((NS + 1,), jnp.int32), whole_rows(layers + 2), tile(layers + 4), whole_rows(layers), whole_rows(layers),
            tile(NS, layers + 2), tile(2, NS, layers + 4), tile(2, NS + 1, layers),
            pltpu.VMEM((devices, 1, LANES), jnp.float32),
            code(layers), code(layers), code(2, 5), code(2, 5), code(3, 2, 2), code(3, 2, 2), edge_rho, edge_rho,
            pltpu.SemaphoreType.REGULAR((stages,)), pltpu.SemaphoreType.REGULAR, dma(()), dma((4,)), dma((3,)), dma(()), dma((4,)),
            dma(()), dma((2,)), dma(()), dma((3, 2)), dma(()), dma(()), dma(()), dma(()),
        ],
        compiler_params=pltpu.CompilerParams(
            collective_id=0, has_side_effects=True, vmem_limit_bytes=40 * 1024 * 1024
        ),
        name="scf_step",
    )(*[pltpu.with_memory_space_constraint(v, pltpu.HBM) for v in (charges, w_field, psi_init, start_field)])
    result = pltpu.VMEM((layers, half, depth), jnp.float32)
    return pl.pallas_call(
        finishing,
        out_shape=(out, out),
        in_specs=[vmem] * 4,
        out_specs=(hbm, hbm),
        scratch_shapes=[result, result, slim(layers + 2), dma(()), dma(())],
        name="finishing",
    )(*[pltpu.with_memory_space_constraint(v, pltpu.VMEM) for v in fields])


def solution(mesh):
    in_specs = (P("slab", None, None), P("slab", None, None), P("end", "slab", None, None), P())
    out_specs = (P("slab", "end", None), P("slab", "end", None))
    step = functools.partial(body, mesh.shape["end"], mesh.shape["slab"])
    return jax.shard_map(step, mesh=mesh, in_specs=in_specs, out_specs=out_specs, check_vma=False)
```

```python
import functools
import math

import jax
import jax.numpy as jnp
from jax import lax
from jax.experimental import pallas as pl
from jax.experimental.pallas import tpu as pltpu
from jax.sharding import PartitionSpec as P

NS = 4
PAD = 8
EDGE = 4
LANES = 128
CHUNK = 4
mobility = 0.15
screening = 1.0
OWN, FOREIGN = 0, 1
W_MAX, PSI_MAX = 4.0, 3.0
START_MIN, START_MAX = 0.25, 8.0
CODES, OFFSET = 65535.0, 32768
MARGIN = 0.001
MESH = pl.DeviceIdType.MESH


def kernel(ends, slabs, charges_hbm, w_hbm, psi_hbm, start_hbm, phi, rho, base, scale_ref,
           charges_ref, w_v, psi_v, start_v, theirs_v, factor, u, rounded, sums,
           field_out, field_in, edge_out, edge_in, halo_out, halo_in, rho_out, rho_in,
           gate, seam_gate, charges_sem, field_sem, local_sem, field_send, field_recv, edge_send, edge_recv, halo_send, halo_recv,
           rho_send, rho_recv, sum_send, sum_recv):
    side, slab = lax.axis_index("end"), lax.axis_index("slab")
    other = lax.rem(side + 1, ends)
    left = (side, lax.rem(slab + slabs - 1, slabs))
    right = (side, lax.rem(slab + 1, slabs))
    partner = (other, slab)
    layers, rows = w_hbm.shape[0], w_hbm.shape[1]
    half = rows // ends
    parts = w_hbm.shape[2] // LANES
    devices = ends * slabs
    flat = side * slabs + slab
    delta = 1.0 / NS

    def device(distance):
        target = lax.rem(flat + distance, devices)
        return (target // slabs, lax.rem(target, slabs))

    barrier = pltpu.get_barrier_semaphore()
    charges_copy = pltpu.make_async_copy(charges_hbm, charges_ref, charges_sem)
    charges_copy.start()

    near = []
    width = 1
    while width < slabs:
        near.append((side, slab + width - 2 * width * lax.rem(slab // width, 2)))
        width *= 2
    near.append(partner)
    first_slab, last_slab = slab == 0, slab == slabs - 1
    for neighbour in near + [left]:
        pl.semaphore_signal(barrier, inc=1, device_id=neighbour, device_id_type=MESH)

    @pl.when(jnp.logical_not(last_slab))
    def _():
        pl.semaphore_signal(barrier, inc=1, device_id=right, device_id_type=MESH)

    greeted = len(near) + jnp.where(first_slab, 1, 2)
    targets = (left, right)

    def pieces(which):
        first = which * half
        return (
            (pl.multiple_of(first, 8), PAD, half),
            (pl.multiple_of(lax.rem(first + rows - PAD, rows), 8), 0, PAD),
            (pl.multiple_of(lax.rem(first + half, rows), 8), PAD + half, PAD),
        )

    mine, theirs = pieces(side), pieces(other)
    groups = [(0, layers - 1), (1, layers - 2), (2, layers - 3), tuple(range(3, layers - 3))]
    firsts = [sum(len(group) for group in groups[:k]) for k in range(len(groups))]
    slots = [pl.ds(first, len(group)) for first, group in zip(firsts, groups)]
    slot_of = {x: first + k for first, group in zip(firsts, groups) for k, x in enumerate(group)}
    for k, group in enumerate(groups):
        for x in group:
            for begin, at, count in theirs:
                pltpu.make_async_copy(
                    start_hbm.at[0, x, pl.ds(begin, count)], theirs_v.at[slot_of[x], pl.ds(at, count)], field_sem.at[k],
                ).start()
    for begin, at, count in mine:
        pltpu.make_async_copy(
            w_hbm.at[:, pl.ds(begin, count)], w_v.at[pl.ds(1, layers), pl.ds(at, count)], local_sem.at[0],
        ).start()
        for h in range(parts):
            pltpu.make_async_copy(
                psi_hbm.at[:, pl.ds(begin, count), pl.ds(h * LANES, LANES)],
                psi_v.at[pl.ds(2, layers), h, pl.ds(at, count)], local_sem.at[1],
            ).start()
        pltpu.make_async_copy(
            start_hbm.at[0, :, pl.ds(begin, count)], start_v.at[:, pl.ds(at, count)], local_sem.at[2],
        ).start()

    def taken(ref, semaphore):
        pltpu.make_async_copy(ref, ref, semaphore).wait()

    def loop(low, high, step):
        def body(x, carry):
            step(x)
            return carry

        lax.fori_loop(low, high, body, 0, unroll=True)

    def span(t):
        reach = 0.5 * delta * (W_MAX + PSI_MAX) * t + MARGIN
        shift = 0.5 * math.log(mobility) if t else 0.0
        return math.log(START_MIN) - reach + shift, math.log(START_MAX) + reach + shift

    def write_code(value, low, high):
        scaled = value * (CODES / (high - low)) + (0.5 - low * (CODES / (high - low)))
        return (scaled.astype(jnp.int32) - OFFSET).astype(jnp.int16)

    def read_code(code, low, high):
        step = (high - low) / CODES
        return code.astype(jnp.int32).astype(jnp.float32) * step + (low + OFFSET * step)

    def write_log(value, t):
        return write_code(jnp.log(value), *span(t))

    def read_log(code, t):
        return jnp.exp(read_code(code, *span(t)))

    w_span, psi_span = (-W_MAX - MARGIN, W_MAX + MARGIN), (-PSI_MAX - MARGIN, PSI_MAX + MARGIN)

    def plane(h):
        return slice(h * LANES, (h + 1) * LANES)

    def field(k):
        return pltpu.make_async_remote_copy(
            field_out.at[slots[k]], field_in.at[slots[k]], field_send, field_recv.at[k],
            device_id=partner, device_id_type=MESH,
        )

    def code_group(k):
        taken(theirs_v.at[slots[k]], field_sem.at[k])
        for x in groups[k]:
            for h in range(parts):
                field_out[slot_of[x], h] = write_log(theirs_v[slot_of[x], :, plane(h)], 0)

    code_group(0)
    pl.semaphore_wait(barrier, greeted)

    @pl.when(last_slab)
    def _():
        pl.semaphore_signal(seam_gate, inc=1, device_id=right, device_id_type=MESH)

    field(0).start()

    charges_copy.wait()
    q = [charges_ref[side * (NS - 2 * t) + t].astype(jnp.float32) for t in range(NS + 1)]
    pair = [0.5 * (q[k] + q[k + 1]) for k in range(NS)]

    def make_factor(x):
        for h in range(parts):
            level = 0.5 * math.log(mobility) - 0.5 * delta * w_v[x + 1, :, plane(h)]
            psi = psi_v[x + 2, h]
            for k in range(NS):
                factor[k, x + 1, h] = jnp.exp(level - (0.5 * delta * pair[k]) * psi)

    def index(chain, t):
        return t if chain == OWN else NS - 1 - t

    def to_bfloat16(value):
        return value.astype(jnp.bfloat16).astype(jnp.float32)

    window = pl.ds(EDGE, half + 2 * (PAD - EDGE))
    inner = pl.ds(PAD - EDGE, half)

    def begin_chain(chain, x):
        for h in range(parts):
            value = start_v[x, :, plane(h)] if chain == OWN else read_log(field_in[slot_of[x], h], 0)
            u[chain, 0, x + 2, h] = factor[index(chain, 0), x + 1, h] * value
            rounded[chain, 0, x, h] = to_bfloat16(value)

    def advanced(chain, t, x):
        center, sums = around(u, (chain, t, x + 2), EDGE, window.size)
        return [
            factor[index(chain, t), x + 1, h, window] * (
                (u[chain, t, x + 1, h, window] + u[chain, t, x + 3, h, window])
                + (sums[h] + ((1.0 - 6.0 * mobility) / mobility) * center[h])
            )
            for h in range(parts)
        ]

    def advance_halo(chain, t, x):
        for h, value in enumerate(advanced(chain, t, x)):
            u[chain, t + 1, x + 2, h, window] = factor[index(chain, t + 1), x + 1, h, window] * value

    def advance(chain, t, x):
        for h, value in enumerate(advanced(chain, t, x)):
            rounded[chain, t + 1, x, h, window] = to_bfloat16(value)
            if t + 1 < NS:
                u[chain, t + 1, x + 2, h, window] = factor[index(chain, t + 1), x + 1, h, window] * value

    def adv(chain, t, low, high):
        loop(low, high, functools.partial(advance, chain, t))

    def outer(step):
        loop(0, 2, lambda k: step((layers - 1) * k))

    def ring(first, step):
        loop(0, 2, lambda k: step(first + (layers - 1 - 2 * first) * k))

    def beyond(step):
        loop(0, 2, lambda k: step((layers + 1) * k - 1))

    def edge_pair(d, step):
        loop(0, 2, lambda j: step(j + d * (layers - 2)))

    def out_layer(d, j):
        return layers - 1 - j if d else j

    def in_layer(d, j):
        return -1 - j if d else layers + j

    taken(w_v.at[pl.ds(1, layers)], local_sem.at[0])
    taken(psi_v.at[pl.ds(2, layers)], local_sem.at[1])
    taken(start_v, local_sem.at[2])
    def neighbour_of(d):
        return (side, lax.rem(slab + slabs + 2 * d - 1, slabs))

    def edge(d, k):
        return d * (layers - 1) + k * (1 - 2 * d)

    def edge_copy(n, d):
        first, count = ((0, 4), (4, 1))[n]
        return pltpu.make_async_remote_copy(
            edge_out.at[d, pl.ds(first, count)], edge_in.at[d, pl.ds(first, count)],
            edge_send, edge_recv.at[n], device_id=neighbour_of(d), device_id_type=MESH,
        )

    def code_edges(d):
        for j in (0, 1):
            x = edge(d, j)
            make_factor(x)
            begin_chain(OWN, x)
            edge_out[d, j] = write_log(u[OWN, 0, x + 2], 1)
            edge_out[d, 3 + j] = write_code(psi_v[x + 2], *psi_span)
        for h in range(parts):
            edge_out[d, 2, h] = write_code(w_v[edge(d, 0) + 1, :, plane(h)], *w_span)

    far = slab % 2
    code_edges(far)

    @pl.when(jnp.logical_not(first_slab))
    def _():
        edge_copy(0, far).start()

    code_group(1)
    field(1).start()
    code_edges(1 - far)
    edge_copy(0, 1 - far).start()
    code_group(2)
    code_group(3)
    field(2).start()
    field(3).start()

    stages = len(near)

    def open_gate(stage):
        pl.semaphore_signal(gate.at[stage], inc=1, device_id=near[stage], device_id_type=MESH)

    def pass_gate(stage):
        pl.semaphore_wait(gate.at[stage], 1)
        if stage + 1 < stages:
            open_gate(stage + 1)

    open_gate(0)
    loop(2, layers - 2, make_factor)
    loop(2, layers - 2, functools.partial(begin_chain, OWN))
    pass_gate(0)
    adv(OWN, 0, 1, layers - 1)
    adv(OWN, 1, 2, layers - 2)
    adv(OWN, 2, 3, layers - 3)

    def make_base(x):
        center, sums = around(psi_v, (x + 2,), EDGE, window.size)
        for h in range(parts):
            total = psi_v[x + 1, h, window] + psi_v[x + 3, h, window] + sums[h]
            base[x + 1, h] = relaxation(center[h], total)

    @pl.when(first_slab)
    def _():
        pl.semaphore_wait(seam_gate, 1)
        edge_copy(0, 0).start()

    loop(1, layers - 1, make_base)
    pass_gate(1)

    def halo(kind, d, first, count):
        return pltpu.make_async_remote_copy(
            halo_out.at[kind, d, pl.ds(first, count)], halo_in.at[kind, d, pl.ds(first, count)],
            halo_send, halo_recv.at[kind, d],
            device_id=neighbour_of(d), device_id_type=MESH,
        )

    def arrive(group):
        taken(field_in.at[slots[group]], field_recv.at[group])
        for x in groups[group]:
            begin_chain(FOREIGN, x)

    for j in (0, 1):
        arrive(j)
        for d in (0, 1):
            halo_out[0, d, j] = write_log(u[FOREIGN, 0, out_layer(d, j) + 2], 1)
            halo(0, d, j, 1).start()
    edge_copy(1, 0).start()
    edge_copy(1, 1).start()

    pass_gate(2)
    taken(edge_in.at[:, pl.ds(0, 4)], edge_recv.at[0])
    for d in (0, 1):
        x = in_layer(d, 0)
        for h in range(parts):
            w_v[x + 1, :, plane(h)] = read_code(edge_in[d, 2, h], *w_span)
        psi_v[x + 2] = read_code(edge_in[d, 3], *psi_span)
        for j in (0, 1):
            u[OWN, 0, in_layer(d, j) + 2] = read_log(edge_in[d, j], 1)
    beyond(make_factor)
    beyond(functools.partial(advance_halo, OWN, 0))
    outer(functools.partial(advance, OWN, 0))

    def half_way(chain, kind):
        for d in (0, 1):
            edge_pair(d, functools.partial(advance, chain, 1))
            for j in (0, 1):
                halo_out[kind, d, j] = write_log(u[chain, 2, out_layer(d, j) + 2], 5)
            halo(kind, d, 0, 2).start()

    half_way(OWN, 1)
    arrive(2)
    ring(1, functools.partial(advance, FOREIGN, 0))
    arrive(3)
    ring(2, functools.partial(advance, FOREIGN, 0))
    sides = (1 - slab % 2, slab % 2)
    first_side = jnp.where(slab % (slabs - 1) == 0, sides[0], sides[1])
    for d in (first_side, 1 - first_side):
        taken(halo_in.at[0, 1 - d], halo_recv.at[0, 1 - d])
        for j in (0, 1):
            u[FOREIGN, 0, edge(d, -1 - j) + 2] = read_log(halo_in[0, 1 - d, j], 1)
        advance_halo(FOREIGN, 0, edge(d, -1))
        for j in (0,):
            advance(FOREIGN, 0, edge(d, j))
        for j in (0, 1):
            advance(FOREIGN, 1, edge(d, j))
            halo_out[2, d, j] = write_log(u[FOREIGN, 2, edge(d, j) + 2], 5)
        halo(2, d, 0, 2).start()

    adv(FOREIGN, 0, 3, layers - 3)
    for stage in range(3, stages - 1):
        pass_gate(stage)
    adv(OWN, 2, 1, 3)
    adv(OWN, 2, layers - 3, layers - 1)
    adv(OWN, 3, 2, layers - 2)
    adv(FOREIGN, 1, 2, layers - 2)
    adv(FOREIGN, 2, 1, layers - 1)

    def second_half(chain, kind):
        for d in (0, 1):
            taken(halo_in.at[kind, d], halo_recv.at[kind, d])
            for j in (0, 1):
                u[chain, 2, in_layer(d, j) + 2] = read_log(halo_in[kind, d, j], 5)
        beyond(functools.partial(advance_halo, chain, 2))
        outer(functools.partial(advance, chain, 2))

    weights = [0.5 if t in (0, NS) else 1.0 for t in range(NS + 1)]
    charged = [weights[t] * q[t] for t in range(NS + 1)]

    def gathered(x, h, terms):
        phi_layer, rho_layer = 0.0, 0.0
        for t in terms:
            product = rounded[OWN, t, x, h, window] * rounded[FOREIGN, NS - t, x, h, window]
            phi_layer = phi_layer + (product if weights[t] == 1.0 else weights[t] * product)
            rho_layer = rho_layer + charged[t] * product
        return phi_layer, rho_layer

    def gather(x):
        for h in range(parts):
            phi[x, h], rho[x + 1, h] = gathered(x, h, range(2, NS + 1))

    def complete(x, early):
        for h, value in enumerate(advanced(FOREIGN, NS - 1, x)):
            phi_layer, rho_layer = gathered(x, h, range(1, 2 if early else NS + 1))
            product = rounded[OWN, 0, x, h, window] * to_bfloat16(value)
            phi_layer = phi_layer + weights[0] * product
            rho_layer = rho_layer + charged[0] * product
            phi[x, h] = phi[x, h] + phi_layer if early else phi_layer
            rho[x + 1, h] = rho[x + 1, h] + rho_layer if early else rho_layer

    def whole(x):
        complete(x, False)

    def finish(x):
        complete(x, True)

    loop(2, layers - 2, whole)

    pass_gate(stages - 1)
    second_half(OWN, 1)
    for d in (0, 1):
        edge_pair(d, functools.partial(advance, OWN, 3))

    def cells_of(x):
        return sum(phi[x, h, inner] for h in range(parts))

    partial = sum(cells_of(x) for x in range(2, layers - 2))

    for d in (0, 1):
        edge_pair(d, gather)

    taken(edge_in.at[:, pl.ds(4, 1)], edge_recv.at[1])
    for d in (0, 1):
        psi_v[in_layer(d, 1) + 2] = read_code(edge_in[d, 4], *psi_span)
    for k in (-1, 0):
        make_base(k)
        make_base(layers - 1 - k)

    bits = [1 << k for k in range(slabs.bit_length() - 1)]
    flips = [bit - 2 * bit * lax.rem(slab // bit, 2) for bit in bits]

    def mirror(mask):
        target = slab
        for bit, flip in zip(bits, flips):
            target = target + flip if mask & bit else target
        return (other if mask >= slabs else side, target)

    masks = sorted(range(1, devices), key=lambda mask: (-(mask % slabs // 4), -mask))
    receivers = [(mask, mirror(mask)) for mask in masks] if ends == 2 and devices <= 32 else None
    for d in sides:
        taken(halo_in.at[2, 1 - d], halo_recv.at[2, 1 - d])
        for j in (0, 1):
            u[FOREIGN, 2, edge(d, -1 - j) + 2] = read_log(halo_in[2, 1 - d, j], 5)
        advance_halo(FOREIGN, 2, edge(d, -1))
        advance(FOREIGN, 2, edge(d, 0))
        finish(edge(d, 0))
        rho_out[d] = rho[edge(d, 0) + 1].astype(jnp.bfloat16)
        pltpu.make_async_remote_copy(
            rho_out.at[d], rho_in.at[d], rho_send, rho_recv, device_id=neighbour_of(d), device_id_type=MESH,
        ).start()
        finish(edge(d, 1))
        partial = partial + cells_of(edge(d, 0)) + cells_of(edge(d, 1))
    sums[0] = jnp.sum(partial, axis=0, keepdims=True)

    def share(step, target):
        pltpu.make_async_remote_copy(
            sums.at[0], sums.at[step], sum_send, sum_recv, device_id=target, device_id_type=MESH,
        ).start()

    if receivers is not None:
        for step, target in receivers:
            share(step, target)
    else:
        lax.fori_loop(1, devices, lambda step, carry: (share(step, device(step)), carry)[1], 0)

    others = sums.at[pl.ds(1, devices - 1)]
    taken(rho_in, rho_recv)
    for d in (0, 1):
        rho[in_layer(d, 0) + 1] = rho_in[d].astype(jnp.float32)
    taken(others, sum_recv)
    cells = float(devices * layers * half * w_hbm.shape[2])
    inverse = cells / jnp.sum(sums[...])
    scale_ref[...] = jnp.broadcast_to(inverse, scale_ref.shape)

    for ref, semaphore in (
        (field_out, field_send), (edge_out, edge_send), (halo_out, halo_send), (rho_out, rho_send), (others, sum_send)
    ):
        taken(ref, semaphore)


def ion_charge(value):
    return (2.0 * screening) * jnp.tanh(0.5 * value)


def relaxation(center, total):
    return (total - ion_charge(center) + screening * center) * (1.0 / (6.0 + screening))


def around(ref, at, first, count):
    parts = ref.shape[-3]
    lane = lax.broadcasted_iota(jnp.int32, (1, LANES), 1)
    lowest, highest = lane == 0, lane == LANES - 1
    center = [ref[(*at, h, pl.ds(first, count))] for h in range(parts)]
    lower = [pltpu.roll(value, 1, 1) for value in center]
    upper = [pltpu.roll(value, LANES - 1, 1) for value in center]
    sums = []
    for h in range(parts):
        total = ref[(*at, h, pl.ds(first - 1, count))] + ref[(*at, h, pl.ds(first + 1, count))]
        total = total + jnp.where(lowest, lower[h - 1], lower[h])
        sums.append(total + jnp.where(highest, upper[(h + 1) % parts], upper[h]))
    return center, sums


def finishing(phi, rho, base, scale_ref, density_hbm, potential_hbm, density, potential, relaxed, density_sem, potential_sem):
    layers, half = density_hbm.shape[0], density_hbm.shape[1]
    parts = phi.shape[1]
    inner = pl.ds(PAD - EDGE, half)
    inverse = scale_ref[...]
    scaled = inverse * (1.0 / (6.0 + screening))

    def plane(h):
        return slice(h * LANES, (h + 1) * LANES)

    for x in range(layers):
        for h in range(parts):
            density[x, :, plane(h)] = phi[x, h, inner] * inverse
    pltpu.make_async_copy(density, density_hbm, density_sem).start()
    for x in range(layers + 2):
        for h in range(parts):
            relaxed[x, h] = base[x, h] + rho[x, h] * scaled
    for x in range(layers):
        center, sums = around(relaxed, (x + 1,), PAD - EDGE, half)
        for h in range(parts):
            total = relaxed[x, h, inner] + relaxed[x + 2, h, inner] + sums[h]
            potential[x, :, plane(h)] = relaxation(center[h], total) + rho[x + 1, h, inner] * scaled
        if x % CHUNK == CHUNK - 1:
            done = pl.ds(x + 1 - CHUNK, CHUNK)
            pltpu.make_async_copy(potential.at[done], potential_hbm.at[done], potential_sem).start()
    pltpu.make_async_copy(density, density_hbm, density_sem).wait()
    pltpu.make_async_copy(potential, potential_hbm, potential_sem).wait()


def body(ends, slabs, w_field, psi_init, start_field, charges):
    layers, rows, depth = w_field.shape
    half = rows // ends
    wide = half + 2 * PAD
    devices = ends * slabs
    stages = slabs.bit_length()
    out = jax.ShapeDtypeStruct((layers, half, depth), jnp.float32)
    dma = pltpu.SemaphoreType.DMA

    parts = depth // LANES
    narrow = half + 2 * (PAD - EDGE)

    def tile(*lead):
        return pltpu.VMEM((*lead, parts, wide, LANES), jnp.float32)

    def slim(*lead):
        return pltpu.VMEM((*lead, parts, narrow, LANES), jnp.float32)

    def whole_rows(*lead):
        return pltpu.VMEM((*lead, wide, depth), jnp.float32)

    edge_rho = pltpu.VMEM((2, parts, narrow, LANES), jnp.bfloat16)

    def code(*lead):
        return pltpu.VMEM((*lead, parts, wide, LANES), jnp.int16)

    hbm = pl.BlockSpec(memory_space=pltpu.HBM)
    vmem = pl.BlockSpec(memory_space=pltpu.VMEM)
    def planes(count):
        return jax.ShapeDtypeStruct((count, parts, narrow, LANES), jnp.float32)

    fields = pl.pallas_call(
        functools.partial(kernel, ends, slabs),
        out_shape=(planes(layers), planes(layers + 2), planes(layers + 2), jax.ShapeDtypeStruct((1, LANES), jnp.float32)),
        in_specs=[hbm, hbm, hbm, hbm],
        out_specs=(vmem, vmem, vmem, vmem),
        scratch_shapes=[
            pltpu.SMEM((NS + 1,), jnp.int32), whole_rows(layers + 2), tile(layers + 4), whole_rows(layers), whole_rows(layers),
            tile(NS, layers + 2), tile(2, NS, layers + 4), tile(2, NS + 1, layers),
            pltpu.VMEM((devices, 1, LANES), jnp.float32),
            code(layers), code(layers), code(2, 5), code(2, 5), code(3, 2, 2), code(3, 2, 2), edge_rho, edge_rho,
            pltpu.SemaphoreType.REGULAR((stages,)), pltpu.SemaphoreType.REGULAR, dma(()), dma((4,)), dma((3,)), dma(()), dma((4,)),
            dma(()), dma((2,)), dma(()), dma((3, 2)), dma(()), dma(()), dma(()), dma(()),
        ],
        compiler_params=pltpu.CompilerParams(
            collective_id=0, has_side_effects=True, vmem_limit_bytes=40 * 1024 * 1024
        ),
        name="scf_step",
    )(*[pltpu.with_memory_space_constraint(v, pltpu.HBM) for v in (charges, w_field, psi_init, start_field)])
    result = pltpu.VMEM((layers, half, depth), jnp.float32)
    return pl.pallas_call(
        finishing,
        out_shape=(out, out),
        in_specs=[vmem] * 4,
        out_specs=(hbm, hbm),
        scratch_shapes=[result, result, slim(layers + 2), dma(()), dma(())],
        name="finishing",
    )(*[pltpu.with_memory_space_constraint(v, pltpu.VMEM) for v in fields])


def solution(mesh):
    in_specs = (P("slab", None, None), P("slab", None, None), P("end", "slab", None, None), P())
    out_specs = (P("slab", "end", None), P("slab", "end", None))
    step = functools.partial(body, mesh.shape["end"], mesh.shape["slab"])
    return jax.shard_map(step, mesh=mesh, in_specs=in_specs, out_specs=out_specs, check_vma=False)
```

```python
import functools
import math

import jax
import jax.numpy as jnp
from jax import lax
from jax.experimental import pallas as pl
from jax.experimental.pallas import tpu as pltpu
from jax.sharding import PartitionSpec as P

NS = 4
PAD = 8
EDGE = 4
LANES = 128
CHUNK = 4
mobility = 0.15
screening = 1.0
OWN, FOREIGN = 0, 1
W_MAX, PSI_MAX = 4.0, 3.0
START_MIN, START_MAX = 0.25, 8.0
CODES, OFFSET = 65535.0, 32768
MARGIN = 0.001
MESH = pl.DeviceIdType.MESH


def kernel(ends, slabs, charges_hbm, w_hbm, psi_hbm, start_hbm, phi, rho, base, scale_ref,
           charges_ref, w_v, psi_v, start_v, theirs_v, factor, u, rounded, sums,
           field_out, field_in, edge_out, edge_in, halo_out, halo_in, rho_out, rho_in,
           gate, seam_gate, charges_sem, field_sem, local_sem, field_send, field_recv, edge_send, edge_recv, halo_send, halo_recv,
           rho_send, rho_recv, sum_send, sum_recv):
    side, slab = lax.axis_index("end"), lax.axis_index("slab")
    other = lax.rem(side + 1, ends)
    left = (side, lax.rem(slab + slabs - 1, slabs))
    right = (side, lax.rem(slab + 1, slabs))
    partner = (other, slab)
    layers, rows = w_hbm.shape[0], w_hbm.shape[1]
    half = rows // ends
    parts = w_hbm.shape[2] // LANES
    devices = ends * slabs
    flat = side * slabs + slab
    delta = 1.0 / NS

    def device(distance):
        target = lax.rem(flat + distance, devices)
        return (target // slabs, lax.rem(target, slabs))

    barrier = pltpu.get_barrier_semaphore()
    charges_copy = pltpu.make_async_copy(charges_hbm, charges_ref, charges_sem)
    charges_copy.start()

    near = []
    width = 1
    while width < slabs:
        near.append((side, slab + width - 2 * width * lax.rem(slab // width, 2)))
        width *= 2
    near.append(partner)
    first_slab, last_slab = slab == 0, slab == slabs - 1
    for neighbour in near + [left]:
        pl.semaphore_signal(barrier, inc=1, device_id=neighbour, device_id_type=MESH)

    @pl.when(jnp.logical_not(last_slab))
    def _():
        pl.semaphore_signal(barrier, inc=1, device_id=right, device_id_type=MESH)

    greeted = len(near) + jnp.where(first_slab, 1, 2)
    targets = (left, right)

    def pieces(which):
        first = which * half
        return (
            (pl.multiple_of(first, 8), PAD, half),
            (pl.multiple_of(lax.rem(first + rows - PAD, rows), 8), 0, PAD),
            (pl.multiple_of(lax.rem(first + half, rows), 8), PAD + half, PAD),
        )

    mine, theirs = pieces(side), pieces(other)
    groups = [(0, layers - 1), (1, layers - 2), (2, layers - 3), tuple(range(3, layers - 3))]
    firsts = [sum(len(group) for group in groups[:k]) for k in range(len(groups))]
    slots = [pl.ds(first, len(group)) for first, group in zip(firsts, groups)]
    slot_of = {x: first + k for first, group in zip(firsts, groups) for k, x in enumerate(group)}
    for k, group in enumerate(groups):
        for x in group:
            for begin, at, count in theirs:
                pltpu.make_async_copy(
                    start_hbm.at[0, x, pl.ds(begin, count)], theirs_v.at[slot_of[x], pl.ds(at, count)], field_sem.at[k],
                ).start()
    for begin, at, count in mine:
        pltpu.make_async_copy(
            w_hbm.at[:, pl.ds(begin, count)], w_v.at[pl.ds(1, layers), pl.ds(at, count)], local_sem.at[0],
        ).start()
        for h in range(parts):
            pltpu.make_async_copy(
                psi_hbm.at[:, pl.ds(begin, count), pl.ds(h * LANES, LANES)],
                psi_v.at[pl.ds(2, layers), h, pl.ds(at, count)], local_sem.at[1],
            ).start()
        pltpu.make_async_copy(
            start_hbm.at[0, :, pl.ds(begin, count)], start_v.at[:, pl.ds(at, count)], local_sem.at[2],
        ).start()

    def taken(ref, semaphore):
        pltpu.make_async_copy(ref, ref, semaphore).wait()

    def loop(low, high, step):
        def body(x, carry):
            step(x)
            return carry

        lax.fori_loop(low, high, body, 0, unroll=True)

    def span(t):
        reach = 0.5 * delta * (W_MAX + PSI_MAX) * t + MARGIN
        shift = 0.5 * math.log(mobility) if t else 0.0
        return math.log(START_MIN) - reach + shift, math.log(START_MAX) + reach + shift

    def write_code(value, low, high):
        scaled = value * (CODES / (high - low)) + (0.5 - low * (CODES / (high - low)))
        return (scaled.astype(jnp.int32) - OFFSET).astype(jnp.int16)

    def read_code(code, low, high):
        step = (high - low) / CODES
        return code.astype(jnp.int32).astype(jnp.float32) * step + (low + OFFSET * step)

    def write_log(value, t):
        return write_code(jnp.log(value), *span(t))

    def read_log(code, t):
        return jnp.exp(read_code(code, *span(t)))

    w_span, psi_span = (-W_MAX - MARGIN, W_MAX + MARGIN), (-PSI_MAX - MARGIN, PSI_MAX + MARGIN)

    def plane(h):
        return slice(h * LANES, (h + 1) * LANES)

    def field(k):
        return pltpu.make_async_remote_copy(
            field_out.at[slots[k]], field_in.at[slots[k]], field_send, field_recv.at[k],
            device_id=partner, device_id_type=MESH,
        )

    def code_group(k):
        taken(theirs_v.at[slots[k]], field_sem.at[k])
        for x in groups[k]:
            for h in range(parts):
                field_out[slot_of[x], h] = write_log(theirs_v[slot_of[x], :, plane(h)], 0)

    code_group(0)
    pl.semaphore_wait(barrier, greeted)

    @pl.when(last_slab)
    def _():
        pl.semaphore_signal(seam_gate, inc=1, device_id=right, device_id_type=MESH)

    field(0).start()

    charges_copy.wait()
    q = [charges_ref[side * (NS - 2 * t) + t].astype(jnp.float32) for t in range(NS + 1)]
    pair = [0.5 * (q[k] + q[k + 1]) for k in range(NS)]

    def make_factor(x):
        for h in range(parts):
            level = 0.5 * math.log(mobility) - 0.5 * delta * w_v[x + 1, :, plane(h)]
            psi = psi_v[x + 2, h]
            for k in range(NS):
                factor[k, x + 1, h] = jnp.exp(level - (0.5 * delta * pair[k]) * psi)

    def index(chain, t):
        return t if chain == OWN else NS - 1 - t

    def to_bfloat16(value):
        return value.astype(jnp.bfloat16).astype(jnp.float32)

    window = pl.ds(EDGE, half + 2 * (PAD - EDGE))
    inner = pl.ds(PAD - EDGE, half)

    def begin_chain(chain, x):
        for h in range(parts):
            value = start_v[x, :, plane(h)] if chain == OWN else read_log(field_in[slot_of[x], h], 0)
            u[chain, 0, x + 2, h] = factor[index(chain, 0), x + 1, h] * value
            rounded[chain, 0, x, h] = to_bfloat16(value)

    def advanced(chain, t, x):
        center, sums = around(u, (chain, t, x + 2), EDGE, window.size)
        return [
            factor[index(chain, t), x + 1, h, window] * (
                (u[chain, t, x + 1, h, window] + u[chain, t, x + 3, h, window])
                + (sums[h] + ((1.0 - 6.0 * mobility) / mobility) * center[h])
            )
            for h in range(parts)
        ]

    def advance_halo(chain, t, x):
        for h, value in enumerate(advanced(chain, t, x)):
            u[chain, t + 1, x + 2, h, window] = factor[index(chain, t + 1), x + 1, h, window] * value

    def advance(chain, t, x):
        for h, value in enumerate(advanced(chain, t, x)):
            rounded[chain, t + 1, x, h, window] = to_bfloat16(value)
            if t + 1 < NS:
                u[chain, t + 1, x + 2, h, window] = factor[index(chain, t + 1), x + 1, h, window] * value

    def adv(chain, t, low, high):
        loop(low, high, functools.partial(advance, chain, t))

    def outer(step):
        loop(0, 2, lambda k: step((layers - 1) * k))

    def ring(first, step):
        loop(0, 2, lambda k: step(first + (layers - 1 - 2 * first) * k))

    def beyond(step):
        loop(0, 2, lambda k: step((layers + 1) * k - 1))

    def edge_pair(d, step):
        loop(0, 2, lambda j: step(j + d * (layers - 2)))

    def out_layer(d, j):
        return layers - 1 - j if d else j

    def in_layer(d, j):
        return -1 - j if d else layers + j

    taken(w_v.at[pl.ds(1, layers)], local_sem.at[0])
    taken(psi_v.at[pl.ds(2, layers)], local_sem.at[1])
    taken(start_v, local_sem.at[2])
    def neighbour_of(d):
        return (side, lax.rem(slab + slabs + 2 * d - 1, slabs))

    def edge(d, k):
        return d * (layers - 1) + k * (1 - 2 * d)

    def edge_copy(n, d):
        first, count = ((0, 4), (4, 1))[n]
        return pltpu.make_async_remote_copy(
            edge_out.at[d, pl.ds(first, count)], edge_in.at[d, pl.ds(first, count)],
            edge_send, edge_recv.at[n, d], device_id=neighbour_of(d), device_id_type=MESH,
        )

    def code_edges(d):
        for j in (0, 1):
            x = edge(d, j)
            make_factor(x)
            begin_chain(OWN, x)
            edge_out[d, j] = write_log(u[OWN, 0, x + 2], 1)
            edge_out[d, 3 + j] = write_code(psi_v[x + 2], *psi_span)
        for h in range(parts):
            edge_out[d, 2, h] = write_code(w_v[edge(d, 0) + 1, :, plane(h)], *w_span)

    far = slab % 2
    code_edges(far)

    @pl.when(jnp.logical_not(first_slab))
    def _():
        edge_copy(0, far).start()

    code_group(1)
    field(1).start()
    code_edges(1 - far)
    edge_copy(0, 1 - far).start()
    code_group(2)
    code_group(3)
    field(2).start()
    field(3).start()

    stages = len(near)

    def open_gate(stage):
        pl.semaphore_signal(gate.at[stage], inc=1, device_id=near[stage], device_id_type=MESH)

    def pass_gate(stage):
        pl.semaphore_wait(gate.at[stage], 1)
        if stage + 1 < stages:
            open_gate(stage + 1)

    open_gate(0)
    loop(2, layers - 2, make_factor)
    loop(2, layers - 2, functools.partial(begin_chain, OWN))
    pass_gate(0)
    adv(OWN, 0, 1, layers - 1)
    adv(OWN, 1, 2, layers - 2)
    adv(OWN, 2, 3, layers - 3)

    def make_base(x):
        center, sums = around(psi_v, (x + 2,), EDGE, window.size)
        for h in range(parts):
            total = psi_v[x + 1, h, window] + psi_v[x + 3, h, window] + sums[h]
            base[x + 1, h] = relaxation(center[h], total)

    @pl.when(first_slab)
    def _():
        pl.semaphore_wait(seam_gate, 1)
        edge_copy(0, 0).start()

    loop(1, layers - 1, make_base)
    pass_gate(1)

    def halo(kind, d, first, count):
        return pltpu.make_async_remote_copy(
            halo_out.at[kind, d, pl.ds(first, count)], halo_in.at[kind, d, pl.ds(first, count)],
            halo_send, halo_recv.at[kind, d],
            device_id=neighbour_of(d), device_id_type=MESH,
        )

    def arrive(group):
        taken(field_in.at[slots[group]], field_recv.at[group])
        for x in groups[group]:
            begin_chain(FOREIGN, x)

    for j in (0, 1):
        arrive(j)
        for d in (0, 1):
            halo_out[0, d, j] = write_log(u[FOREIGN, 0, out_layer(d, j) + 2], 1)
            halo(0, d, j, 1).start()
    edge_copy(1, 0).start()
    edge_copy(1, 1).start()

    pass_gate(2)
    for d in (1 - far, far):
        taken(edge_in.at[1 - d, pl.ds(0, 4)], edge_recv.at[0, 1 - d])
        x = edge(d, -1)
        for h in range(parts):
            w_v[x + 1, :, plane(h)] = read_code(edge_in[1 - d, 2, h], *w_span)
        psi_v[x + 2] = read_code(edge_in[1 - d, 3], *psi_span)
        for j in (0, 1):
            u[OWN, 0, edge(d, -1 - j) + 2] = read_log(edge_in[1 - d, j], 1)
        make_factor(x)
        advance_halo(OWN, 0, x)
        advance(OWN, 0, edge(d, 0))
        for j in (0, 1):
            advance(OWN, 1, edge(d, j))
            halo_out[1, d, j] = write_log(u[OWN, 2, edge(d, j) + 2], 5)
        halo(1, d, 0, 2).start()
    arrive(2)
    ring(1, functools.partial(advance, FOREIGN, 0))
    arrive(3)
    ring(2, functools.partial(advance, FOREIGN, 0))
    sides = (1 - slab % 2, slab % 2)
    first_side = jnp.where(slab % (slabs - 1) == 0, sides[0], sides[1])
    for d in (first_side, 1 - first_side):
        taken(halo_in.at[0, 1 - d], halo_recv.at[0, 1 - d])
        for j in (0, 1):
            u[FOREIGN, 0, edge(d, -1 - j) + 2] = read_log(halo_in[0, 1 - d, j], 1)
        advance_halo(FOREIGN, 0, edge(d, -1))
        for j in (0,):
            advance(FOREIGN, 0, edge(d, j))
        for j in (0, 1):
            advance(FOREIGN, 1, edge(d, j))
            halo_out[2, d, j] = write_log(u[FOREIGN, 2, edge(d, j) + 2], 5)
        halo(2, d, 0, 2).start()

    adv(FOREIGN, 0, 3, layers - 3)
    for stage in range(3, stages - 1):
        pass_gate(stage)
    adv(OWN, 2, 1, 3)
    adv(OWN, 2, layers - 3, layers - 1)
    adv(OWN, 3, 2, layers - 2)
    adv(FOREIGN, 1, 2, layers - 2)
    adv(FOREIGN, 2, 1, layers - 1)

    def second_half(chain, kind):
        for d in (0, 1):
            taken(halo_in.at[kind, d], halo_recv.at[kind, d])
            for j in (0, 1):
                u[chain, 2, in_layer(d, j) + 2] = read_log(halo_in[kind, d, j], 5)
        beyond(functools.partial(advance_halo, chain, 2))
        outer(functools.partial(advance, chain, 2))

    weights = [0.5 if t in (0, NS) else 1.0 for t in range(NS + 1)]
    charged = [weights[t] * q[t] for t in range(NS + 1)]

    def gathered(x, h, terms):
        phi_layer, rho_layer = 0.0, 0.0
        for t in terms:
            product = rounded[OWN, t, x, h, window] * rounded[FOREIGN, NS - t, x, h, window]
            phi_layer = phi_layer + (product if weights[t] == 1.0 else weights[t] * product)
            rho_layer = rho_layer + charged[t] * product
        return phi_layer, rho_layer

    def gather(x):
        for h in range(parts):
            phi[x, h], rho[x + 1, h] = gathered(x, h, range(2, NS + 1))

    def complete(x, early):
        for h, value in enumerate(advanced(FOREIGN, NS - 1, x)):
            phi_layer, rho_layer = gathered(x, h, range(1, 2 if early else NS + 1))
            product = rounded[OWN, 0, x, h, window] * to_bfloat16(value)
            phi_layer = phi_layer + weights[0] * product
            rho_layer = rho_layer + charged[0] * product
            phi[x, h] = phi[x, h] + phi_layer if early else phi_layer
            rho[x + 1, h] = rho[x + 1, h] + rho_layer if early else rho_layer

    def whole(x):
        complete(x, False)

    def finish(x):
        complete(x, True)

    loop(2, layers - 2, whole)

    pass_gate(stages - 1)
    second_half(OWN, 1)
    for d in (0, 1):
        edge_pair(d, functools.partial(advance, OWN, 3))

    def cells_of(x):
        return sum(phi[x, h, inner] for h in range(parts))

    partial = sum(cells_of(x) for x in range(2, layers - 2))

    for d in (0, 1):
        edge_pair(d, gather)

    for d in (0, 1):
        taken(edge_in.at[d, pl.ds(4, 1)], edge_recv.at[1, d])
    for d in (0, 1):
        psi_v[in_layer(d, 1) + 2] = read_code(edge_in[d, 4], *psi_span)
    for k in (-1, 0):
        make_base(k)
        make_base(layers - 1 - k)

    bits = [1 << k for k in range(slabs.bit_length() - 1)]
    flips = [bit - 2 * bit * lax.rem(slab // bit, 2) for bit in bits]

    def mirror(mask):
        target = slab
        for bit, flip in zip(bits, flips):
            target = target + flip if mask & bit else target
        return (other if mask >= slabs else side, target)

    masks = sorted(range(1, devices), key=lambda mask: (-(mask % slabs // 4), -mask))
    receivers = [(mask, mirror(mask)) for mask in masks] if ends == 2 and devices <= 32 else None
    for d in sides:
        taken(halo_in.at[2, 1 - d], halo_recv.at[2, 1 - d])
        for j in (0, 1):
            u[FOREIGN, 2, edge(d, -1 - j) + 2] = read_log(halo_in[2, 1 - d, j], 5)
        advance_halo(FOREIGN, 2, edge(d, -1))
        advance(FOREIGN, 2, edge(d, 0))
        finish(edge(d, 0))
        rho_out[d] = rho[edge(d, 0) + 1].astype(jnp.bfloat16)
        pltpu.make_async_remote_copy(
            rho_out.at[d], rho_in.at[d], rho_send, rho_recv, device_id=neighbour_of(d), device_id_type=MESH,
        ).start()
        finish(edge(d, 1))
        partial = partial + cells_of(edge(d, 0)) + cells_of(edge(d, 1))
    sums[0] = jnp.sum(partial, axis=0, keepdims=True)

    def share(step, target):
        pltpu.make_async_remote_copy(
            sums.at[0], sums.at[step], sum_send, sum_recv, device_id=target, device_id_type=MESH,
        ).start()

    if receivers is not None:
        for step, target in receivers:
            share(step, target)
    else:
        lax.fori_loop(1, devices, lambda step, carry: (share(step, device(step)), carry)[1], 0)

    others = sums.at[pl.ds(1, devices - 1)]
    taken(rho_in, rho_recv)
    for d in (0, 1):
        rho[in_layer(d, 0) + 1] = rho_in[d].astype(jnp.float32)
    taken(others, sum_recv)
    cells = float(devices * layers * half * w_hbm.shape[2])
    inverse = cells / jnp.sum(sums[...])
    scale_ref[...] = jnp.broadcast_to(inverse, scale_ref.shape)

    for ref, semaphore in (
        (field_out, field_send), (edge_out, edge_send), (halo_out, halo_send), (rho_out, rho_send), (others, sum_send)
    ):
        taken(ref, semaphore)


def ion_charge(value):
    return (2.0 * screening) * jnp.tanh(0.5 * value)


def relaxation(center, total):
    return (total - ion_charge(center) + screening * center) * (1.0 / (6.0 + screening))


def around(ref, at, first, count):
    parts = ref.shape[-3]
    lane = lax.broadcasted_iota(jnp.int32, (1, LANES), 1)
    lowest, highest = lane == 0, lane == LANES - 1
    center = [ref[(*at, h, pl.ds(first, count))] for h in range(parts)]
    lower = [pltpu.roll(value, 1, 1) for value in center]
    upper = [pltpu.roll(value, LANES - 1, 1) for value in center]
    sums = []
    for h in range(parts):
        total = ref[(*at, h, pl.ds(first - 1, count))] + ref[(*at, h, pl.ds(first + 1, count))]
        total = total + jnp.where(lowest, lower[h - 1], lower[h])
        sums.append(total + jnp.where(highest, upper[(h + 1) % parts], upper[h]))
    return center, sums


def finishing(phi, rho, base, scale_ref, density_hbm, potential_hbm, density, potential, relaxed, density_sem, potential_sem):
    layers, half = density_hbm.shape[0], density_hbm.shape[1]
    parts = phi.shape[1]
    inner = pl.ds(PAD - EDGE, half)
    inverse = scale_ref[...]
    scaled = inverse * (1.0 / (6.0 + screening))

    def plane(h):
        return slice(h * LANES, (h + 1) * LANES)

    for x in range(layers):
        for h in range(parts):
            density[x, :, plane(h)] = phi[x, h, inner] * inverse
    pltpu.make_async_copy(density, density_hbm, density_sem).start()
    for x in range(layers + 2):
        for h in range(parts):
            relaxed[x, h] = base[x, h] + rho[x, h] * scaled
    for x in range(layers):
        center, sums = around(relaxed, (x + 1,), PAD - EDGE, half)
        for h in range(parts):
            total = relaxed[x, h, inner] + relaxed[x + 2, h, inner] + sums[h]
            potential[x, :, plane(h)] = relaxation(center[h], total) + rho[x + 1, h, inner] * scaled
        if x % CHUNK == CHUNK - 1:
            done = pl.ds(x + 1 - CHUNK, CHUNK)
            pltpu.make_async_copy(potential.at[done], potential_hbm.at[done], potential_sem).start()
    pltpu.make_async_copy(density, density_hbm, density_sem).wait()
    pltpu.make_async_copy(potential, potential_hbm, potential_sem).wait()


def body(ends, slabs, w_field, psi_init, start_field, charges):
    layers, rows, depth = w_field.shape
    half = rows // ends
    wide = half + 2 * PAD
    devices = ends * slabs
    stages = slabs.bit_length()
    out = jax.ShapeDtypeStruct((layers, half, depth), jnp.float32)
    dma = pltpu.SemaphoreType.DMA

    parts = depth // LANES
    narrow = half + 2 * (PAD - EDGE)

    def tile(*lead):
        return pltpu.VMEM((*lead, parts, wide, LANES), jnp.float32)

    def slim(*lead):
        return pltpu.VMEM((*lead, parts, narrow, LANES), jnp.float32)

    def whole_rows(*lead):
        return pltpu.VMEM((*lead, wide, depth), jnp.float32)

    edge_rho = pltpu.VMEM((2, parts, narrow, LANES), jnp.bfloat16)

    def code(*lead):
        return pltpu.VMEM((*lead, parts, wide, LANES), jnp.int16)

    hbm = pl.BlockSpec(memory_space=pltpu.HBM)
    vmem = pl.BlockSpec(memory_space=pltpu.VMEM)
    def planes(count):
        return jax.ShapeDtypeStruct((count, parts, narrow, LANES), jnp.float32)

    fields = pl.pallas_call(
        functools.partial(kernel, ends, slabs),
        out_shape=(planes(layers), planes(layers + 2), planes(layers + 2), jax.ShapeDtypeStruct((1, LANES), jnp.float32)),
        in_specs=[hbm, hbm, hbm, hbm],
        out_specs=(vmem, vmem, vmem, vmem),
        scratch_shapes=[
            pltpu.SMEM((NS + 1,), jnp.int32), whole_rows(layers + 2), tile(layers + 4), whole_rows(layers), whole_rows(layers),
            tile(NS, layers + 2), tile(2, NS, layers + 4), tile(2, NS + 1, layers),
            pltpu.VMEM((devices, 1, LANES), jnp.float32),
            code(layers), code(layers), code(2, 5), code(2, 5), code(3, 2, 2), code(3, 2, 2), edge_rho, edge_rho,
            pltpu.SemaphoreType.REGULAR((stages,)), pltpu.SemaphoreType.REGULAR, dma(()), dma((4,)), dma((3,)), dma(()), dma((4,)),
            dma(()), dma((2, 2)), dma(()), dma((3, 2)), dma(()), dma(()), dma(()), dma(()),
        ],
        compiler_params=pltpu.CompilerParams(
            collective_id=0, has_side_effects=True, vmem_limit_bytes=40 * 1024 * 1024
        ),
        name="scf_step",
    )(*[pltpu.with_memory_space_constraint(v, pltpu.HBM) for v in (charges, w_field, psi_init, start_field)])
    result = pltpu.VMEM((layers, half, depth), jnp.float32)
    return pl.pallas_call(
        finishing,
        out_shape=(out, out),
        in_specs=[vmem] * 4,
        out_specs=(hbm, hbm),
        scratch_shapes=[result, result, slim(layers + 2), dma(()), dma(())],
        name="finishing",
    )(*[pltpu.with_memory_space_constraint(v, pltpu.VMEM) for v in fields])


def solution(mesh):
    in_specs = (P("slab", None, None), P("slab", None, None), P("end", "slab", None, None), P())
    out_specs = (P("slab", "end", None), P("slab", "end", None))
    step = functools.partial(body, mesh.shape["end"], mesh.shape["slab"])
    return jax.shard_map(step, mesh=mesh, in_specs=in_specs, out_specs=out_specs, check_vma=False)
```

```python
import functools
import math

import jax
import jax.numpy as jnp
from jax import lax
from jax.experimental import pallas as pl
from jax.experimental.pallas import tpu as pltpu
from jax.sharding import PartitionSpec as P

NS = 4
PAD = 8
EDGE = 4
LANES = 128
CHUNK = 4
mobility = 0.15
screening = 1.0
OWN, FOREIGN = 0, 1
W_MAX, PSI_MAX = 4.0, 3.0
START_MIN, START_MAX = 0.25, 8.0
CODES, OFFSET = 65535.0, 32768
MARGIN = 0.001
MESH = pl.DeviceIdType.MESH


def kernel(ends, slabs, charges_hbm, w_hbm, psi_hbm, start_hbm, phi, rho, base, scale_ref,
           charges_ref, w_v, psi_v, start_v, theirs_v, factor, u, rounded, sums,
           field_out, field_in, edge_out, edge_in, halo_out, halo_in, rho_out, rho_in,
           gate, seam_gate, charges_sem, field_sem, local_sem, field_send, field_recv, edge_send, edge_recv, halo_send, halo_recv,
           rho_send, rho_recv, sum_send, sum_recv):
    side, slab = lax.axis_index("end"), lax.axis_index("slab")
    other = lax.rem(side + 1, ends)
    left = (side, lax.rem(slab + slabs - 1, slabs))
    right = (side, lax.rem(slab + 1, slabs))
    partner = (other, slab)
    layers, rows = w_hbm.shape[0], w_hbm.shape[1]
    half = rows // ends
    parts = w_hbm.shape[2] // LANES
    devices = ends * slabs
    flat = side * slabs + slab
    delta = 1.0 / NS

    def device(distance):
        target = lax.rem(flat + distance, devices)
        return (target // slabs, lax.rem(target, slabs))

    barrier = pltpu.get_barrier_semaphore()
    charges_copy = pltpu.make_async_copy(charges_hbm, charges_ref, charges_sem)
    charges_copy.start()

    near = []
    width = 1
    while width < slabs:
        near.append((side, slab + width - 2 * width * lax.rem(slab // width, 2)))
        width *= 2
    near.append(partner)
    first_slab, last_slab = slab == 0, slab == slabs - 1
    for neighbour in near + [left]:
        pl.semaphore_signal(barrier, inc=1, device_id=neighbour, device_id_type=MESH)

    @pl.when(jnp.logical_not(last_slab))
    def _():
        pl.semaphore_signal(barrier, inc=1, device_id=right, device_id_type=MESH)

    greeted = len(near) + jnp.where(first_slab, 1, 2)
    targets = (left, right)

    def pieces(which):
        first = which * half
        return (
            (pl.multiple_of(first, 8), PAD, half),
            (pl.multiple_of(lax.rem(first + rows - PAD, rows), 8), 0, PAD),
            (pl.multiple_of(lax.rem(first + half, rows), 8), PAD + half, PAD),
        )

    mine, theirs = pieces(side), pieces(other)
    groups = [(0, layers - 1), (1, layers - 2), (2, layers - 3), tuple(range(3, layers - 3))]
    firsts = [sum(len(group) for group in groups[:k]) for k in range(len(groups))]
    slots = [pl.ds(first, len(group)) for first, group in zip(firsts, groups)]
    slot_of = {x: first + k for first, group in zip(firsts, groups) for k, x in enumerate(group)}
    for k, group in enumerate(groups):
        for x in group:
            for begin, at, count in theirs:
                pltpu.make_async_copy(
                    start_hbm.at[0, x, pl.ds(begin, count)], theirs_v.at[slot_of[x], pl.ds(at, count)], field_sem.at[k],
                ).start()
    for begin, at, count in mine:
        pltpu.make_async_copy(
            w_hbm.at[:, pl.ds(begin, count)], w_v.at[pl.ds(1, layers), pl.ds(at, count)], local_sem.at[0],
        ).start()
        for h in range(parts):
            pltpu.make_async_copy(
                psi_hbm.at[:, pl.ds(begin, count), pl.ds(h * LANES, LANES)],
                psi_v.at[pl.ds(2, layers), h, pl.ds(at, count)], local_sem.at[1],
            ).start()
        pltpu.make_async_copy(
            start_hbm.at[0, :, pl.ds(begin, count)], start_v.at[:, pl.ds(at, count)], local_sem.at[2],
        ).start()

    def taken(ref, semaphore):
        pltpu.make_async_copy(ref, ref, semaphore).wait()

    def loop(low, high, step):
        def body(x, carry):
            step(x)
            return carry

        lax.fori_loop(low, high, body, 0, unroll=True)

    def span(t):
        reach = 0.5 * delta * (W_MAX + PSI_MAX) * t + MARGIN
        shift = 0.5 * math.log(mobility) if t else 0.0
        return math.log(START_MIN) - reach + shift, math.log(START_MAX) + reach + shift

    def write_code(value, low, high):
        scaled = value * (CODES / (high - low)) + (0.5 - low * (CODES / (high - low)))
        return (scaled.astype(jnp.int32) - OFFSET).astype(jnp.int16)

    def read_code(code, low, high):
        step = (high - low) / CODES
        return code.astype(jnp.int32).astype(jnp.float32) * step + (low + OFFSET * step)

    def write_log(value, t):
        return write_code(jnp.log(value), *span(t))

    def read_log(code, t):
        return jnp.exp(read_code(code, *span(t)))

    w_span, psi_span = (-W_MAX - MARGIN, W_MAX + MARGIN), (-PSI_MAX - MARGIN, PSI_MAX + MARGIN)

    def plane(h):
        return slice(h * LANES, (h + 1) * LANES)

    def field(k):
        return pltpu.make_async_remote_copy(
            field_out.at[slots[k]], field_in.at[slots[k]], field_send, field_recv.at[k],
            device_id=partner, device_id_type=MESH,
        )

    def code_group(k):
        taken(theirs_v.at[slots[k]], field_sem.at[k])
        for x in groups[k]:
            for h in range(parts):
                field_out[slot_of[x], h] = write_log(theirs_v[slot_of[x], :, plane(h)], 0)

    code_group(0)
    pl.semaphore_wait(barrier, greeted)

    @pl.when(last_slab)
    def _():
        pl.semaphore_signal(seam_gate, inc=1, device_id=right, device_id_type=MESH)

    field(0).start()

    charges_copy.wait()
    q = [charges_ref[side * (NS - 2 * t) + t].astype(jnp.float32) for t in range(NS + 1)]
    pair = [0.5 * (q[k] + q[k + 1]) for k in range(NS)]

    def make_factor(x):
        for h in range(parts):
            level = 0.5 * math.log(mobility) - 0.5 * delta * w_v[x + 1, :, plane(h)]
            psi = psi_v[x + 2, h]
            for k in range(NS):
                factor[k, x + 1, h] = jnp.exp(level - (0.5 * delta * pair[k]) * psi)

    def index(chain, t):
        return t if chain == OWN else NS - 1 - t

    def to_bfloat16(value):
        return value.astype(jnp.bfloat16).astype(jnp.float32)

    window = pl.ds(EDGE, half + 2 * (PAD - EDGE))
    inner = pl.ds(PAD - EDGE, half)

    def begin_chain(chain, x):
        for h in range(parts):
            value = start_v[x, :, plane(h)] if chain == OWN else read_log(field_in[slot_of[x], h], 0)
            u[chain, 0, x + 2, h] = factor[index(chain, 0), x + 1, h] * value
            rounded[chain, 0, x, h] = to_bfloat16(value)

    def advanced(chain, t, x):
        center, sums = around(u, (chain, t, x + 2), EDGE, window.size)
        return [
            factor[index(chain, t), x + 1, h, window] * (
                (u[chain, t, x + 1, h, window] + u[chain, t, x + 3, h, window])
                + (sums[h] + ((1.0 - 6.0 * mobility) / mobility) * center[h])
            )
            for h in range(parts)
        ]

    def advance_halo(chain, t, x):
        for h, value in enumerate(advanced(chain, t, x)):
            u[chain, t + 1, x + 2, h, window] = factor[index(chain, t + 1), x + 1, h, window] * value

    def advance(chain, t, x):
        for h, value in enumerate(advanced(chain, t, x)):
            rounded[chain, t + 1, x, h, window] = to_bfloat16(value)
            if t + 1 < NS:
                u[chain, t + 1, x + 2, h, window] = factor[index(chain, t + 1), x + 1, h, window] * value

    def adv(chain, t, low, high):
        loop(low, high, functools.partial(advance, chain, t))

    def outer(step):
        loop(0, 2, lambda k: step((layers - 1) * k))

    def ring(first, step):
        loop(0, 2, lambda k: step(first + (layers - 1 - 2 * first) * k))

    def beyond(step):
        loop(0, 2, lambda k: step((layers + 1) * k - 1))

    def edge_pair(d, step):
        loop(0, 2, lambda j: step(j + d * (layers - 2)))

    def out_layer(d, j):
        return layers - 1 - j if d else j

    def in_layer(d, j):
        return -1 - j if d else layers + j

    taken(w_v.at[pl.ds(1, layers)], local_sem.at[0])
    taken(psi_v.at[pl.ds(2, layers)], local_sem.at[1])
    taken(start_v, local_sem.at[2])
    def neighbour_of(d):
        return (side, lax.rem(slab + slabs + 2 * d - 1, slabs))

    def edge(d, k):
        return d * (layers - 1) + k * (1 - 2 * d)

    def edge_copy(n, d):
        first, count = ((0, 4), (4, 1))[n]
        return pltpu.make_async_remote_copy(
            edge_out.at[d, pl.ds(first, count)], edge_in.at[d, pl.ds(first, count)],
            edge_send, edge_recv.at[n, d], device_id=neighbour_of(d), device_id_type=MESH,
        )

    def code_edges(d):
        for j in (0, 1):
            x = edge(d, j)
            make_factor(x)
            begin_chain(OWN, x)
            edge_out[d, j] = write_log(u[OWN, 0, x + 2], 1)
            edge_out[d, 3 + j] = write_code(psi_v[x + 2], *psi_span)
        for h in range(parts):
            edge_out[d, 2, h] = write_code(w_v[edge(d, 0) + 1, :, plane(h)], *w_span)

    far = slab % 2
    code_edges(far)

    @pl.when(jnp.logical_not(first_slab))
    def _():
        edge_copy(0, far).start()

    code_group(1)
    field(1).start()
    code_edges(1 - far)
    edge_copy(0, 1 - far).start()
    code_group(2)
    code_group(3)
    field(2).start()
    field(3).start()

    stages = len(near)

    def open_gate(stage):
        pl.semaphore_signal(gate.at[stage], inc=1, device_id=near[stage], device_id_type=MESH)

    def pass_gate(stage):
        pl.semaphore_wait(gate.at[stage], 1)
        if stage + 1 < stages:
            open_gate(stage + 1)

    open_gate(0)
    loop(2, layers - 2, make_factor)
    loop(2, layers - 2, functools.partial(begin_chain, OWN))
    pass_gate(0)
    adv(OWN, 0, 1, layers - 1)
    adv(OWN, 1, 2, layers - 2)
    adv(OWN, 2, 3, layers - 3)

    def make_base(x):
        center, sums = around(psi_v, (x + 2,), EDGE, window.size)
        for h in range(parts):
            total = psi_v[x + 1, h, window] + psi_v[x + 3, h, window] + sums[h]
            base[x + 1, h] = relaxation(center[h], total)

    @pl.when(first_slab)
    def _():
        pl.semaphore_wait(seam_gate, 1)
        edge_copy(0, 0).start()

    loop(1, layers - 1, make_base)
    pass_gate(1)

    def halo(kind, d, first, count):
        return pltpu.make_async_remote_copy(
            halo_out.at[kind, d, pl.ds(first, count)], halo_in.at[kind, d, pl.ds(first, count)],
            halo_send, halo_recv.at[kind, d],
            device_id=neighbour_of(d), device_id_type=MESH,
        )

    def arrive(group):
        taken(field_in.at[slots[group]], field_recv.at[group])
        for x in groups[group]:
            begin_chain(FOREIGN, x)

    for j in (0, 1):
        arrive(j)
        for d in (0, 1):
            halo_out[0, d, j] = write_log(u[FOREIGN, 0, out_layer(d, j) + 2], 1)
            halo(0, d, j, 1).start()
    edge_copy(1, 0).start()
    edge_copy(1, 1).start()

    pass_gate(2)
    for d in (1 - far, far):
        taken(edge_in.at[1 - d, pl.ds(0, 4)], edge_recv.at[0, 1 - d])
        x = edge(d, -1)
        for h in range(parts):
            w_v[x + 1, :, plane(h)] = read_code(edge_in[1 - d, 2, h], *w_span)
        psi_v[x + 2] = read_code(edge_in[1 - d, 3], *psi_span)
        for j in (0, 1):
            u[OWN, 0, edge(d, -1 - j) + 2] = read_log(edge_in[1 - d, j], 1)
        make_factor(x)
        advance_halo(OWN, 0, x)
        advance(OWN, 0, edge(d, 0))
        for j in (0, 1):
            advance(OWN, 1, edge(d, j))
            halo_out[1, d, j] = write_log(u[OWN, 2, edge(d, j) + 2], 5)
        halo(1, d, 0, 2).start()
    arrive(2)
    ring(1, functools.partial(advance, FOREIGN, 0))
    arrive(3)
    ring(2, functools.partial(advance, FOREIGN, 0))
    sides = (1 - slab % 2, slab % 2)
    first_side = jnp.where(slab % (slabs - 1) == 0, sides[0], sides[1])
    for d in (first_side, 1 - first_side):
        taken(halo_in.at[0, 1 - d], halo_recv.at[0, 1 - d])
        for j in (0, 1):
            u[FOREIGN, 0, edge(d, -1 - j) + 2] = read_log(halo_in[0, 1 - d, j], 1)
        advance_halo(FOREIGN, 0, edge(d, -1))
        for j in (0,):
            advance(FOREIGN, 0, edge(d, j))
        for j in (0, 1):
            advance(FOREIGN, 1, edge(d, j))
            halo_out[2, d, j] = write_log(u[FOREIGN, 2, edge(d, j) + 2], 5)
        halo(2, d, 0, 2).start()

    adv(FOREIGN, 0, 3, layers - 3)
    for stage in range(3, stages - 1):
        pass_gate(stage)
    adv(OWN, 2, 1, 3)
    adv(OWN, 2, layers - 3, layers - 1)
    adv(OWN, 3, 2, layers - 2)
    adv(FOREIGN, 1, 2, layers - 2)
    adv(FOREIGN, 2, 1, layers - 1)

    weights = [0.5 if t in (0, NS) else 1.0 for t in range(NS + 1)]
    charged = [weights[t] * q[t] for t in range(NS + 1)]

    def gathered(x, h, terms):
        phi_layer, rho_layer = 0.0, 0.0
        for t in terms:
            product = rounded[OWN, t, x, h, window] * rounded[FOREIGN, NS - t, x, h, window]
            phi_layer = phi_layer + (product if weights[t] == 1.0 else weights[t] * product)
            rho_layer = rho_layer + charged[t] * product
        return phi_layer, rho_layer

    def gather(x):
        for h in range(parts):
            phi[x, h], rho[x + 1, h] = gathered(x, h, range(2, NS + 1))

    def complete(x, early):
        for h, value in enumerate(advanced(FOREIGN, NS - 1, x)):
            phi_layer, rho_layer = gathered(x, h, range(1, 2 if early else NS + 1))
            product = rounded[OWN, 0, x, h, window] * to_bfloat16(value)
            phi_layer = phi_layer + weights[0] * product
            rho_layer = rho_layer + charged[0] * product
            phi[x, h] = phi[x, h] + phi_layer if early else phi_layer
            rho[x + 1, h] = rho[x + 1, h] + rho_layer if early else rho_layer

    def whole(x):
        complete(x, False)

    def finish(x):
        complete(x, True)

    loop(2, layers - 2, whole)

    pass_gate(stages - 1)
    for d in sides:
        taken(halo_in.at[1, 1 - d], halo_recv.at[1, 1 - d])
        for j in (0, 1):
            u[OWN, 2, edge(d, -1 - j) + 2] = read_log(halo_in[1, 1 - d, j], 5)
        advance_halo(OWN, 2, edge(d, -1))
        advance(OWN, 2, edge(d, 0))
        for j in (0, 1):
            advance(OWN, 3, edge(d, j))
            gather(edge(d, j))

    def cells_of(x):
        return sum(phi[x, h, inner] for h in range(parts))

    partial = sum(cells_of(x) for x in range(2, layers - 2))

    for d in (0, 1):
        taken(edge_in.at[d, pl.ds(4, 1)], edge_recv.at[1, d])
    for d in (0, 1):
        psi_v[in_layer(d, 1) + 2] = read_code(edge_in[d, 4], *psi_span)
    for k in (-1, 0):
        make_base(k)
        make_base(layers - 1 - k)

    bits = [1 << k for k in range(slabs.bit_length() - 1)]
    flips = [bit - 2 * bit * lax.rem(slab // bit, 2) for bit in bits]

    def mirror(mask):
        target = slab
        for bit, flip in zip(bits, flips):
            target = target + flip if mask & bit else target
        return (other if mask >= slabs else side, target)

    masks = sorted(range(1, devices), key=lambda mask: (-(mask % slabs // 4), -mask))
    receivers = [(mask, mirror(mask)) for mask in masks] if ends == 2 and devices <= 32 else None
    for d in sides:
        taken(halo_in.at[2, 1 - d], halo_recv.at[2, 1 - d])
        for j in (0, 1):
            u[FOREIGN, 2, edge(d, -1 - j) + 2] = read_log(halo_in[2, 1 - d, j], 5)
        advance_halo(FOREIGN, 2, edge(d, -1))
        advance(FOREIGN, 2, edge(d, 0))
        finish(edge(d, 0))
        rho_out[d] = rho[edge(d, 0) + 1].astype(jnp.bfloat16)
        pltpu.make_async_remote_copy(
            rho_out.at[d], rho_in.at[d], rho_send, rho_recv, device_id=neighbour_of(d), device_id_type=MESH,
        ).start()
        finish(edge(d, 1))
        partial = partial + cells_of(edge(d, 0)) + cells_of(edge(d, 1))
    sums[0] = jnp.sum(partial, axis=0, keepdims=True)

    def share(step, target):
        pltpu.make_async_remote_copy(
            sums.at[0], sums.at[step], sum_send, sum_recv, device_id=target, device_id_type=MESH,
        ).start()

    if receivers is not None:
        for step, target in receivers:
            share(step, target)
    else:
        lax.fori_loop(1, devices, lambda step, carry: (share(step, device(step)), carry)[1], 0)

    others = sums.at[pl.ds(1, devices - 1)]
    taken(rho_in, rho_recv)
    for d in (0, 1):
        rho[in_layer(d, 0) + 1] = rho_in[d].astype(jnp.float32)
    taken(others, sum_recv)
    cells = float(devices * layers * half * w_hbm.shape[2])
    inverse = cells / jnp.sum(sums[...])
    scale_ref[...] = jnp.broadcast_to(inverse, scale_ref.shape)

    for ref, semaphore in (
        (field_out, field_send), (edge_out, edge_send), (halo_out, halo_send), (rho_out, rho_send), (others, sum_send)
    ):
        taken(ref, semaphore)


def ion_charge(value):
    return (2.0 * screening) * jnp.tanh(0.5 * value)


def relaxation(center, total):
    return (total - ion_charge(center) + screening * center) * (1.0 / (6.0 + screening))


def around(ref, at, first, count):
    parts = ref.shape[-3]
    lane = lax.broadcasted_iota(jnp.int32, (1, LANES), 1)
    lowest, highest = lane == 0, lane == LANES - 1
    center = [ref[(*at, h, pl.ds(first, count))] for h in range(parts)]
    lower = [pltpu.roll(value, 1, 1) for value in center]
    upper = [pltpu.roll(value, LANES - 1, 1) for value in center]
    sums = []
    for h in range(parts):
        total = ref[(*at, h, pl.ds(first - 1, count))] + ref[(*at, h, pl.ds(first + 1, count))]
        total = total + jnp.where(lowest, lower[h - 1], lower[h])
        sums.append(total + jnp.where(highest, upper[(h + 1) % parts], upper[h]))
    return center, sums


def finishing(phi, rho, base, scale_ref, density_hbm, potential_hbm, density, potential, relaxed, density_sem, potential_sem):
    layers, half = density_hbm.shape[0], density_hbm.shape[1]
    parts = phi.shape[1]
    inner = pl.ds(PAD - EDGE, half)
    inverse = scale_ref[...]
    scaled = inverse * (1.0 / (6.0 + screening))

    def plane(h):
        return slice(h * LANES, (h + 1) * LANES)

    for x in range(layers):
        for h in range(parts):
            density[x, :, plane(h)] = phi[x, h, inner] * inverse
    pltpu.make_async_copy(density, density_hbm, density_sem).start()
    for x in range(layers + 2):
        for h in range(parts):
            relaxed[x, h] = base[x, h] + rho[x, h] * scaled
    for x in range(layers):
        center, sums = around(relaxed, (x + 1,), PAD - EDGE, half)
        for h in range(parts):
            total = relaxed[x, h, inner] + relaxed[x + 2, h, inner] + sums[h]
            potential[x, :, plane(h)] = relaxation(center[h], total) + rho[x + 1, h, inner] * scaled
        if x % CHUNK == CHUNK - 1:
            done = pl.ds(x + 1 - CHUNK, CHUNK)
            pltpu.make_async_copy(potential.at[done], potential_hbm.at[done], potential_sem).start()
    pltpu.make_async_copy(density, density_hbm, density_sem).wait()
    pltpu.make_async_copy(potential, potential_hbm, potential_sem).wait()


def body(ends, slabs, w_field, psi_init, start_field, charges):
    layers, rows, depth = w_field.shape
    half = rows // ends
    wide = half + 2 * PAD
    devices = ends * slabs
    stages = slabs.bit_length()
    out = jax.ShapeDtypeStruct((layers, half, depth), jnp.float32)
    dma = pltpu.SemaphoreType.DMA

    parts = depth // LANES
    narrow = half + 2 * (PAD - EDGE)

    def tile(*lead):
        return pltpu.VMEM((*lead, parts, wide, LANES), jnp.float32)

    def slim(*lead):
        return pltpu.VMEM((*lead, parts, narrow, LANES), jnp.float32)

    def whole_rows(*lead):
        return pltpu.VMEM((*lead, wide, depth), jnp.float32)

    edge_rho = pltpu.VMEM((2, parts, narrow, LANES), jnp.bfloat16)

    def code(*lead):
        return pltpu.VMEM((*lead, parts, wide, LANES), jnp.int16)

    hbm = pl.BlockSpec(memory_space=pltpu.HBM)
    vmem = pl.BlockSpec(memory_space=pltpu.VMEM)
    def planes(count):
        return jax.ShapeDtypeStruct((count, parts, narrow, LANES), jnp.float32)

    fields = pl.pallas_call(
        functools.partial(kernel, ends, slabs),
        out_shape=(planes(layers), planes(layers + 2), planes(layers + 2), jax.ShapeDtypeStruct((1, LANES), jnp.float32)),
        in_specs=[hbm, hbm, hbm, hbm],
        out_specs=(vmem, vmem, vmem, vmem),
        scratch_shapes=[
            pltpu.SMEM((NS + 1,), jnp.int32), whole_rows(layers + 2), tile(layers + 4), whole_rows(layers), whole_rows(layers),
            tile(NS, layers + 2), tile(2, NS, layers + 4), tile(2, NS + 1, layers),
            pltpu.VMEM((devices, 1, LANES), jnp.float32),
            code(layers), code(layers), code(2, 5), code(2, 5), code(3, 2, 2), code(3, 2, 2), edge_rho, edge_rho,
            pltpu.SemaphoreType.REGULAR((stages,)), pltpu.SemaphoreType.REGULAR, dma(()), dma((4,)), dma((3,)), dma(()), dma((4,)),
            dma(()), dma((2, 2)), dma(()), dma((3, 2)), dma(()), dma(()), dma(()), dma(()),
        ],
        compiler_params=pltpu.CompilerParams(
            collective_id=0, has_side_effects=True, vmem_limit_bytes=40 * 1024 * 1024
        ),
        name="scf_step",
    )(*[pltpu.with_memory_space_constraint(v, pltpu.HBM) for v in (charges, w_field, psi_init, start_field)])
    result = pltpu.VMEM((layers, half, depth), jnp.float32)
    return pl.pallas_call(
        finishing,
        out_shape=(out, out),
        in_specs=[vmem] * 4,
        out_specs=(hbm, hbm),
        scratch_shapes=[result, result, slim(layers + 2), dma(()), dma(())],
        name="finishing",
    )(*[pltpu.with_memory_space_constraint(v, pltpu.VMEM) for v in fields])


def solution(mesh):
    in_specs = (P("slab", None, None), P("slab", None, None), P("end", "slab", None, None), P())
    out_specs = (P("slab", "end", None), P("slab", "end", None))
    step = functools.partial(body, mesh.shape["end"], mesh.shape["slab"])
    return jax.shard_map(step, mesh=mesh, in_specs=in_specs, out_specs=out_specs, check_vma=False)
```
